256 devices in a mesh: clip: 32 (over z_hi, x, y), tm: 8 (over z_lo, core).
Axes of the slice: x: 4, y: 4, z: 8 (z_hi: 2, z_lo: 4; z = z_hi * 4 + z_lo), core: 2. Of those that a mesh axis runs over, the one named last changes fastest.
Arguments:
- audio_feats: bfloat16 [128, 2048, 256], P('clip', 'tm'), may hold values from -6 to 6
- lip_feats: bfloat16 [128, 2048, 256], P('clip', 'tm'), may hold values from -6 to 6
- lengths: int32 [128], P('clip'), may hold values from 1024 to 2048
- labels: int32 [128], P('clip'), may hold values from -15 to 15
- w_audio_conv: bfloat16 [3, 256, 512], replicated, may hold values from -0.21875 to 0.21875
- w_audio_proj: bfloat16 [512, 512], replicated, may hold values from -0.25 to 0.25
- w_lip_conv: bfloat16 [3, 256, 512], replicated, may hold values from -0.21875 to 0.21875
- w_lip_proj: bfloat16 [512, 512], replicated, may hold values from -0.25 to 0.25
Outputs:
- loss: float32 [], replicated
- grad_audio_conv: float32 [3, 256, 512], replicated
- grad_audio_proj: float32 [512, 512], replicated
- grad_lip_conv: float32 [3, 256, 512], replicated
- grad_lip_proj: float32 [512, 512], replicated
The draws below stay inside these ranges and needn't reach their ends.
All inputs are finite; a program needn't handle non-finite values.
Results may differ from the reference program's by a relative error of at most 0.0075.
Values may be sent and summed in bfloat16 or wider, within the bound.
A program may use at most 64 MiB of HBM per device.

```python
import jax
import jax.numpy as jnp
from jax import lax

C_IN = 256
E = 512
SPAN = 15
CLIPS = 128
FRAMES = 2048


def set_ends(array, stream_key, smallest, high):
    spot = [jax.random.randint(jax.random.fold_in(stream_key, axis), (), 0, length) for axis, length in enumerate(array.shape)]
    longest = array.shape.index(max(array.shape))
    next_to = spot[:longest] + [(spot[longest] + 1) % array.shape[longest]] + spot[longest + 1:]
    return array.at[tuple(spot)].set(smallest).at[tuple(next_to)].set(high)


def steps_of(stream_key, dims, split, smallest, top_value):
    level, own = 1.0, jax.random.fold_in(stream_key, 6)
    for dim, shards_of in split:
        heights = jnp.exp(jax.random.uniform(jax.random.fold_in(own, dim), (shards_of,), jnp.float32, smallest / len(split), top_value / len(split)))
        level = level * jnp.repeat(heights, dims[dim] // shards_of).reshape([-1 if axis == dim else 1 for axis in range(len(dims))])
    return level


def bell_draw(stream_key, dims, spread, most, cuts=(), kind=jnp.bfloat16):
    values = spread * jax.random.normal(stream_key, dims, jnp.float32)
    if cuts:
        values = values * steps_of(stream_key, dims, cuts, -0.22, 0.18)
    return jnp.clip(values, -most, most).astype(kind)


def setup_inputs(seed: int = 0) -> dict:
    splits = jax.random.split(jax.random.key(seed), 9)
    return {
        "audio_feats": bell_draw(splits[0], (CLIPS, FRAMES, C_IN), 1.0, 6.0, ((0, 32), (1, 8))),
        "lip_feats": bell_draw(splits[1], (CLIPS, FRAMES, C_IN), 1.0, 6.0, ((0, 32), (1, 8))),
        "lengths": set_ends(jax.random.randint(splits[2], (CLIPS,), FRAMES // 2, FRAMES + 1), jax.random.fold_in(splits[2], 1), FRAMES // 2, FRAMES).astype(jnp.int32),
        "labels": set_ends(jax.random.randint(splits[3], (CLIPS,), 0 - SPAN, SPAN + 1), jax.random.fold_in(splits[3], 1), 0 - SPAN, SPAN).astype(jnp.int32),
        "w_audio_conv": bell_draw(splits[4], (3, C_IN, E), (3 * C_IN) ** -0.5, 0.21875),
        "w_audio_proj": bell_draw(splits[5], (E, E), E ** -0.5, 0.25),
        "w_lip_conv": bell_draw(splits[6], (3, C_IN, E), (3 * C_IN) ** -0.5, 0.21875),
        "w_lip_proj": bell_draw(splits[7], (E, E), E ** -0.5, 0.25),
    }


logit_sharpening_divisor = 10.0
loss_scale = 1024.0
epsilon = 1e-06

def silu_slope(values):
    sigma = jax.nn.sigmoid(values)
    return sigma * (1.0 + values * (1.0 - sigma))

def encoder(inputs, w_conv, w_proj):
    frame_total = inputs.shape[0]
    padded = jnp.pad(inputs, ((1, 1), (0, 0)))
    columns = jnp.concatenate([padded[0:frame_total], padded[1:frame_total + 1], padded[2:frame_total + 2]], axis=1)
    before = jnp.dot(columns, w_conv.reshape(3 * C_IN, E), preferred_element_type=jnp.float32)
    hidden = jax.nn.silu(before).astype(jnp.bfloat16)
    embedded = jnp.dot(hidden, w_proj, preferred_element_type=jnp.float32).astype(jnp.bfloat16)
    return (columns, before, hidden, embedded)

def inverse_norm(embedded):
    values = embedded.astype(jnp.float32)
    return lax.rsqrt(lax.optimization_barrier(jnp.sum(values * values, axis=-1)) + epsilon)

def encoder_grads(columns, before, hidden, grad_emb, w_proj):
    grad_proj = jnp.dot(hidden.T, grad_emb, preferred_element_type=jnp.float32)
    grad_hidden = jnp.dot(grad_emb, w_proj.T, preferred_element_type=jnp.float32)
    grad_before = (grad_hidden * silu_slope(before)).astype(jnp.bfloat16)
    grad_conv = jnp.dot(columns.T, grad_before, preferred_element_type=jnp.float32).reshape(3, C_IN, E)
    return (grad_conv, grad_proj)

def reference(audio_feats, lip_feats, lengths, labels, w_audio_conv, w_audio_proj, w_lip_conv, w_lip_proj):
    offsets = 2 * SPAN + 1
    count = jnp.sum((lengths - jnp.abs(labels)).astype(jnp.float32))
    shifts = jnp.arange(offsets, dtype=jnp.int32) - SPAN
    frame_ids = jnp.arange(FRAMES, dtype=jnp.int32)

    def per_clip(carry, items):
        audio, lip, length, label = items
        cols_a, pre_a, hid_a, emb_a = encoder(audio, w_audio_conv, w_audio_proj)
        cols_v, pre_v, hid_v, emb_v = encoder(lip, w_lip_conv, w_lip_proj)
        emb_a_pad = jnp.pad(emb_a, ((SPAN, SPAN), (0, 0)))
        inv_a_pad = inverse_norm(emb_a_pad)
        reciprocal_visual_length = inverse_norm(emb_v)
        audio_vals = emb_a_pad.astype(jnp.float32)
        lip_vals = emb_v.astype(jnp.float32)
        lagged_inner_terms = jnp.stack([lax.optimization_barrier(jnp.sum(lip_vals * audio_vals[offset:offset + FRAMES], axis=-1)) for offset in range(offsets)], axis=1)
        reciprocal_lag_strip = jnp.stack([inv_a_pad[offset:offset + FRAMES] for offset in range(offsets)], axis=1)
        positions = frame_ids[:, None] + shifts[None, :]
        inside = frame_ids < length
        valid = inside[:, None] & (positions >= 0) & (positions < length)
        counted = inside & (frame_ids + label >= 0) & (frame_ids + label < length)
        correct_lag_position = (shifts == label).astype(jnp.float32)
        lag_similarity_logits = logit_sharpening_divisor * lagged_inner_terms * reciprocal_visual_length[:, None] * reciprocal_lag_strip
        exponentiated_logits = jnp.where(valid, jnp.exp(lag_similarity_logits), 0.0)
        partition_sums = jnp.where(inside, lax.optimization_barrier(jnp.sum(exponentiated_logits, axis=1)), 1.0)
        picked = lax.optimization_barrier(jnp.sum(lag_similarity_logits * correct_lag_position[None, :], axis=1))
        frame_loss = jnp.where(counted, jnp.log(partition_sums) - picked, 0.0)
        normalized_probabilities = jnp.where(counted, loss_scale / count, 0.0)
        logit_derivative = logit_sharpening_divisor * normalized_probabilities[:, None] * (exponentiated_logits / partition_sums[:, None] - correct_lag_position[None, :])
        grad_dots = (logit_derivative * reciprocal_visual_length[:, None] * reciprocal_lag_strip).astype(jnp.bfloat16)
        grad_inv_v = lax.optimization_barrier(jnp.sum(logit_derivative * lagged_inner_terms * reciprocal_lag_strip, axis=1))
        audio_term = logit_derivative * lagged_inner_terms * reciprocal_visual_length[:, None]
        dot_vals = grad_dots.astype(jnp.float32)
        lip_sum = jnp.zeros((FRAMES, E), jnp.float32)
        audio_sum = jnp.zeros((FRAMES + 2 * SPAN, E), jnp.float32)
        inv_sum = jnp.zeros((FRAMES + 2 * SPAN,), jnp.float32)
        for offset in range(offsets):
            lip_sum = lip_sum + dot_vals[:, offset, None] * audio_vals[offset:offset + FRAMES]
            audio_sum = audio_sum.at[offset:offset + FRAMES].add(dot_vals[:, offset, None] * lip_vals)
            inv_sum = inv_sum.at[offset:offset + FRAMES].add(audio_term[:, offset])
        grad_lip = (lip_sum - (reciprocal_visual_length * reciprocal_visual_length * reciprocal_visual_length * grad_inv_v)[:, None] * lip_vals).astype(jnp.bfloat16)
        audio_sum = audio_sum - (inv_a_pad * inv_a_pad * inv_a_pad * inv_sum)[:, None] * audio_vals
        grad_audio = audio_sum[SPAN:SPAN + FRAMES].astype(jnp.bfloat16)
        gca, gpa = encoder_grads(cols_a, pre_a, hid_a, grad_audio, w_audio_proj)
        gcv, gpv = encoder_grads(cols_v, pre_v, hid_v, grad_lip, w_lip_proj)
        acc_ac, acc_ap, acc_vc, acc_vp, acc_loss = carry
        return ((acc_ac + gca, acc_ap + gpa, acc_vc + gcv, acc_vp + gpv, acc_loss + jnp.sum(frame_loss)), None)
    start = (jnp.zeros((3, C_IN, E), jnp.float32), jnp.zeros((E, E), jnp.float32), jnp.zeros((3, C_IN, E), jnp.float32), jnp.zeros((E, E), jnp.float32), jnp.zeros((), jnp.float32))
    totals_out, unused = lax.scan(per_clip, start, (audio_feats, lip_feats, lengths, labels))
    grad_ac, grad_ap, grad_vc, grad_vp, loss_sum = totals_out
    return (loss_sum / count, grad_ac, grad_ap, grad_vc, grad_vp)
```

```python
import jax
import jax.numpy as jnp
from jax import lax
from jax.sharding import PartitionSpec as P
import functools
from jax.experimental import pallas as pl
from jax.experimental.pallas import tpu as pltpu

SPAN = 15


MESH_ID = pl.DeviceIdType.MESH


def _coords():
    ci = lax.axis_index("clip")
    ti = lax.axis_index("tm")
    y = ci % 4
    x = (ci // 4) % 4
    zh = ci // 16
    core = ti % 2
    zl = ti // 2
    return ci, ti, y, x, zh, core, zl


def _levels(rows):
    ci, ti, y, x, zh, core, zl = _coords()
    z = zh * 4 + zl

    def at_y(v):
        return (zh * 16 + x * 4 + v % 4, ti)

    def at_x(v):
        return (zh * 16 + (v % 4) * 4 + y, ti)

    def at_z(v):
        w = v % 8
        return ((w // 4) * 16 + x * 4 + y, (w % 4) * 2 + core)

    def at_c(v):
        return (ci, zl * 2 + v % 2)

    return [("c", 2, core, at_c, 1), ("y", 4, y, at_y, 2), ("x", 4, x, at_x, 2), ("z", 8, z, at_z, 1)]


def _kernel(rows, x_ref, o_ref, work, rbuf, send_sem, recv_sem):
    levels = _levels(rows)
    barrier = pltpu.get_barrier_semaphore()
    peers = []
    for name, n, me, nbr, ndir in levels:
        peers.append(nbr(me + 1))
        if n > 2:
            peers.append(nbr(me - 1))
    for p in peers:
        pl.semaphore_signal(barrier, inc=1, device_id=p, device_id_type=MESH_ID)
    pl.semaphore_wait(barrier, len(peers))

    base = 0
    size = rows
    slot = 0
    sem = 0
    plan = []
    for li, (name, n, me, nbr, ndir) in enumerate(levels):
        chunk = size // n
        piece = chunk // ndir
        own = x_ref if li == 0 else work

        def pos(k, d, base=base, chunk=chunk, piece=piece):
            return pl.multiple_of(base + k * chunk + d * piece, 8)

        for s in range(n - 1):
            copies = []
            for d in range(ndir):
                sign = 1 if d == 0 else -1
                send_k = (me - sign * (s + 1)) % n
                recv_k = (me - sign * (s + 2)) % n
                src = own if s == 0 else work
                c = pltpu.make_async_remote_copy(
                    src_ref=src.at[pl.ds(pos(send_k, d), piece)],
                    dst_ref=rbuf.at[pl.ds(slot, piece)],
                    send_sem=send_sem.at[sem],
                    recv_sem=recv_sem.at[sem],
                    device_id=nbr(me + sign),
                    device_id_type=MESH_ID,
                )
                c.start()
                copies.append((c, slot, recv_k, d))
                slot += piece
                sem += 1
            for c, sl, recv_k, d in copies:
                c.wait_recv()
                at = pl.ds(pos(recv_k, d), piece)
                work[at] = rbuf[pl.ds(sl, piece)] + own[at]
            for c, sl, recv_k, d in copies:
                c.wait_send()
        plan.append((name, n, me, nbr, ndir, base, chunk, piece))
        base = base + me * chunk
        size = chunk

    fin = pl.ds(pl.multiple_of(base, 8), size)
    o_ref[fin] = work[fin]
    for name, n, me, nbr, ndir, lbase, chunk, piece in reversed(plan):

        def pos(k, d, base=lbase, chunk=chunk, piece=piece):
            return pl.multiple_of(base + k * chunk + d * piece, 8)

        for s in range(n - 1):
            copies = []
            for d in range(ndir):
                sign = 1 if d == 0 else -1
                send_k = (me - sign * s) % n
                at = pl.ds(pos(send_k, d), piece)
                c = pltpu.make_async_remote_copy(
                    src_ref=o_ref.at[at],
                    dst_ref=o_ref.at[at],
                    send_sem=send_sem.at[sem],
                    recv_sem=recv_sem.at[sem],
                    device_id=nbr(me + sign),
                    device_id_type=MESH_ID,
                )
                c.start()
                copies.append(c)
                sem += 1
            for c in copies:
                c.wait()
    return None


def _counts(rows):
    slot = 0
    sem = 0
    size = rows
    for name, n, ndir in (("c", 2, 1), ("y", 4, 2), ("x", 4, 2), ("z", 8, 1)):
        chunk = size // n
        piece = chunk // ndir
        slot += piece * ndir * (n - 1)
        sem += 2 * ndir * (n - 1)
        size = chunk
    return slot, sem


def all_sum(flat):
    rows = flat.shape[0]
    slots, sems = _counts(rows)
    return pl.pallas_call(
        functools.partial(_kernel, rows),
        out_shape=jax.ShapeDtypeStruct(flat.shape, flat.dtype),
        in_specs=[pl.BlockSpec(memory_space=pltpu.VMEM)],
        out_specs=pl.BlockSpec(memory_space=pltpu.VMEM),
        scratch_shapes=[
            pltpu.VMEM(flat.shape, flat.dtype),
            pltpu.VMEM((slots, flat.shape[1]), flat.dtype),
            pltpu.SemaphoreType.DMA((sems,)),
            pltpu.SemaphoreType.DMA((sems,)),
        ],
        compiler_params=pltpu.CompilerParams(
            collective_id=0, has_side_effects=True, vmem_limit_bytes=48 * 1024 * 1024
        ),
    )(flat)


logit_sharpening_divisor = 10.0
loss_scale = 1024.0
epsilon = 1e-06


def padded_2(cells, sides, width):
    for axis, dim in sides:
        count = lax.axis_size(axis)
        ends = count - 1
        head = lax.slice_in_dim(cells, 0, width, axis=dim)
        tail = lax.slice_in_dim(cells, cells.shape[dim] - width, cells.shape[dim], axis=dim)
        cells = jnp.concatenate(
            [
                lax.ppermute(tail, axis, [(i, (i + 1) % count) for i in range(ends)]),
                cells,
                lax.ppermute(head, axis, [((i + 1) % count, i) for i in range(ends)]),
            ],
            axis=dim,
        )
    return cells


def from_behind(value, axis, steps):
    count = lax.axis_size(axis)
    initial, last = (max(0, -steps), min(count, count - steps))
    return lax.ppermute(value, axis, [(source, source + steps) for source in range(initial, last)])


def silu_slope(values):
    sigma = jax.nn.sigmoid(values)
    return sigma * (1.0 + values * (1.0 - sigma))


def encoder(padded, w_conv, w_proj):
    clip_num, frame_pad, chan_num = padded.shape
    frame_num = frame_pad - 2
    columns = jnp.concatenate(
        [padded[:, 0:frame_num], padded[:, 1 : frame_num + 1], padded[:, 2 : frame_num + 2]], axis=2
    )
    before = jnp.einsum(
        "cfk,ke->cfe",
        columns,
        w_conv.reshape(3 * chan_num, w_conv.shape[2]),
        preferred_element_type=jnp.float32,
    )
    hidden = jax.nn.silu(before).astype(jnp.bfloat16)
    embedded = jnp.einsum("cfe,eg->cfg", hidden, w_proj, preferred_element_type=jnp.float32).astype(
        jnp.bfloat16
    )
    return (columns, before, hidden, embedded)


def inverse_norm(embedded):
    values = embedded.astype(jnp.float32)
    return lax.rsqrt(jnp.sum(values * values, axis=-1) + epsilon)


def spread_band(band, wide_len):
    clip_num, row_num, band_len = band.shape
    full_band = jnp.pad(band, ((0, 0), (0, 0), (0, wide_len + 1 - band_len)))
    flat_band = full_band.reshape(clip_num, row_num * (wide_len + 1))[:, : row_num * wide_len]
    return flat_band.reshape(clip_num, row_num, wide_len)


def narrow_band(matrix, band_len):
    clip_num, row_num, wide_len = matrix.shape
    flat_mat = jnp.pad(matrix.reshape(clip_num, row_num * wide_len), ((0, 0), (0, row_num)))
    return flat_mat.reshape(clip_num, row_num, wide_len + 1)[:, :, :band_len]


def flatten_rows(values):
    return values.reshape(values.shape[0] * values.shape[1], values.shape[2])


def proj_grad(hidden, grad_emb):
    return jnp.einsum("re,rf->ef", hidden, grad_emb, preferred_element_type=jnp.float32)


def conv_grad(columns, before, grad_emb, w_proj, w_conv):
    grad_hidden = jnp.einsum("rf,ef->re", grad_emb, w_proj, preferred_element_type=jnp.float32)
    grad_before = (grad_hidden * silu_slope(before)).astype(jnp.bfloat16)
    grad_conv = jnp.einsum("rk,re->ke", columns, grad_before, preferred_element_type=jnp.float32)
    return grad_conv.reshape(w_conv.shape)


def shards(
    audio_feats, lip_feats, lengths, labels, w_audio_conv, w_audio_proj, w_lip_conv, w_lip_proj
):
    clip_num, frame_num, chan_num = audio_feats.shape
    width = w_audio_proj.shape[1]
    offsets = 2 * SPAN + 1
    wide_len = frame_num + 2 * SPAN
    first_frame = lax.axis_index("tm") * frame_num
    stacked = jnp.stack([audio_feats, lip_feats])
    padded = padded_2(stacked, (("tm", 2),), 1)
    cols_a, pre_a, hid_a, emb_a = encoder(padded[0], w_audio_conv, w_audio_proj)
    cols_v, pre_v, hid_v, emb_v = encoder(padded[1], w_lip_conv, w_lip_proj)
    window = padded_2(emb_a, (("tm", 1),), SPAN)
    cols_a, pre_a, hid_a = (flatten_rows(cols_a), flatten_rows(pre_a), flatten_rows(hid_a))
    cols_v, pre_v, hid_v = (flatten_rows(cols_v), flatten_rows(pre_v), flatten_rows(hid_v))
    count_part = jnp.sum(lengths - jnp.abs(labels))
    count = jnp.sum(lax.all_gather(count_part, "clip")).astype(jnp.float32)
    matrix = jnp.einsum("cfe,cwe->cfw", emb_v, window, preferred_element_type=jnp.float32)
    lagged_inner_terms = narrow_band(matrix, offsets)
    inv_win = inverse_norm(window)
    reciprocal_visual_length = inverse_norm(emb_v)
    reciprocal_lag_strip = jnp.stack(
        [inv_win[:, offset : offset + frame_num] for offset in range(offsets)], axis=2
    )
    frame_ids = first_frame + jnp.arange(frame_num, dtype=jnp.int32)
    shifts = jnp.arange(offsets, dtype=jnp.int32) - SPAN
    positions = frame_ids[:, None] + shifts[None, :]
    inside = frame_ids[None, :] < lengths[:, None]
    valid = inside[:, :, None] & (positions[None] >= 0) & (positions[None] < lengths[:, None, None])
    target_pos = frame_ids[None, :] + labels[:, None]
    counted = inside & (target_pos >= 0) & (target_pos < lengths[:, None])
    correct_lag_position = (shifts[None, :] == labels[:, None]).astype(jnp.float32)
    lag_similarity_logits = (
        logit_sharpening_divisor
        * lagged_inner_terms
        * reciprocal_visual_length[:, :, None]
        * reciprocal_lag_strip
    )
    exponentiated_logits = jnp.where(valid, jnp.exp(lag_similarity_logits), 0.0)
    partition_sums = jnp.where(inside, jnp.sum(exponentiated_logits, axis=2), 1.0)
    picked = jnp.sum(lag_similarity_logits * correct_lag_position[:, None, :], axis=2)
    loss_local = jnp.sum(jnp.where(counted, jnp.log(partition_sums) - picked, 0.0))
    normalized_probabilities = jnp.where(counted, loss_scale / count, 0.0)
    logit_derivative = (
        logit_sharpening_divisor
        * normalized_probabilities[:, :, None]
        * (exponentiated_logits / partition_sums[:, :, None] - correct_lag_position[:, None, :])
    )
    grad_dots = (
        logit_derivative * reciprocal_visual_length[:, :, None] * reciprocal_lag_strip
    ).astype(jnp.bfloat16)
    grad_inv_v = jnp.sum(logit_derivative * lagged_inner_terms * reciprocal_lag_strip, axis=2)
    grad_inv_win = jnp.sum(
        spread_band(
            logit_derivative * lagged_inner_terms * reciprocal_visual_length[:, :, None], wide_len
        ),
        axis=1,
    )
    band_full = spread_band(grad_dots, wide_len)
    lip_sum = jnp.einsum("cfw,cwe->cfe", band_full, window, preferred_element_type=jnp.float32)
    lip_vals = emb_v.astype(jnp.float32)
    grad_lip = (
        lip_sum
        - (
            reciprocal_visual_length
            * reciprocal_visual_length
            * reciprocal_visual_length
            * grad_inv_v
        )[:, :, None]
        * lip_vals
    ).astype(jnp.bfloat16)
    win_sum = jnp.einsum("cfw,cfe->cwe", band_full, emb_v, preferred_element_type=jnp.float32)
    win_sum = win_sum - (inv_win * inv_win * inv_win * grad_inv_win)[:, :, None] * window.astype(
        jnp.float32
    )
    own_grad = win_sum[:, SPAN : SPAN + frame_num]
    from_after = from_behind(win_sum[:, :SPAN], "tm", -1)
    from_before = from_behind(win_sum[:, frame_num + SPAN :], "tm", 1)
    own_grad = own_grad.at[:, frame_num - SPAN :].add(from_after)
    own_grad = own_grad.at[:, :SPAN].add(from_before)
    grad_audio = own_grad.astype(jnp.bfloat16).reshape(clip_num * frame_num, width)
    grad_lip = grad_lip.reshape(clip_num * frame_num, width)
    grad_ap = proj_grad(hid_a, grad_audio)
    grad_vp = proj_grad(hid_v, grad_lip)
    grad_ac = conv_grad(cols_a, pre_a, grad_audio, w_audio_proj, w_audio_conv)
    grad_vc = conv_grad(cols_v, pre_v, grad_lip, w_lip_proj, w_lip_conv)
    parts = (grad_ac, grad_vc, grad_ap, grad_vp)
    flat = jnp.concatenate([g.reshape(-1, 128) for g in parts], axis=0)
    total = all_sum(flat)
    outs = []
    start = 0
    for g in parts:
        rows = g.size // 128
        outs.append(total[start : start + rows].reshape(g.shape))
        start += rows
    grad_ac, grad_vc, grad_ap, grad_vp = outs
    loss_sum = jnp.sum(lax.all_gather(loss_local, ("clip", "tm")))
    return (loss_sum / count, grad_ac, grad_ap, grad_vc, grad_vp)


def solution(mesh):
    placed = (
        P("clip", "tm", None),
        P("clip", "tm", None),
        P("clip"),
        P("clip"),
        P(),
        P(),
        P(),
        P(),
    )
    return jax.shard_map(
        shards, mesh=mesh, in_specs=placed, out_specs=(P(), P(), P(), P(), P()), check_vma=False
    )
```

```python
import jax
import jax.numpy as jnp
from jax import lax
from jax.sharding import PartitionSpec as P
import functools
from jax.experimental import pallas as pl
from jax.experimental.pallas import tpu as pltpu

SPAN = 15


MESH_ID = pl.DeviceIdType.MESH


def _coords():
    ci = lax.axis_index("clip")
    ti = lax.axis_index("tm")
    return ci, ti, ci % 4, (ci // 4) % 4, ci // 16, ti % 2, ti // 2


def _levels():
    ci, ti, y, x, zh, core, zl = _coords()
    z = zh * 4 + zl

    def at_y(v):
        return (zh * 16 + x * 4 + v % 4, ti)

    def at_x(v):
        return (zh * 16 + (v % 4) * 4 + y, ti)

    def at_z(v):
        w = v % 8
        return ((w // 4) * 16 + x * 4 + y, (w % 4) * 2 + core)

    def at_c(v):
        return (ci, zl * 2 + v % 2)

    def at_h(v):
        return ((v % 2) * 16 + x * 4 + y, ti)

    return {
        "c": (2, core, at_c, 1),
        "y": (4, y, at_y, 2),
        "x": (4, x, at_x, 2),
        "z": (8, z, at_z, 1),
        "h": (2, zh, at_h, 1),
    }


def _barrier(levels):
    barrier = pltpu.get_barrier_semaphore()
    peers = []
    for n, me, nbr, ndir in levels:
        peers.append(nbr(me + 1))
        if n > 2:
            peers.append(nbr(me - 1))
    for p in peers:
        pl.semaphore_signal(barrier, inc=1, device_id=p, device_id_type=MESH_ID)
    pl.semaphore_wait(barrier, len(peers))


def _small_start(n, me, nbr, s, tbuf, toff, tsend, trecv, tsem):
    at = toff + (me - s) % n
    c = pltpu.make_async_remote_copy(
        src_ref=tbuf.at[at],
        dst_ref=tbuf.at[at],
        send_sem=tsend.at[tsem],
        recv_sem=trecv.at[tsem],
        device_id=nbr(me + 1),
        device_id_type=MESH_ID,
    )
    c.start()
    return c


def _small_sum(n, tbuf, toff):
    acc = tbuf[toff]
    for k in range(1, n):
        acc = acc + tbuf[toff + k]
    return acc


def _small_kernel(names, t_ref, to_ref, tbuf, tsend, trecv):
    table = _levels()
    levels = [table[k] for k in names]
    _barrier(levels)
    toff = 0
    tsem = 0
    for li, (n, me, nbr, ndir) in enumerate(levels):
        tbuf[toff + me] = t_ref[...] if li == 0 else to_ref[...]
        for s in range(n - 1):
            c = _small_start(n, me, nbr, s, tbuf, toff, tsend, trecv, tsem)
            c.wait()
            tsem += 1
        to_ref[...] = _small_sum(n, tbuf, toff)
        toff += n


def small_sum(t, names, cid):
    table_n = {"c": 2, "y": 4, "x": 4, "z": 8, "h": 2}
    slots = sum(table_n[k] for k in names)
    sems = sum(table_n[k] - 1 for k in names)
    return pl.pallas_call(
        functools.partial(_small_kernel, names),
        out_shape=jax.ShapeDtypeStruct(t.shape, t.dtype),
        in_specs=[pl.BlockSpec(memory_space=pltpu.VMEM)],
        out_specs=pl.BlockSpec(memory_space=pltpu.VMEM),
        scratch_shapes=[
            pltpu.VMEM((slots,) + t.shape, t.dtype),
            pltpu.SemaphoreType.DMA((sems,)),
            pltpu.SemaphoreType.DMA((sems,)),
        ],
        compiler_params=pltpu.CompilerParams(collective_id=cid, has_side_effects=True),
    )(t)


BIG_LEVELS = ("c", "y", "x", "z")


def _kernel(rows, x_ref, t_ref, o_ref, to_ref, work, rbuf, send_sem, recv_sem, tbuf, tsend, trecv):
    table = _levels()
    levels = [table[k] for k in BIG_LEVELS]
    _barrier(levels)

    base = 0
    size = rows
    slot = 0
    sem = 0
    toff = 0
    tsem = 0
    plan = []
    for li, (n, me, nbr, ndir) in enumerate(levels):
        chunk = size // n
        piece = chunk // ndir
        own = x_ref if li == 0 else work
        tbuf[toff + me] = t_ref[...] if li == 0 else to_ref[...]

        def pos(k, d, base=base, chunk=chunk, piece=piece):
            return pl.multiple_of(base + k * chunk + d * piece, 8)

        for s in range(n - 1):
            copies = []
            for d in range(ndir):
                sign = 1 if d == 0 else -1
                send_k = (me - sign * (s + 1)) % n
                recv_k = (me - sign * (s + 2)) % n
                src = own if s == 0 else work
                c = pltpu.make_async_remote_copy(
                    src_ref=src.at[pl.ds(pos(send_k, d), piece)],
                    dst_ref=rbuf.at[pl.ds(slot, piece)],
                    send_sem=send_sem.at[sem],
                    recv_sem=recv_sem.at[sem],
                    device_id=nbr(me + sign),
                    device_id_type=MESH_ID,
                )
                c.start()
                copies.append((c, slot, recv_k, d))
                slot += piece
                sem += 1
            tc = _small_start(n, me, nbr, s, tbuf, toff, tsend, trecv, tsem)
            tsem += 1
            for c, sl, recv_k, d in copies:
                c.wait_recv()
                at = pl.ds(pos(recv_k, d), piece)
                work[at] = rbuf[pl.ds(sl, piece)] + own[at]
            for c, sl, recv_k, d in copies:
                c.wait_send()
            tc.wait()
        to_ref[...] = _small_sum(n, tbuf, toff)
        toff += n
        plan.append((n, me, nbr, ndir, base, chunk, piece))
        base = base + me * chunk
        size = chunk

    fin = pl.ds(pl.multiple_of(base, 8), size)
    o_ref[fin] = work[fin]
    for n, me, nbr, ndir, lbase, chunk, piece in reversed(plan):

        def pos(k, d, base=lbase, chunk=chunk, piece=piece):
            return pl.multiple_of(base + k * chunk + d * piece, 8)

        for s in range(n - 1):
            copies = []
            for d in range(ndir):
                sign = 1 if d == 0 else -1
                send_k = (me - sign * s) % n
                at = pl.ds(pos(send_k, d), piece)
                c = pltpu.make_async_remote_copy(
                    src_ref=o_ref.at[at],
                    dst_ref=o_ref.at[at],
                    send_sem=send_sem.at[sem],
                    recv_sem=recv_sem.at[sem],
                    device_id=nbr(me + sign),
                    device_id_type=MESH_ID,
                )
                c.start()
                copies.append(c)
                sem += 1
            for c in copies:
                c.wait()


def _counts(rows):
    slot = 0
    sem = 0
    tslots = 0
    tsems = 0
    size = rows
    for n, ndir in ((2, 1), (4, 2), (4, 2), (8, 1)):
        chunk = size // n
        piece = chunk // ndir
        slot += piece * ndir * (n - 1)
        sem += 2 * ndir * (n - 1)
        tslots += n
        tsems += n - 1
        size = chunk
    return slot, sem, tslots, tsems


def all_sum(flat, small):
    rows = flat.shape[0]
    slots, sems, tslots, tsems = _counts(rows)
    return pl.pallas_call(
        functools.partial(_kernel, rows),
        out_shape=(
            jax.ShapeDtypeStruct(flat.shape, flat.dtype),
            jax.ShapeDtypeStruct(small.shape, small.dtype),
        ),
        in_specs=[pl.BlockSpec(memory_space=pltpu.VMEM)] * 2,
        out_specs=(pl.BlockSpec(memory_space=pltpu.VMEM),) * 2,
        scratch_shapes=[
            pltpu.VMEM(flat.shape, flat.dtype),
            pltpu.VMEM((slots, flat.shape[1]), flat.dtype),
            pltpu.SemaphoreType.DMA((sems,)),
            pltpu.SemaphoreType.DMA((sems,)),
            pltpu.VMEM((tslots,) + small.shape, small.dtype),
            pltpu.SemaphoreType.DMA((tsems,)),
            pltpu.SemaphoreType.DMA((tsems,)),
        ],
        compiler_params=pltpu.CompilerParams(
            collective_id=0, has_side_effects=True, vmem_limit_bytes=48 * 1024 * 1024
        ),
    )(flat, small)


logit_sharpening_divisor = 10.0
loss_scale = 1024.0
epsilon = 1e-06


def padded_2(cells, sides, width):
    for axis, dim in sides:
        count = lax.axis_size(axis)
        ends = count - 1
        head = lax.slice_in_dim(cells, 0, width, axis=dim)
        tail = lax.slice_in_dim(cells, cells.shape[dim] - width, cells.shape[dim], axis=dim)
        cells = jnp.concatenate(
            [
                lax.ppermute(tail, axis, [(i, (i + 1) % count) for i in range(ends)]),
                cells,
                lax.ppermute(head, axis, [((i + 1) % count, i) for i in range(ends)]),
            ],
            axis=dim,
        )
    return cells


def from_behind(value, axis, steps):
    count = lax.axis_size(axis)
    initial, last = (max(0, -steps), min(count, count - steps))
    return lax.ppermute(value, axis, [(source, source + steps) for source in range(initial, last)])


def silu_slope(values):
    sigma = jax.nn.sigmoid(values)
    return sigma * (1.0 + values * (1.0 - sigma))


def encoder(padded, w_conv, w_proj):
    clip_num, frame_pad, chan_num = padded.shape
    frame_num = frame_pad - 2
    columns = jnp.concatenate(
        [padded[:, 0:frame_num], padded[:, 1 : frame_num + 1], padded[:, 2 : frame_num + 2]], axis=2
    )
    before = jnp.einsum(
        "cfk,ke->cfe",
        columns,
        w_conv.reshape(3 * chan_num, w_conv.shape[2]),
        preferred_element_type=jnp.float32,
    )
    hidden = jax.nn.silu(before).astype(jnp.bfloat16)
    embedded = jnp.einsum("cfe,eg->cfg", hidden, w_proj, preferred_element_type=jnp.float32).astype(
        jnp.bfloat16
    )
    return (columns, before, hidden, embedded)


def inverse_norm(embedded):
    values = embedded.astype(jnp.float32)
    return lax.rsqrt(jnp.sum(values * values, axis=-1) + epsilon)


def spread_band(band, wide_len):
    clip_num, row_num, band_len = band.shape
    full_band = jnp.pad(band, ((0, 0), (0, 0), (0, wide_len + 1 - band_len)))
    flat_band = full_band.reshape(clip_num, row_num * (wide_len + 1))[:, : row_num * wide_len]
    return flat_band.reshape(clip_num, row_num, wide_len)


def narrow_band(matrix, band_len):
    clip_num, row_num, wide_len = matrix.shape
    flat_mat = jnp.pad(matrix.reshape(clip_num, row_num * wide_len), ((0, 0), (0, row_num)))
    return flat_mat.reshape(clip_num, row_num, wide_len + 1)[:, :, :band_len]


def flatten_rows(values):
    return values.reshape(values.shape[0] * values.shape[1], values.shape[2])


def proj_grad(hidden, grad_emb):
    return jnp.einsum("re,rf->ef", hidden, grad_emb, preferred_element_type=jnp.float32)


def conv_grad(columns, before, grad_emb, w_proj, w_conv):
    grad_hidden = jnp.einsum("rf,ef->re", grad_emb, w_proj, preferred_element_type=jnp.float32)
    grad_before = (grad_hidden * silu_slope(before)).astype(jnp.bfloat16)
    grad_conv = jnp.einsum("rk,re->ke", columns, grad_before, preferred_element_type=jnp.float32)
    return grad_conv.reshape(w_conv.shape)


def shards(
    audio_feats, lip_feats, lengths, labels, w_audio_conv, w_audio_proj, w_lip_conv, w_lip_proj
):
    clip_num, frame_num, chan_num = audio_feats.shape
    width = w_audio_proj.shape[1]
    offsets = 2 * SPAN + 1
    wide_len = frame_num + 2 * SPAN
    first_frame = lax.axis_index("tm") * frame_num
    stacked = jnp.stack([audio_feats, lip_feats])
    padded = padded_2(stacked, (("tm", 2),), 1)
    cols_a, pre_a, hid_a, emb_a = encoder(padded[0], w_audio_conv, w_audio_proj)
    cols_v, pre_v, hid_v, emb_v = encoder(padded[1], w_lip_conv, w_lip_proj)
    window = padded_2(emb_a, (("tm", 1),), SPAN)
    cols_a, pre_a, hid_a = (flatten_rows(cols_a), flatten_rows(pre_a), flatten_rows(hid_a))
    cols_v, pre_v, hid_v = (flatten_rows(cols_v), flatten_rows(pre_v), flatten_rows(hid_v))
    count_part = jnp.sum(lengths - jnp.abs(labels))
    count_block = jnp.zeros((8, 128), jnp.int32).at[0, 0].set(count_part)
    count = small_sum(count_block, ("y", "x", "h"), 1)[0, 0].astype(jnp.float32)
    matrix = jnp.einsum("cfe,cwe->cfw", emb_v, window, preferred_element_type=jnp.float32)
    lagged_inner_terms = narrow_band(matrix, offsets)
    inv_win = inverse_norm(window)
    reciprocal_visual_length = inverse_norm(emb_v)
    reciprocal_lag_strip = jnp.stack(
        [inv_win[:, offset : offset + frame_num] for offset in range(offsets)], axis=2
    )
    frame_ids = first_frame + jnp.arange(frame_num, dtype=jnp.int32)
    shifts = jnp.arange(offsets, dtype=jnp.int32) - SPAN
    positions = frame_ids[:, None] + shifts[None, :]
    inside = frame_ids[None, :] < lengths[:, None]
    valid = inside[:, :, None] & (positions[None] >= 0) & (positions[None] < lengths[:, None, None])
    target_pos = frame_ids[None, :] + labels[:, None]
    counted = inside & (target_pos >= 0) & (target_pos < lengths[:, None])
    correct_lag_position = (shifts[None, :] == labels[:, None]).astype(jnp.float32)
    lag_similarity_logits = (
        logit_sharpening_divisor
        * lagged_inner_terms
        * reciprocal_visual_length[:, :, None]
        * reciprocal_lag_strip
    )
    exponentiated_logits = jnp.where(valid, jnp.exp(lag_similarity_logits), 0.0)
    partition_sums = jnp.where(inside, jnp.sum(exponentiated_logits, axis=2), 1.0)
    picked = jnp.sum(lag_similarity_logits * correct_lag_position[:, None, :], axis=2)
    loss_local = jnp.sum(jnp.where(counted, jnp.log(partition_sums) - picked, 0.0))
    normalized_probabilities = jnp.where(counted, loss_scale / count, 0.0)
    logit_derivative = (
        logit_sharpening_divisor
        * normalized_probabilities[:, :, None]
        * (exponentiated_logits / partition_sums[:, :, None] - correct_lag_position[:, None, :])
    )
    grad_dots = (
        logit_derivative * reciprocal_visual_length[:, :, None] * reciprocal_lag_strip
    ).astype(jnp.bfloat16)
    grad_inv_v = jnp.sum(logit_derivative * lagged_inner_terms * reciprocal_lag_strip, axis=2)
    grad_inv_win = jnp.sum(
        spread_band(
            logit_derivative * lagged_inner_terms * reciprocal_visual_length[:, :, None], wide_len
        ),
        axis=1,
    )
    band_full = spread_band(grad_dots, wide_len)
    lip_sum = jnp.einsum("cfw,cwe->cfe", band_full, window, preferred_element_type=jnp.float32)
    lip_vals = emb_v.astype(jnp.float32)
    grad_lip = (
        lip_sum
        - (
            reciprocal_visual_length
            * reciprocal_visual_length
            * reciprocal_visual_length
            * grad_inv_v
        )[:, :, None]
        * lip_vals
    ).astype(jnp.bfloat16)
    win_sum = jnp.einsum("cfw,cfe->cwe", band_full, emb_v, preferred_element_type=jnp.float32)
    win_sum = win_sum - (inv_win * inv_win * inv_win * grad_inv_win)[:, :, None] * window.astype(
        jnp.float32
    )
    own_grad = win_sum[:, SPAN : SPAN + frame_num]
    from_after = from_behind(win_sum[:, :SPAN], "tm", -1)
    from_before = from_behind(win_sum[:, frame_num + SPAN :], "tm", 1)
    own_grad = own_grad.at[:, frame_num - SPAN :].add(from_after)
    own_grad = own_grad.at[:, :SPAN].add(from_before)
    grad_audio = own_grad.astype(jnp.bfloat16).reshape(clip_num * frame_num, width)
    grad_lip = grad_lip.reshape(clip_num * frame_num, width)
    grad_ap = proj_grad(hid_a, grad_audio)
    grad_vp = proj_grad(hid_v, grad_lip)
    grad_ac = conv_grad(cols_a, pre_a, grad_audio, w_audio_proj, w_audio_conv)
    grad_vc = conv_grad(cols_v, pre_v, grad_lip, w_lip_proj, w_lip_conv)
    parts = (grad_ac, grad_vc, grad_ap, grad_vp)
    flat = jnp.concatenate([g.reshape(-1, 128) for g in parts], axis=0)
    loss_block = jnp.zeros((8, 128), jnp.float32).at[0, 0].set(loss_local)
    total, loss_total = all_sum(flat, loss_block)
    outs = []
    start = 0
    for g in parts:
        rows = g.size // 128
        outs.append(total[start : start + rows].reshape(g.shape))
        start += rows
    grad_ac, grad_vc, grad_ap, grad_vp = outs
    loss_sum = loss_total[0, 0]
    return (loss_sum / count, grad_ac, grad_ap, grad_vc, grad_vp)


def solution(mesh):
    placed = (
        P("clip", "tm", None),
        P("clip", "tm", None),
        P("clip"),
        P("clip"),
        P(),
        P(),
        P(),
        P(),
    )
    return jax.shard_map(
        shards, mesh=mesh, in_specs=placed, out_specs=(P(), P(), P(), P(), P()), check_vma=False
    )
```

```python
import jax
import jax.numpy as jnp
from jax import lax
from jax.sharding import PartitionSpec as P
import functools
from jax.experimental import pallas as pl
from jax.experimental.pallas import tpu as pltpu

SPAN = 15


MESH_ID = pl.DeviceIdType.MESH


def _coords():
    ci = lax.axis_index("clip")
    ti = lax.axis_index("tm")
    return ci, ti, ci % 4, (ci // 4) % 4, ci // 16, ti % 2, ti // 2


def _levels():
    ci, ti, y, x, zh, core, zl = _coords()
    z = zh * 4 + zl

    def at_y(v):
        return (zh * 16 + x * 4 + v % 4, ti)

    def at_x(v):
        return (zh * 16 + (v % 4) * 4 + y, ti)

    def at_z(v):
        w = v % 8
        return ((w // 4) * 16 + x * 4 + y, (w % 4) * 2 + core)

    def at_c(v):
        return (ci, zl * 2 + v % 2)

    def at_h(v):
        return ((v % 2) * 16 + x * 4 + y, ti)

    return {
        "c": (2, core, at_c, 1),
        "y": (4, y, at_y, 2),
        "x": (4, x, at_x, 2),
        "z": (8, z, at_z, 1),
        "h": (2, zh, at_h, 1),
    }


def _barrier(levels):
    barrier = pltpu.get_barrier_semaphore()
    peers = []
    for n, me, nbr, ndir in levels:
        peers.append(nbr(me + 1))
        if n > 2:
            peers.append(nbr(me - 1))
    for p in peers:
        pl.semaphore_signal(barrier, inc=1, device_id=p, device_id_type=MESH_ID)
    pl.semaphore_wait(barrier, len(peers))


def _small_start(n, me, nbr, s, tbuf, toff, tsend, trecv, tsem):
    at = toff + (me - s) % n
    c = pltpu.make_async_remote_copy(
        src_ref=tbuf.at[at],
        dst_ref=tbuf.at[at],
        send_sem=tsend.at[tsem],
        recv_sem=trecv.at[tsem],
        device_id=nbr(me + 1),
        device_id_type=MESH_ID,
    )
    c.start()
    return c


def _small_sum(n, tbuf, toff):
    acc = tbuf[toff]
    for k in range(1, n):
        acc = acc + tbuf[toff + k]
    return acc


def _small_kernel(names, t_ref, to_ref, tbuf, tsend, trecv):
    table = _levels()
    levels = [table[k] for k in names]
    _barrier(levels)
    toff = 0
    tsem = 0
    for li, (n, me, nbr, ndir) in enumerate(levels):
        tbuf[toff + me] = t_ref[...] if li == 0 else to_ref[...]
        for s in range(n - 1):
            c = _small_start(n, me, nbr, s, tbuf, toff, tsend, trecv, tsem)
            c.wait()
            tsem += 1
        to_ref[...] = _small_sum(n, tbuf, toff)
        toff += n


def small_sum(t, names, cid):
    table_n = {"c": 2, "y": 4, "x": 4, "z": 8, "h": 2}
    slots = sum(table_n[k] for k in names)
    sems = sum(table_n[k] - 1 for k in names)
    return pl.pallas_call(
        functools.partial(_small_kernel, names),
        out_shape=jax.ShapeDtypeStruct(t.shape, t.dtype),
        in_specs=[pl.BlockSpec(memory_space=pltpu.VMEM)],
        out_specs=pl.BlockSpec(memory_space=pltpu.VMEM),
        scratch_shapes=[
            pltpu.VMEM((slots,) + t.shape, t.dtype),
            pltpu.SemaphoreType.DMA((sems,)),
            pltpu.SemaphoreType.DMA((sems,)),
        ],
        compiler_params=pltpu.CompilerParams(collective_id=cid, has_side_effects=True),
    )(t)


def _rs_stage(tasks, work, rbuf, send_sem, recv_sem, slot, sem, rider=None):
    n = tasks[0][0]
    for s in range(n - 1):
        copies = []
        for tn, me, nbr, ndir, base, size, own in tasks:
            chunk = size // tn
            piece = chunk // ndir
            for d in range(ndir):
                sign = 1 if d == 0 else -1
                send_at = pl.multiple_of(base + ((me - sign * (s + 1)) % tn) * chunk + d * piece, 8)
                recv_at = pl.multiple_of(base + ((me - sign * (s + 2)) % tn) * chunk + d * piece, 8)
                src = own if s == 0 else work
                c = pltpu.make_async_remote_copy(
                    src_ref=src.at[pl.ds(send_at, piece)],
                    dst_ref=rbuf.at[pl.ds(slot, piece)],
                    send_sem=send_sem.at[sem],
                    recv_sem=recv_sem.at[sem],
                    device_id=nbr(me + sign),
                    device_id_type=MESH_ID,
                )
                c.start()
                copies.append((c, slot, recv_at, piece, own))
                slot += piece
                sem += 1
        ride = rider(s) if rider is not None else None
        for c, sl, recv_at, piece, own in copies:
            c.wait_recv()
            at = pl.ds(recv_at, piece)
            work[at] = rbuf[pl.ds(sl, piece)] + own[at]
        for c, sl, recv_at, piece, own in copies:
            c.wait_send()
        if ride is not None:
            ride.wait()
    return slot, sem


def _ag_stage(tasks, o_ref, send_sem, recv_sem, sem):
    n = tasks[0][0]
    for s in range(n - 1):
        copies = []
        for tn, me, nbr, ndir, base, size, own in tasks:
            chunk = size // tn
            piece = chunk // ndir
            for d in range(ndir):
                sign = 1 if d == 0 else -1
                at = pl.ds(pl.multiple_of(base + ((me - sign * s) % tn) * chunk + d * piece, 8), piece)
                c = pltpu.make_async_remote_copy(
                    src_ref=o_ref.at[at],
                    dst_ref=o_ref.at[at],
                    send_sem=send_sem.at[sem],
                    recv_sem=recv_sem.at[sem],
                    device_id=nbr(me + sign),
                    device_id_type=MESH_ID,
                )
                c.start()
                copies.append(c)
                sem += 1
        for c in copies:
            c.wait()
    return sem


def _pass_copy(buf, at, nbr, target, sems, idx):
    c = pltpu.make_async_remote_copy(
        src_ref=buf.at[at],
        dst_ref=buf.at[at],
        send_sem=sems[0].at[idx],
        recv_sem=sems[1].at[idx],
        device_id=nbr(target),
        device_id_type=MESH_ID,
    )
    c.start()
    return c


def _kernel(rows, x_ref, t_ref, o_ref, to_ref, work, rbuf, zbuf, send_sem, recv_sem, tbuf, tsend, trecv):
    table = _levels()
    lc, ly, lx, lz = (table[k] for k in ("c", "y", "x", "z"))
    _barrier([lc, ly, lx, lz])
    tsems = (tsend, trecv)
    state = {"toff": 0, "tsem": 0}

    def tiny_level(level, first):
        n, me, nbr, ndir = level
        toff = state["toff"]
        tbuf[toff + me] = t_ref[...] if first else to_ref[...]

        def rider(s):
            c = _pass_copy(tbuf, toff + (me - s) % n, nbr, me + 1, tsems, state["tsem"])
            state["tsem"] += 1
            return c

        return rider

    def tiny_done(n):
        to_ref[...] = _small_sum(n, tbuf, state["toff"])
        state["toff"] += n

    slot, sem = 0, 0
    half = rows // 2
    quarter = rows // 4
    nc, core, nbc, _ = lc
    ny, yi, nby, _ = ly
    nx, xi, nbx, _ = lx
    nz, zi, nbz, _ = lz

    rider = tiny_level(lc, True)
    slot, sem = _rs_stage([(nc, core, nbc, 1, 0, rows, x_ref)], work, rbuf, send_sem, recv_sem, slot, sem, rider)
    tiny_done(nc)
    r0 = core * half
    a1, b1 = r0, r0 + quarter
    rider = tiny_level(ly, False)
    slot, sem = _rs_stage(
        [(ny, yi, nby, 2, a1, quarter, work), (nx, xi, nbx, 2, b1, quarter, work)],
        work, rbuf, send_sem, recv_sem, slot, sem, rider,
    )
    tiny_done(ny)
    c1 = quarter // 4
    a2, b2 = a1 + yi * c1, b1 + xi * c1
    rider = tiny_level(lx, False)
    slot, sem = _rs_stage(
        [(nx, xi, nbx, 1, a2, c1, work), (ny, yi, nby, 1, b2, c1, work)],
        work, rbuf, send_sem, recv_sem, slot, sem, rider,
    )
    tiny_done(nx)
    c2 = c1 // 4
    a3, b3 = a2 + xi * c2, b2 + yi * c2
    zbuf[zi, 0] = work[pl.ds(pl.multiple_of(a3, 8), c2)]
    zbuf[zi, 1] = work[pl.ds(pl.multiple_of(b3, 8), c2)]
    toff = state["toff"]
    tbuf[toff + zi] = to_ref[...]
    right = nz // 2
    left = nz - 1 - right
    for s in range(right):
        cs = [
            _pass_copy(zbuf, (zi - s) % nz, nbz, zi + 1, (send_sem, recv_sem), sem),
            _pass_copy(tbuf, toff + (zi - s) % nz, nbz, zi + 1, tsems, state["tsem"]),
        ]
        sem += 1
        state["tsem"] += 1
        if s < left:
            cs.append(_pass_copy(zbuf, (zi + s) % nz, nbz, zi - 1, (send_sem, recv_sem), sem))
            cs.append(_pass_copy(tbuf, toff + (zi + s) % nz, nbz, zi - 1, tsems, state["tsem"]))
            sem += 1
            state["tsem"] += 1
        for c in cs:
            c.wait()
    for colour, at in ((0, a3), (1, b3)):
        acc = zbuf[0, colour]
        for k in range(1, nz):
            acc = acc + zbuf[k, colour]
        o_ref[pl.ds(pl.multiple_of(at, 8), c2)] = acc
    tiny_done(nz)
    sem = _ag_stage([(nx, xi, nbx, 1, a2, c1, None), (ny, yi, nby, 1, b2, c1, None)], o_ref, send_sem, recv_sem, sem)
    sem = _ag_stage([(ny, yi, nby, 2, a1, quarter, None), (nx, xi, nbx, 2, b1, quarter, None)], o_ref, send_sem, recv_sem, sem)
    sem = _ag_stage([(nc, core, nbc, 1, 0, rows, None)], o_ref, send_sem, recv_sem, sem)


def _counts(rows):
    half, quarter = rows // 2, rows // 4
    c1 = quarter // 4
    slots = half + 3 * 2 * quarter // 4 + 3 * 2 * c1 // 4
    sems = 1 + 3 * 4 + 3 * 2 + 7 + 3 * 2 + 3 * 4 + 1
    return slots, sems, 2 + 4 + 4 + 8, 1 + 3 + 3 + 7


def all_sum(flat, small):
    rows = flat.shape[0]
    slots, sems, tslots, tsems = _counts(rows)
    c2 = rows // 64
    return pl.pallas_call(
        functools.partial(_kernel, rows),
        out_shape=(
            jax.ShapeDtypeStruct(flat.shape, flat.dtype),
            jax.ShapeDtypeStruct(small.shape, small.dtype),
        ),
        in_specs=[pl.BlockSpec(memory_space=pltpu.VMEM)] * 2,
        out_specs=(pl.BlockSpec(memory_space=pltpu.VMEM),) * 2,
        scratch_shapes=[
            pltpu.VMEM(flat.shape, flat.dtype),
            pltpu.VMEM((slots, flat.shape[1]), flat.dtype),
            pltpu.VMEM((8, 2, c2, flat.shape[1]), flat.dtype),
            pltpu.SemaphoreType.DMA((sems,)),
            pltpu.SemaphoreType.DMA((sems,)),
            pltpu.VMEM((tslots,) + small.shape, small.dtype),
            pltpu.SemaphoreType.DMA((tsems,)),
            pltpu.SemaphoreType.DMA((tsems,)),
        ],
        compiler_params=pltpu.CompilerParams(
            collective_id=0, has_side_effects=True, vmem_limit_bytes=48 * 1024 * 1024
        ),
    )(flat, small)


logit_sharpening_divisor = 10.0
loss_scale = 1024.0
epsilon = 1e-06


def padded_2(cells, sides, width):
    for axis, dim in sides:
        count = lax.axis_size(axis)
        ends = count - 1
        head = lax.slice_in_dim(cells, 0, width, axis=dim)
        tail = lax.slice_in_dim(cells, cells.shape[dim] - width, cells.shape[dim], axis=dim)
        cells = jnp.concatenate(
            [
                lax.ppermute(tail, axis, [(i, (i + 1) % count) for i in range(ends)]),
                cells,
                lax.ppermute(head, axis, [((i + 1) % count, i) for i in range(ends)]),
            ],
            axis=dim,
        )
    return cells


def from_behind(value, axis, steps):
    count = lax.axis_size(axis)
    initial, last = (max(0, -steps), min(count, count - steps))
    return lax.ppermute(value, axis, [(source, source + steps) for source in range(initial, last)])


def silu_slope(values):
    sigma = jax.nn.sigmoid(values)
    return sigma * (1.0 + values * (1.0 - sigma))


def encoder(padded, w_conv, w_proj):
    clip_num, frame_pad, chan_num = padded.shape
    frame_num = frame_pad - 2
    columns = jnp.concatenate(
        [padded[:, 0:frame_num], padded[:, 1 : frame_num + 1], padded[:, 2 : frame_num + 2]], axis=2
    )
    before = jnp.einsum(
        "cfk,ke->cfe",
        columns,
        w_conv.reshape(3 * chan_num, w_conv.shape[2]),
        preferred_element_type=jnp.float32,
    )
    hidden = jax.nn.silu(before).astype(jnp.bfloat16)
    embedded = jnp.einsum("cfe,eg->cfg", hidden, w_proj, preferred_element_type=jnp.float32).astype(
        jnp.bfloat16
    )
    return (columns, before, hidden, embedded)


def inverse_norm(embedded):
    values = embedded.astype(jnp.float32)
    return lax.rsqrt(jnp.sum(values * values, axis=-1) + epsilon)


def spread_band(band, wide_len):
    clip_num, row_num, band_len = band.shape
    full_band = jnp.pad(band, ((0, 0), (0, 0), (0, wide_len + 1 - band_len)))
    flat_band = full_band.reshape(clip_num, row_num * (wide_len + 1))[:, : row_num * wide_len]
    return flat_band.reshape(clip_num, row_num, wide_len)


def narrow_band(matrix, band_len):
    clip_num, row_num, wide_len = matrix.shape
    flat_mat = jnp.pad(matrix.reshape(clip_num, row_num * wide_len), ((0, 0), (0, row_num)))
    return flat_mat.reshape(clip_num, row_num, wide_len + 1)[:, :, :band_len]


def flatten_rows(values):
    return values.reshape(values.shape[0] * values.shape[1], values.shape[2])


def proj_grad(hidden, grad_emb):
    return jnp.einsum("re,rf->ef", hidden, grad_emb, preferred_element_type=jnp.float32)


def conv_grad(columns, before, grad_emb, w_proj, w_conv):
    grad_hidden = jnp.einsum("rf,ef->re", grad_emb, w_proj, preferred_element_type=jnp.float32)
    grad_before = (grad_hidden * silu_slope(before)).astype(jnp.bfloat16)
    grad_conv = jnp.einsum("rk,re->ke", columns, grad_before, preferred_element_type=jnp.float32)
    return grad_conv.reshape(w_conv.shape)


def shards(
    audio_feats, lip_feats, lengths, labels, w_audio_conv, w_audio_proj, w_lip_conv, w_lip_proj
):
    clip_num, frame_num, chan_num = audio_feats.shape
    width = w_audio_proj.shape[1]
    offsets = 2 * SPAN + 1
    wide_len = frame_num + 2 * SPAN
    first_frame = lax.axis_index("tm") * frame_num
    stacked = jnp.stack([audio_feats, lip_feats])
    padded = padded_2(stacked, (("tm", 2),), 1)
    cols_a, pre_a, hid_a, emb_a = encoder(padded[0], w_audio_conv, w_audio_proj)
    cols_v, pre_v, hid_v, emb_v = encoder(padded[1], w_lip_conv, w_lip_proj)
    window = padded_2(emb_a, (("tm", 1),), SPAN)
    cols_a, pre_a, hid_a = (flatten_rows(cols_a), flatten_rows(pre_a), flatten_rows(hid_a))
    cols_v, pre_v, hid_v = (flatten_rows(cols_v), flatten_rows(pre_v), flatten_rows(hid_v))
    count_part = jnp.sum(lengths - jnp.abs(labels))
    count_block = jnp.zeros((8, 128), jnp.int32).at[0, 0].set(count_part)
    count = small_sum(count_block, ("y", "x", "h"), 1)[0, 0].astype(jnp.float32)
    matrix = jnp.einsum("cfe,cwe->cfw", emb_v, window, preferred_element_type=jnp.float32)
    lagged_inner_terms = narrow_band(matrix, offsets)
    inv_win = inverse_norm(window)
    reciprocal_visual_length = inverse_norm(emb_v)
    reciprocal_lag_strip = jnp.stack(
        [inv_win[:, offset : offset + frame_num] for offset in range(offsets)], axis=2
    )
    frame_ids = first_frame + jnp.arange(frame_num, dtype=jnp.int32)
    shifts = jnp.arange(offsets, dtype=jnp.int32) - SPAN
    positions = frame_ids[:, None] + shifts[None, :]
    inside = frame_ids[None, :] < lengths[:, None]
    valid = inside[:, :, None] & (positions[None] >= 0) & (positions[None] < lengths[:, None, None])
    target_pos = frame_ids[None, :] + labels[:, None]
    counted = inside & (target_pos >= 0) & (target_pos < lengths[:, None])
    correct_lag_position = (shifts[None, :] == labels[:, None]).astype(jnp.float32)
    lag_similarity_logits = (
        logit_sharpening_divisor
        * lagged_inner_terms
        * reciprocal_visual_length[:, :, None]
        * reciprocal_lag_strip
    )
    exponentiated_logits = jnp.where(valid, jnp.exp(lag_similarity_logits), 0.0)
    partition_sums = jnp.where(inside, jnp.sum(exponentiated_logits, axis=2), 1.0)
    picked = jnp.sum(lag_similarity_logits * correct_lag_position[:, None, :], axis=2)
    loss_local = jnp.sum(jnp.where(counted, jnp.log(partition_sums) - picked, 0.0))
    normalized_probabilities = jnp.where(counted, loss_scale / count, 0.0)
    logit_derivative = (
        logit_sharpening_divisor
        * normalized_probabilities[:, :, None]
        * (exponentiated_logits / partition_sums[:, :, None] - correct_lag_position[:, None, :])
    )
    grad_dots = (
        logit_derivative * reciprocal_visual_length[:, :, None] * reciprocal_lag_strip
    ).astype(jnp.bfloat16)
    grad_inv_v = jnp.sum(logit_derivative * lagged_inner_terms * reciprocal_lag_strip, axis=2)
    grad_inv_win = jnp.sum(
        spread_band(
            logit_derivative * lagged_inner_terms * reciprocal_visual_length[:, :, None], wide_len
        ),
        axis=1,
    )
    band_full = spread_band(grad_dots, wide_len)
    lip_sum = jnp.einsum("cfw,cwe->cfe", band_full, window, preferred_element_type=jnp.float32)
    lip_vals = emb_v.astype(jnp.float32)
    grad_lip = (
        lip_sum
        - (
            reciprocal_visual_length
            * reciprocal_visual_length
            * reciprocal_visual_length
            * grad_inv_v
        )[:, :, None]
        * lip_vals
    ).astype(jnp.bfloat16)
    win_sum = jnp.einsum("cfw,cfe->cwe", band_full, emb_v, preferred_element_type=jnp.float32)
    win_sum = win_sum - (inv_win * inv_win * inv_win * grad_inv_win)[:, :, None] * window.astype(
        jnp.float32
    )
    own_grad = win_sum[:, SPAN : SPAN + frame_num]
    from_after = from_behind(win_sum[:, :SPAN], "tm", -1)
    from_before = from_behind(win_sum[:, frame_num + SPAN :], "tm", 1)
    own_grad = own_grad.at[:, frame_num - SPAN :].add(from_after)
    own_grad = own_grad.at[:, :SPAN].add(from_before)
    grad_audio = own_grad.astype(jnp.bfloat16).reshape(clip_num * frame_num, width)
    grad_lip = grad_lip.reshape(clip_num * frame_num, width)
    grad_ap = proj_grad(hid_a, grad_audio)
    grad_vp = proj_grad(hid_v, grad_lip)
    grad_ac = conv_grad(cols_a, pre_a, grad_audio, w_audio_proj, w_audio_conv)
    grad_vc = conv_grad(cols_v, pre_v, grad_lip, w_lip_proj, w_lip_conv)
    parts = (grad_ac, grad_vc, grad_ap, grad_vp)
    lanes = grad_ap.shape[1]
    flat = jnp.concatenate([g.reshape(-1, lanes) for g in parts], axis=0)
    loss_block = jnp.zeros((8, 128), jnp.float32).at[0, 0].set(loss_local)
    total, loss_total = all_sum(flat, loss_block)
    outs = []
    start = 0
    for g in parts:
        rows = g.size // lanes
        outs.append(total[start : start + rows].reshape(g.shape))
        start += rows
    grad_ac, grad_vc, grad_ap, grad_vp = outs
    loss_sum = loss_total[0, 0]
    return (loss_sum / count, grad_ac, grad_ap, grad_vc, grad_vp)


def solution(mesh):
    placed = (
        P("clip", "tm", None),
        P("clip", "tm", None),
        P("clip"),
        P("clip"),
        P(),
        P(),
        P(),
        P(),
    )
    return jax.shard_map(
        shards, mesh=mesh, in_specs=placed, out_specs=(P(), P(), P(), P(), P()), check_vma=False
    )
```

```python
import jax
import jax.numpy as jnp
from jax import lax
from jax.sharding import PartitionSpec as P
import functools
from jax.experimental import pallas as pl
from jax.experimental.pallas import tpu as pltpu

SPAN = 15


MESH_ID = pl.DeviceIdType.MESH


def _coords():
    ci = lax.axis_index("clip")
    ti = lax.axis_index("tm")
    return ci, ti, ci % 4, (ci // 4) % 4, ci // 16, ti % 2, ti // 2


def _levels():
    ci, ti, y, x, zh, core, zl = _coords()
    z = zh * 4 + zl

    def at_y(v):
        return (zh * 16 + x * 4 + v % 4, ti)

    def at_x(v):
        return (zh * 16 + (v % 4) * 4 + y, ti)

    def at_z(v):
        w = v % 8
        return ((w // 4) * 16 + x * 4 + y, (w % 4) * 2 + core)

    def at_c(v):
        return (ci, zl * 2 + v % 2)

    def at_h(v):
        return ((v % 2) * 16 + x * 4 + y, ti)

    return {
        "c": (2, core, at_c, 1),
        "y": (4, y, at_y, 2),
        "x": (4, x, at_x, 2),
        "z": (8, z, at_z, 1),
        "h": (2, zh, at_h, 1),
    }


def _barrier(levels):
    barrier = pltpu.get_barrier_semaphore()
    peers = []
    for n, me, nbr, ndir in levels:
        peers.append(nbr(me + 1))
        if n > 2:
            peers.append(nbr(me - 1))
    for p in peers:
        pl.semaphore_signal(barrier, inc=1, device_id=p, device_id_type=MESH_ID)
    pl.semaphore_wait(barrier, len(peers))


def _small_start(n, me, nbr, s, tbuf, toff, tsend, trecv, tsem):
    at = toff + (me - s) % n
    c = pltpu.make_async_remote_copy(
        src_ref=tbuf.at[at],
        dst_ref=tbuf.at[at],
        send_sem=tsend.at[tsem],
        recv_sem=trecv.at[tsem],
        device_id=nbr(me + 1),
        device_id_type=MESH_ID,
    )
    c.start()
    return c


def _small_sum(n, tbuf, toff):
    acc = tbuf[toff]
    for k in range(1, n):
        acc = acc + tbuf[toff + k]
    return acc


def _small_kernel(names, t_ref, to_ref, tbuf, tsend, trecv):
    table = _levels()
    levels = [table[k] for k in names]
    barrier = pltpu.get_barrier_semaphore()
    peers = [nbr(me + j) for n, me, nbr, ndir in levels for j in range(1, n)]
    for p in peers:
        pl.semaphore_signal(barrier, inc=1, device_id=p, device_id_type=MESH_ID)
    pl.semaphore_wait(barrier, len(peers))
    toff = 0
    tsem = 0
    for li, (n, me, nbr, ndir) in enumerate(levels):
        tbuf[toff + me] = t_ref[...] if li == 0 else to_ref[...]
        copies = []
        for j in range(1, n):
            c = pltpu.make_async_remote_copy(
                src_ref=tbuf.at[toff + me],
                dst_ref=tbuf.at[toff + me],
                send_sem=tsend.at[tsem],
                recv_sem=trecv.at[tsem],
                device_id=nbr(me + j),
                device_id_type=MESH_ID,
            )
            c.start()
            copies.append(c)
            tsem += 1
        for c in copies:
            c.wait()
        to_ref[...] = _small_sum(n, tbuf, toff)
        toff += n


def small_sum(t, names, cid):
    table_n = {"c": 2, "y": 4, "x": 4, "z": 8, "h": 2}
    slots = sum(table_n[k] for k in names)
    sems = sum(table_n[k] - 1 for k in names)
    return pl.pallas_call(
        functools.partial(_small_kernel, names),
        out_shape=jax.ShapeDtypeStruct(t.shape, t.dtype),
        in_specs=[pl.BlockSpec(memory_space=pltpu.VMEM)],
        out_specs=pl.BlockSpec(memory_space=pltpu.VMEM),
        scratch_shapes=[
            pltpu.VMEM((slots,) + t.shape, t.dtype),
            pltpu.SemaphoreType.DMA((sems,)),
            pltpu.SemaphoreType.DMA((sems,)),
        ],
        compiler_params=pltpu.CompilerParams(collective_id=cid, has_side_effects=True),
    )(t)


def _rs_stage(tasks, work, rbuf, send_sem, recv_sem, slot, sem, rider=None):
    n = tasks[0][0]
    for s in range(n - 1):
        copies = []
        for tn, me, nbr, ndir, base, size, own in tasks:
            chunk = size // tn
            piece = chunk // ndir
            for d in range(ndir):
                sign = 1 if d == 0 else -1
                send_at = pl.multiple_of(base + ((me - sign * (s + 1)) % tn) * chunk + d * piece, 8)
                recv_at = pl.multiple_of(base + ((me - sign * (s + 2)) % tn) * chunk + d * piece, 8)
                src = own if s == 0 else work
                c = pltpu.make_async_remote_copy(
                    src_ref=src.at[pl.ds(send_at, piece)],
                    dst_ref=rbuf.at[pl.ds(slot, piece)],
                    send_sem=send_sem.at[sem],
                    recv_sem=recv_sem.at[sem],
                    device_id=nbr(me + sign),
                    device_id_type=MESH_ID,
                )
                c.start()
                copies.append((c, slot, recv_at, piece, own))
                slot += piece
                sem += 1
        ride = rider(s) if rider is not None else None
        for c, sl, recv_at, piece, own in copies:
            c.wait_recv()
            at = pl.ds(recv_at, piece)
            work[at] = rbuf[pl.ds(sl, piece)] + own[at]
        for c, sl, recv_at, piece, own in copies:
            c.wait_send()
        if ride is not None:
            ride.wait()
    return slot, sem


def _ag_stage(tasks, o_ref, send_sem, recv_sem, sem):
    n = tasks[0][0]
    for s in range(n - 1):
        copies = []
        for tn, me, nbr, ndir, base, size, own in tasks:
            chunk = size // tn
            piece = chunk // ndir
            for d in range(ndir):
                sign = 1 if d == 0 else -1
                at = pl.ds(pl.multiple_of(base + ((me - sign * s) % tn) * chunk + d * piece, 8), piece)
                c = pltpu.make_async_remote_copy(
                    src_ref=o_ref.at[at],
                    dst_ref=o_ref.at[at],
                    send_sem=send_sem.at[sem],
                    recv_sem=recv_sem.at[sem],
                    device_id=nbr(me + sign),
                    device_id_type=MESH_ID,
                )
                c.start()
                copies.append(c)
                sem += 1
        for c in copies:
            c.wait()
    return sem


def _pass_copy(buf, at, nbr, target, sems, idx):
    c = pltpu.make_async_remote_copy(
        src_ref=buf.at[at],
        dst_ref=buf.at[at],
        send_sem=sems[0].at[idx],
        recv_sem=sems[1].at[idx],
        device_id=nbr(target),
        device_id_type=MESH_ID,
    )
    c.start()
    return c


def _kernel(rows, x_ref, t_ref, o_ref, to_ref, work, rbuf, zbuf, send_sem, recv_sem, tbuf, tsend, trecv):
    table = _levels()
    lc, ly, lx, lz = (table[k] for k in ("c", "y", "x", "z"))
    _barrier([lc, ly, lx, lz])
    tsems = (tsend, trecv)
    state = {"toff": 0, "tsem": 0}

    def tiny_level(level, first):
        n, me, nbr, ndir = level
        toff = state["toff"]
        tbuf[toff + me] = t_ref[...] if first else to_ref[...]

        def rider(s):
            c = _pass_copy(tbuf, toff + (me - s) % n, nbr, me + 1, tsems, state["tsem"])
            state["tsem"] += 1
            return c

        return rider

    def tiny_done(n):
        to_ref[...] = _small_sum(n, tbuf, state["toff"])
        state["toff"] += n

    slot, sem = 0, 0
    half = rows // 2
    quarter = rows // 4
    nc, core, nbc, _ = lc
    ny, yi, nby, _ = ly
    nx, xi, nbx, _ = lx
    nz, zi, nbz, _ = lz

    rider = tiny_level(lc, True)
    slot, sem = _rs_stage([(nc, core, nbc, 1, 0, rows, x_ref)], work, rbuf, send_sem, recv_sem, slot, sem, rider)
    tiny_done(nc)
    r0 = core * half
    a1, b1 = r0, r0 + quarter
    rider = tiny_level(ly, False)
    slot, sem = _rs_stage(
        [(ny, yi, nby, 2, a1, quarter, work), (nx, xi, nbx, 2, b1, quarter, work)],
        work, rbuf, send_sem, recv_sem, slot, sem, rider,
    )
    tiny_done(ny)
    c1 = quarter // 4
    a2, b2 = a1 + yi * c1, b1 + xi * c1
    rider = tiny_level(lx, False)
    slot, sem = _rs_stage(
        [(nx, xi, nbx, 1, a2, c1, work), (ny, yi, nby, 1, b2, c1, work)],
        work, rbuf, send_sem, recv_sem, slot, sem, rider,
    )
    tiny_done(nx)
    c2 = c1 // 4
    a3, b3 = a2 + xi * c2, b2 + yi * c2
    zbuf[zi, 0] = work[pl.ds(pl.multiple_of(a3, 8), c2)]
    zbuf[zi, 1] = work[pl.ds(pl.multiple_of(b3, 8), c2)]
    toff = state["toff"]
    tbuf[toff + zi] = to_ref[...]
    right = nz // 2
    left = nz - 1 - right
    for s in range(right):
        cs = [
            _pass_copy(zbuf, (zi - s) % nz, nbz, zi + 1, (send_sem, recv_sem), sem),
            _pass_copy(tbuf, toff + (zi - s) % nz, nbz, zi + 1, tsems, state["tsem"]),
        ]
        sem += 1
        state["tsem"] += 1
        if s < left:
            cs.append(_pass_copy(zbuf, (zi + s) % nz, nbz, zi - 1, (send_sem, recv_sem), sem))
            cs.append(_pass_copy(tbuf, toff + (zi + s) % nz, nbz, zi - 1, tsems, state["tsem"]))
            sem += 1
            state["tsem"] += 1
        for c in cs:
            c.wait()
    for colour, at in ((0, a3), (1, b3)):
        acc = zbuf[0, colour]
        for k in range(1, nz):
            acc = acc + zbuf[k, colour]
        o_ref[pl.ds(pl.multiple_of(at, 8), c2)] = acc
    tiny_done(nz)
    sem = _ag_stage([(nx, xi, nbx, 1, a2, c1, None), (ny, yi, nby, 1, b2, c1, None)], o_ref, send_sem, recv_sem, sem)
    sem = _ag_stage([(ny, yi, nby, 2, a1, quarter, None), (nx, xi, nbx, 2, b1, quarter, None)], o_ref, send_sem, recv_sem, sem)
    sem = _ag_stage([(nc, core, nbc, 1, 0, rows, None)], o_ref, send_sem, recv_sem, sem)


def _counts(rows):
    half, quarter = rows // 2, rows // 4
    c1 = quarter // 4
    slots = half + 3 * 2 * quarter // 4 + 3 * 2 * c1 // 4
    sems = 1 + 3 * 4 + 3 * 2 + 7 + 3 * 2 + 3 * 4 + 1
    return slots, sems, 2 + 4 + 4 + 8, 1 + 3 + 3 + 7


def all_sum(flat, small):
    rows = flat.shape[0]
    slots, sems, tslots, tsems = _counts(rows)
    c2 = rows // 64
    return pl.pallas_call(
        functools.partial(_kernel, rows),
        out_shape=(
            jax.ShapeDtypeStruct(flat.shape, flat.dtype),
            jax.ShapeDtypeStruct(small.shape, small.dtype),
        ),
        in_specs=[pl.BlockSpec(memory_space=pltpu.VMEM)] * 2,
        out_specs=(pl.BlockSpec(memory_space=pltpu.VMEM),) * 2,
        scratch_shapes=[
            pltpu.VMEM(flat.shape, flat.dtype),
            pltpu.VMEM((slots, flat.shape[1]), flat.dtype),
            pltpu.VMEM((8, 2, c2, flat.shape[1]), flat.dtype),
            pltpu.SemaphoreType.DMA((sems,)),
            pltpu.SemaphoreType.DMA((sems,)),
            pltpu.VMEM((tslots,) + small.shape, small.dtype),
            pltpu.SemaphoreType.DMA((tsems,)),
            pltpu.SemaphoreType.DMA((tsems,)),
        ],
        compiler_params=pltpu.CompilerParams(
            collective_id=0, has_side_effects=True, vmem_limit_bytes=48 * 1024 * 1024
        ),
    )(flat, small)


logit_sharpening_divisor = 10.0
loss_scale = 1024.0
epsilon = 1e-06


def padded_2(cells, sides, width):
    for axis, dim in sides:
        count = lax.axis_size(axis)
        ends = count - 1
        head = lax.slice_in_dim(cells, 0, width, axis=dim)
        tail = lax.slice_in_dim(cells, cells.shape[dim] - width, cells.shape[dim], axis=dim)
        cells = jnp.concatenate(
            [
                lax.ppermute(tail, axis, [(i, (i + 1) % count) for i in range(ends)]),
                cells,
                lax.ppermute(head, axis, [((i + 1) % count, i) for i in range(ends)]),
            ],
            axis=dim,
        )
    return cells


def from_behind(value, axis, steps):
    count = lax.axis_size(axis)
    initial, last = (max(0, -steps), min(count, count - steps))
    return lax.ppermute(value, axis, [(source, source + steps) for source in range(initial, last)])


def silu_slope(values):
    sigma = jax.nn.sigmoid(values)
    return sigma * (1.0 + values * (1.0 - sigma))


def encoder(padded, w_conv, w_proj):
    clip_num, frame_pad, chan_num = padded.shape
    frame_num = frame_pad - 2
    columns = jnp.concatenate(
        [padded[:, 0:frame_num], padded[:, 1 : frame_num + 1], padded[:, 2 : frame_num + 2]], axis=2
    )
    before = jnp.einsum(
        "cfk,ke->cfe",
        columns,
        w_conv.reshape(3 * chan_num, w_conv.shape[2]),
        preferred_element_type=jnp.float32,
    )
    hidden = jax.nn.silu(before).astype(jnp.bfloat16)
    embedded = jnp.einsum("cfe,eg->cfg", hidden, w_proj, preferred_element_type=jnp.float32).astype(
        jnp.bfloat16
    )
    return (columns, before, hidden, embedded)


def inverse_norm(embedded):
    values = embedded.astype(jnp.float32)
    return lax.rsqrt(jnp.sum(values * values, axis=-1) + epsilon)


def spread_band(band, wide_len):
    clip_num, row_num, band_len = band.shape
    full_band = jnp.pad(band, ((0, 0), (0, 0), (0, wide_len + 1 - band_len)))
    flat_band = full_band.reshape(clip_num, row_num * (wide_len + 1))[:, : row_num * wide_len]
    return flat_band.reshape(clip_num, row_num, wide_len)


def narrow_band(matrix, band_len):
    clip_num, row_num, wide_len = matrix.shape
    flat_mat = jnp.pad(matrix.reshape(clip_num, row_num * wide_len), ((0, 0), (0, row_num)))
    return flat_mat.reshape(clip_num, row_num, wide_len + 1)[:, :, :band_len]


def flatten_rows(values):
    return values.reshape(values.shape[0] * values.shape[1], values.shape[2])


def proj_grad(hidden, grad_emb):
    return jnp.einsum("re,rf->ef", hidden, grad_emb, preferred_element_type=jnp.float32)


def conv_grad(columns, before, grad_emb, w_proj, w_conv):
    grad_hidden = jnp.einsum("rf,ef->re", grad_emb, w_proj, preferred_element_type=jnp.float32)
    grad_before = (grad_hidden * silu_slope(before)).astype(jnp.bfloat16)
    grad_conv = jnp.einsum("rk,re->ke", columns, grad_before, preferred_element_type=jnp.float32)
    return grad_conv.reshape(w_conv.shape)


def shards(
    audio_feats, lip_feats, lengths, labels, w_audio_conv, w_audio_proj, w_lip_conv, w_lip_proj
):
    clip_num, frame_num, chan_num = audio_feats.shape
    width = w_audio_proj.shape[1]
    offsets = 2 * SPAN + 1
    wide_len = frame_num + 2 * SPAN
    first_frame = lax.axis_index("tm") * frame_num
    stacked = jnp.stack([audio_feats, lip_feats])
    padded = padded_2(stacked, (("tm", 2),), 1)
    cols_a, pre_a, hid_a, emb_a = encoder(padded[0], w_audio_conv, w_audio_proj)
    cols_v, pre_v, hid_v, emb_v = encoder(padded[1], w_lip_conv, w_lip_proj)
    window = padded_2(emb_a, (("tm", 1),), SPAN)
    cols_a, pre_a, hid_a = (flatten_rows(cols_a), flatten_rows(pre_a), flatten_rows(hid_a))
    cols_v, pre_v, hid_v = (flatten_rows(cols_v), flatten_rows(pre_v), flatten_rows(hid_v))
    count_part = jnp.sum(lengths - jnp.abs(labels))
    count_block = jnp.zeros((8, 128), jnp.int32).at[0, 0].set(count_part)
    count = small_sum(count_block, ("y", "x", "h"), 1)[0, 0].astype(jnp.float32)
    matrix = jnp.einsum("cfe,cwe->cfw", emb_v, window, preferred_element_type=jnp.float32)
    lagged_inner_terms = narrow_band(matrix, offsets)
    inv_win = inverse_norm(window)
    reciprocal_visual_length = inverse_norm(emb_v)
    reciprocal_lag_strip = jnp.stack(
        [inv_win[:, offset : offset + frame_num] for offset in range(offsets)], axis=2
    )
    frame_ids = first_frame + jnp.arange(frame_num, dtype=jnp.int32)
    shifts = jnp.arange(offsets, dtype=jnp.int32) - SPAN
    positions = frame_ids[:, None] + shifts[None, :]
    inside = frame_ids[None, :] < lengths[:, None]
    valid = inside[:, :, None] & (positions[None] >= 0) & (positions[None] < lengths[:, None, None])
    target_pos = frame_ids[None, :] + labels[:, None]
    counted = inside & (target_pos >= 0) & (target_pos < lengths[:, None])
    correct_lag_position = (shifts[None, :] == labels[:, None]).astype(jnp.float32)
    lag_similarity_logits = (
        logit_sharpening_divisor
        * lagged_inner_terms
        * reciprocal_visual_length[:, :, None]
        * reciprocal_lag_strip
    )
    exponentiated_logits = jnp.where(valid, jnp.exp(lag_similarity_logits), 0.0)
    partition_sums = jnp.where(inside, jnp.sum(exponentiated_logits, axis=2), 1.0)
    picked = jnp.sum(lag_similarity_logits * correct_lag_position[:, None, :], axis=2)
    loss_local = jnp.sum(jnp.where(counted, jnp.log(partition_sums) - picked, 0.0))
    normalized_probabilities = jnp.where(counted, loss_scale / count, 0.0)
    logit_derivative = (
        logit_sharpening_divisor
        * normalized_probabilities[:, :, None]
        * (exponentiated_logits / partition_sums[:, :, None] - correct_lag_position[:, None, :])
    )
    grad_dots = (
        logit_derivative * reciprocal_visual_length[:, :, None] * reciprocal_lag_strip
    ).astype(jnp.bfloat16)
    grad_inv_v = jnp.sum(logit_derivative * lagged_inner_terms * reciprocal_lag_strip, axis=2)
    grad_inv_win = jnp.sum(
        spread_band(
            logit_derivative * lagged_inner_terms * reciprocal_visual_length[:, :, None], wide_len
        ),
        axis=1,
    )
    band_full = spread_band(grad_dots, wide_len)
    lip_sum = jnp.einsum("cfw,cwe->cfe", band_full, window, preferred_element_type=jnp.float32)
    lip_vals = emb_v.astype(jnp.float32)
    grad_lip = (
        lip_sum
        - (
            reciprocal_visual_length
            * reciprocal_visual_length
            * reciprocal_visual_length
            * grad_inv_v
        )[:, :, None]
        * lip_vals
    ).astype(jnp.bfloat16)
    win_sum = jnp.einsum("cfw,cfe->cwe", band_full, emb_v, preferred_element_type=jnp.float32)
    win_sum = win_sum - (inv_win * inv_win * inv_win * grad_inv_win)[:, :, None] * window.astype(
        jnp.float32
    )
    own_grad = win_sum[:, SPAN : SPAN + frame_num]
    from_after = from_behind(win_sum[:, :SPAN], "tm", -1)
    from_before = from_behind(win_sum[:, frame_num + SPAN :], "tm", 1)
    own_grad = own_grad.at[:, frame_num - SPAN :].add(from_after)
    own_grad = own_grad.at[:, :SPAN].add(from_before)
    grad_audio = own_grad.astype(jnp.bfloat16).reshape(clip_num * frame_num, width)
    grad_lip = grad_lip.reshape(clip_num * frame_num, width)
    grad_ap = proj_grad(hid_a, grad_audio)
    grad_vp = proj_grad(hid_v, grad_lip)
    grad_ac = conv_grad(cols_a, pre_a, grad_audio, w_audio_proj, w_audio_conv)
    grad_vc = conv_grad(cols_v, pre_v, grad_lip, w_lip_proj, w_lip_conv)
    parts = (grad_ac, grad_vc, grad_ap, grad_vp)
    lanes = grad_ap.shape[1]
    flat = jnp.concatenate([g.reshape(-1, lanes) for g in parts], axis=0)
    loss_block = jnp.zeros((8, 128), jnp.float32).at[0, 0].set(loss_local)
    total, loss_total = all_sum(flat, loss_block)
    outs = []
    start = 0
    for g in parts:
        rows = g.size // lanes
        outs.append(total[start : start + rows].reshape(g.shape))
        start += rows
    grad_ac, grad_vc, grad_ap, grad_vp = outs
    loss_sum = loss_total[0, 0]
    return (loss_sum / count, grad_ac, grad_ap, grad_vc, grad_vp)


def solution(mesh):
    placed = (
        P("clip", "tm", None),
        P("clip", "tm", None),
        P("clip"),
        P("clip"),
        P(),
        P(),
        P(),
        P(),
    )
    return jax.shard_map(
        shards, mesh=mesh, in_specs=placed, out_specs=(P(), P(), P(), P(), P()), check_vma=False
    )
```

```python
import jax
import jax.numpy as jnp
from jax import lax
from jax.sharding import PartitionSpec as P
import functools
from jax.experimental import pallas as pl
from jax.experimental.pallas import tpu as pltpu

SPAN = 15


MESH_ID = pl.DeviceIdType.MESH


def _coords():
    ci = lax.axis_index("clip")
    ti = lax.axis_index("tm")
    return ci, ti, ci % 4, (ci // 4) % 4, ci // 16, ti % 2, ti // 2


def _levels():
    ci, ti, y, x, zh, core, zl = _coords()
    z = zh * 4 + zl

    def at_y(v):
        return (zh * 16 + x * 4 + v % 4, ti)

    def at_x(v):
        return (zh * 16 + (v % 4) * 4 + y, ti)

    def at_z(v):
        w = v % 8
        return ((w // 4) * 16 + x * 4 + y, (w % 4) * 2 + core)

    def at_c(v):
        return (ci, zl * 2 + v % 2)

    def at_h(v):
        return ((v % 2) * 16 + x * 4 + y, ti)

    return {
        "c": (2, core, at_c, 1),
        "y": (4, y, at_y, 2),
        "x": (4, x, at_x, 2),
        "z": (8, z, at_z, 1),
        "h": (2, zh, at_h, 1),
    }


def _barrier(levels):
    barrier = pltpu.get_barrier_semaphore()
    peers = []
    for n, me, nbr, ndir in levels:
        peers.append(nbr(me + 1))
        if n > 2:
            peers.append(nbr(me - 1))
    for p in peers:
        pl.semaphore_signal(barrier, inc=1, device_id=p, device_id_type=MESH_ID)
    pl.semaphore_wait(barrier, len(peers))


def _small_start(n, me, nbr, s, tbuf, toff, tsend, trecv, tsem):
    at = toff + (me - s) % n
    c = pltpu.make_async_remote_copy(
        src_ref=tbuf.at[at],
        dst_ref=tbuf.at[at],
        send_sem=tsend.at[tsem],
        recv_sem=trecv.at[tsem],
        device_id=nbr(me + 1),
        device_id_type=MESH_ID,
    )
    c.start()
    return c


def _small_sum(n, tbuf, toff):
    acc = tbuf[toff]
    for k in range(1, n):
        acc = acc + tbuf[toff + k]
    return acc


def _small_kernel(names, t_ref, to_ref, tbuf, tsend, trecv):
    table = _levels()
    levels = [table[k] for k in names]
    barrier = pltpu.get_barrier_semaphore()
    peers = [nbr(me + j) for n, me, nbr, ndir in levels for j in range(1, n)]
    for p in peers:
        pl.semaphore_signal(barrier, inc=1, device_id=p, device_id_type=MESH_ID)
    pl.semaphore_wait(barrier, len(peers))
    toff = 0
    tsem = 0
    for li, (n, me, nbr, ndir) in enumerate(levels):
        tbuf[toff + me] = t_ref[...] if li == 0 else to_ref[...]
        copies = []
        for j in range(1, n):
            c = pltpu.make_async_remote_copy(
                src_ref=tbuf.at[toff + me],
                dst_ref=tbuf.at[toff + me],
                send_sem=tsend.at[tsem],
                recv_sem=trecv.at[tsem],
                device_id=nbr(me + j),
                device_id_type=MESH_ID,
            )
            c.start()
            copies.append(c)
            tsem += 1
        for c in copies:
            c.wait()
        to_ref[...] = _small_sum(n, tbuf, toff)
        toff += n


def small_sum(t, names, cid):
    table_n = {"c": 2, "y": 4, "x": 4, "z": 8, "h": 2}
    slots = sum(table_n[k] for k in names)
    sems = sum(table_n[k] - 1 for k in names)
    return pl.pallas_call(
        functools.partial(_small_kernel, names),
        out_shape=jax.ShapeDtypeStruct(t.shape, t.dtype),
        in_specs=[pl.BlockSpec(memory_space=pltpu.VMEM)],
        out_specs=pl.BlockSpec(memory_space=pltpu.VMEM),
        scratch_shapes=[
            pltpu.VMEM((slots,) + t.shape, t.dtype),
            pltpu.SemaphoreType.DMA((sems,)),
            pltpu.SemaphoreType.DMA((sems,)),
        ],
        compiler_params=pltpu.CompilerParams(collective_id=cid, has_side_effects=True),
    )(t)


def _rs_stage(tasks, work, rbuf, send_sem, recv_sem, slot, sem, rider=None):
    n = tasks[0][0]
    for s in range(n - 1):
        copies = []
        for tn, me, nbr, ndir, base, size, own in tasks:
            chunk = size // tn
            piece = chunk // ndir
            for d in range(ndir):
                sign = 1 if d == 0 else -1
                send_at = pl.multiple_of(base + ((me - sign * (s + 1)) % tn) * chunk + d * piece, 8)
                recv_at = pl.multiple_of(base + ((me - sign * (s + 2)) % tn) * chunk + d * piece, 8)
                src = own if s == 0 else work
                c = pltpu.make_async_remote_copy(
                    src_ref=src.at[pl.ds(send_at, piece)],
                    dst_ref=rbuf.at[pl.ds(slot, piece)],
                    send_sem=send_sem.at[sem],
                    recv_sem=recv_sem.at[sem],
                    device_id=nbr(me + sign),
                    device_id_type=MESH_ID,
                )
                c.start()
                copies.append((c, slot, recv_at, piece, own))
                slot += piece
                sem += 1
        ride = rider(s) if rider is not None else None
        for c, sl, recv_at, piece, own in copies:
            c.wait_recv()
            at = pl.ds(recv_at, piece)
            work[at] = rbuf[pl.ds(sl, piece)] + own[at]
        for c, sl, recv_at, piece, own in copies:
            c.wait_send()
        if ride is not None:
            ride.wait()
    return slot, sem


def _ag_stage(tasks, o_ref, send_sem, recv_sem, sem):
    n = tasks[0][0]
    for s in range(n - 1):
        copies = []
        for tn, me, nbr, ndir, base, size, own in tasks:
            chunk = size // tn
            piece = chunk // ndir
            for d in range(ndir):
                sign = 1 if d == 0 else -1
                at = pl.ds(pl.multiple_of(base + ((me - sign * s) % tn) * chunk + d * piece, 8), piece)
                c = pltpu.make_async_remote_copy(
                    src_ref=o_ref.at[at],
                    dst_ref=o_ref.at[at],
                    send_sem=send_sem.at[sem],
                    recv_sem=recv_sem.at[sem],
                    device_id=nbr(me + sign),
                    device_id_type=MESH_ID,
                )
                c.start()
                copies.append(c)
                sem += 1
        for c in copies:
            c.wait()
    return sem


def _pass_copy(buf, at, nbr, target, sems, idx):
    c = pltpu.make_async_remote_copy(
        src_ref=buf.at[at],
        dst_ref=buf.at[at],
        send_sem=sems[0].at[idx],
        recv_sem=sems[1].at[idx],
        device_id=nbr(target),
        device_id_type=MESH_ID,
    )
    c.start()
    return c


def _kernel(rows, x_ref, t_ref, o_ref, to_ref, work, rbuf, zbuf, send_sem, recv_sem, tbuf, tsend, trecv):
    table = _levels()
    lc, ly, lx, lz = (table[k] for k in ("c", "y", "x", "z"))
    _barrier([lc, ly, lx, lz])
    tsems = (tsend, trecv)
    state = {"toff": 0, "tsem": 0}

    def tiny_level(level, first):
        n, me, nbr, ndir = level
        toff = state["toff"]
        tbuf[toff + me] = t_ref[...] if first else to_ref[...]

        def rider(s):
            c = _pass_copy(tbuf, toff + (me - s) % n, nbr, me + 1, tsems, state["tsem"])
            state["tsem"] += 1
            return c

        return rider

    def tiny_done(n):
        to_ref[...] = _small_sum(n, tbuf, state["toff"])
        state["toff"] += n

    slot, sem = 0, 0
    half = rows // 2
    quarter = rows // 4
    nc, core, nbc, _ = lc
    ny, yi, nby, _ = ly
    nx, xi, nbx, _ = lx
    nz, zi, nbz, _ = lz

    rider = tiny_level(lc, True)
    slot, sem = _rs_stage([(nc, core, nbc, 1, 0, rows, x_ref)], work, rbuf, send_sem, recv_sem, slot, sem, rider)
    tiny_done(nc)
    r0 = core * half
    a1, b1 = r0, r0 + quarter
    rider = tiny_level(ly, False)
    slot, sem = _rs_stage(
        [(ny, yi, nby, 2, a1, quarter, work), (nx, xi, nbx, 2, b1, quarter, work)],
        work, rbuf, send_sem, recv_sem, slot, sem, rider,
    )
    tiny_done(ny)
    c1 = quarter // 4
    a2, b2 = a1 + yi * c1, b1 + xi * c1
    rider = tiny_level(lx, False)
    slot, sem = _rs_stage(
        [(nx, xi, nbx, 1, a2, c1, work), (ny, yi, nby, 1, b2, c1, work)],
        work, rbuf, send_sem, recv_sem, slot, sem, rider,
    )
    tiny_done(nx)
    c2 = c1 // 4
    a3, b3 = a2 + xi * c2, b2 + yi * c2
    zbuf[zi, 0] = work[pl.ds(pl.multiple_of(a3, 8), c2)]
    zbuf[zi, 1] = work[pl.ds(pl.multiple_of(b3, 8), c2)]
    toff = state["toff"]
    tbuf[toff + zi] = to_ref[...]
    right = nz // 2
    left = nz - 1 - right
    for s in range(right):
        cs = [
            _pass_copy(zbuf, (zi - s) % nz, nbz, zi + 1, (send_sem, recv_sem), sem),
            _pass_copy(tbuf, toff + (zi - s) % nz, nbz, zi + 1, tsems, state["tsem"]),
        ]
        sem += 1
        state["tsem"] += 1
        if s < left:
            cs.append(_pass_copy(zbuf, (zi + s) % nz, nbz, zi - 1, (send_sem, recv_sem), sem))
            cs.append(_pass_copy(tbuf, toff + (zi + s) % nz, nbz, zi - 1, tsems, state["tsem"]))
            sem += 1
            state["tsem"] += 1
        for c in cs:
            c.wait()
    for colour, at in ((0, a3), (1, b3)):
        acc = zbuf[0, colour]
        for k in range(1, nz):
            acc = acc + zbuf[k, colour]
        o_ref[pl.ds(pl.multiple_of(at, 8), c2)] = acc
    tiny_done(nz)
    sem = _ag_stage([(nx, xi, nbx, 1, a2, c1, None), (ny, yi, nby, 1, b2, c1, None)], o_ref, send_sem, recv_sem, sem)
    sem = _ag_stage([(ny, yi, nby, 2, a1, quarter, None), (nx, xi, nbx, 2, b1, quarter, None)], o_ref, send_sem, recv_sem, sem)
    sem = _ag_stage([(nc, core, nbc, 1, 0, rows, None)], o_ref, send_sem, recv_sem, sem)


def _counts(rows):
    half, quarter = rows // 2, rows // 4
    c1 = quarter // 4
    slots = half + 3 * 2 * quarter // 4 + 3 * 2 * c1 // 4
    sems = 1 + 3 * 4 + 3 * 2 + 7 + 3 * 2 + 3 * 4 + 1
    return slots, sems, 2 + 4 + 4 + 8, 1 + 3 + 3 + 7


def all_sum(flat, small):
    rows = flat.shape[0]
    slots, sems, tslots, tsems = _counts(rows)
    c2 = rows // 64
    return pl.pallas_call(
        functools.partial(_kernel, rows),
        out_shape=(
            jax.ShapeDtypeStruct(flat.shape, flat.dtype),
            jax.ShapeDtypeStruct(small.shape, small.dtype),
        ),
        in_specs=[pl.BlockSpec(memory_space=pltpu.VMEM)] * 2,
        out_specs=(pl.BlockSpec(memory_space=pltpu.VMEM),) * 2,
        scratch_shapes=[
            pltpu.VMEM(flat.shape, flat.dtype),
            pltpu.VMEM((slots, flat.shape[1]), flat.dtype),
            pltpu.VMEM((8, 2, c2, flat.shape[1]), flat.dtype),
            pltpu.SemaphoreType.DMA((sems,)),
            pltpu.SemaphoreType.DMA((sems,)),
            pltpu.VMEM((tslots,) + small.shape, small.dtype),
            pltpu.SemaphoreType.DMA((tsems,)),
            pltpu.SemaphoreType.DMA((tsems,)),
        ],
        compiler_params=pltpu.CompilerParams(
            collective_id=0, has_side_effects=True, vmem_limit_bytes=48 * 1024 * 1024
        ),
    )(flat, small)


def _corr_fwd_kernel(ev_ref, win_ref, inv_ref, dots_ref, strip_ref):
    wide = win_ref.shape[0]
    lanes = dots_ref.shape[1]
    m = lax.dot_general(
        ev_ref[...], win_ref[...], (((1,), (1,)), ((), ())), preferred_element_type=jnp.float32
    )
    dots_ref[...] = pltpu.roll(m, 0, 1, stride=1, stride_axis=0)[:, wide - lanes :]
    inv = jnp.broadcast_to(inv_ref[...], m.shape)
    strip_ref[...] = pltpu.roll(inv, 0, 1, stride=1, stride_axis=0)[:, wide - lanes :]


def corr_fwd(emb_v, win_pad, inv_pad):
    clips, frames, width = emb_v.shape
    wide = win_pad.shape[1]
    lanes = 128
    return pl.pallas_call(
        _corr_fwd_kernel,
        grid=(clips,),
        in_specs=[
            pl.BlockSpec((None, frames, width), lambda c: (c, 0, 0)),
            pl.BlockSpec((None, wide, width), lambda c: (c, 0, 0)),
            pl.BlockSpec((None, 1, wide), lambda c: (c, 0, 0)),
        ],
        out_specs=[
            pl.BlockSpec((None, frames, lanes), lambda c: (c, 0, 0)),
            pl.BlockSpec((None, frames, lanes), lambda c: (c, 0, 0)),
        ],
        out_shape=[
            jax.ShapeDtypeStruct((clips, frames, lanes), jnp.float32),
            jax.ShapeDtypeStruct((clips, frames, lanes), jnp.float32),
        ],
    )(emb_v, win_pad, inv_pad)


def _corr_bwd_kernel(gd_ref, at_ref, ev_ref, win_ref, lip_ref, wsum_ref, ginv_ref):
    frames, lanes = gd_ref.shape
    wide = win_ref.shape[0]
    pad = jnp.zeros((frames, wide - lanes), jnp.float32)
    g = jnp.concatenate([gd_ref[...].astype(jnp.float32), pad], axis=1)
    band = pltpu.roll(g, 0, 1, stride=1, stride_axis=0)
    lip_ref[...] = jnp.dot(band.astype(jnp.bfloat16), win_ref[...], preferred_element_type=jnp.float32)
    band_t = band.T.astype(jnp.bfloat16)
    wsum_ref[...] = jnp.dot(band_t, ev_ref[...], preferred_element_type=jnp.float32)
    a = jnp.concatenate([at_ref[...], pad], axis=1)
    spread = pltpu.roll(a, 0, 1, stride=1, stride_axis=0)
    ginv_ref[...] = jnp.sum(spread, axis=0, keepdims=True)


def corr_bwd(gd_pad, at_pad, emb_v, win_pad):
    clips, frames, width = emb_v.shape
    wide = win_pad.shape[1]
    lanes = gd_pad.shape[2]
    return pl.pallas_call(
        _corr_bwd_kernel,
        grid=(clips,),
        in_specs=[
            pl.BlockSpec((None, frames, lanes), lambda c: (c, 0, 0)),
            pl.BlockSpec((None, frames, lanes), lambda c: (c, 0, 0)),
            pl.BlockSpec((None, frames, width), lambda c: (c, 0, 0)),
            pl.BlockSpec((None, wide, width), lambda c: (c, 0, 0)),
        ],
        out_specs=[
            pl.BlockSpec((None, frames, width), lambda c: (c, 0, 0)),
            pl.BlockSpec((None, wide, width), lambda c: (c, 0, 0)),
            pl.BlockSpec((None, 1, wide), lambda c: (c, 0, 0)),
        ],
        out_shape=[
            jax.ShapeDtypeStruct((clips, frames, width), jnp.float32),
            jax.ShapeDtypeStruct((clips, wide, width), jnp.float32),
            jax.ShapeDtypeStruct((clips, 1, wide), jnp.float32),
        ],
    )(gd_pad, at_pad, emb_v, win_pad)


logit_sharpening_divisor = 10.0
loss_scale = 1024.0
epsilon = 1e-06


def padded_2(cells, sides, width):
    for axis, dim in sides:
        count = lax.axis_size(axis)
        ends = count - 1
        head = lax.slice_in_dim(cells, 0, width, axis=dim)
        tail = lax.slice_in_dim(cells, cells.shape[dim] - width, cells.shape[dim], axis=dim)
        cells = jnp.concatenate(
            [
                lax.ppermute(tail, axis, [(i, (i + 1) % count) for i in range(ends)]),
                cells,
                lax.ppermute(head, axis, [((i + 1) % count, i) for i in range(ends)]),
            ],
            axis=dim,
        )
    return cells


def from_behind(value, axis, steps):
    count = lax.axis_size(axis)
    initial, last = (max(0, -steps), min(count, count - steps))
    return lax.ppermute(value, axis, [(source, source + steps) for source in range(initial, last)])


def silu_slope(values):
    sigma = jax.nn.sigmoid(values)
    return sigma * (1.0 + values * (1.0 - sigma))


def encoder(padded, w_conv, w_proj):
    clip_num, frame_pad, chan_num = padded.shape
    frame_num = frame_pad - 2
    columns = jnp.concatenate(
        [padded[:, 0:frame_num], padded[:, 1 : frame_num + 1], padded[:, 2 : frame_num + 2]], axis=2
    )
    before = jnp.einsum(
        "cfk,ke->cfe",
        columns,
        w_conv.reshape(3 * chan_num, w_conv.shape[2]),
        preferred_element_type=jnp.float32,
    )
    hidden = jax.nn.silu(before).astype(jnp.bfloat16)
    embedded = jnp.einsum("cfe,eg->cfg", hidden, w_proj, preferred_element_type=jnp.float32).astype(
        jnp.bfloat16
    )
    return (columns, before, hidden, embedded)


def inverse_norm(embedded):
    values = embedded.astype(jnp.float32)
    return lax.rsqrt(jnp.sum(values * values, axis=-1) + epsilon)


def spread_band(band, wide_len):
    clip_num, row_num, band_len = band.shape
    full_band = jnp.pad(band, ((0, 0), (0, 0), (0, wide_len + 1 - band_len)))
    flat_band = full_band.reshape(clip_num, row_num * (wide_len + 1))[:, : row_num * wide_len]
    return flat_band.reshape(clip_num, row_num, wide_len)


def narrow_band(matrix, band_len):
    clip_num, row_num, wide_len = matrix.shape
    flat_mat = jnp.pad(matrix.reshape(clip_num, row_num * wide_len), ((0, 0), (0, row_num)))
    return flat_mat.reshape(clip_num, row_num, wide_len + 1)[:, :, :band_len]


def flatten_rows(values):
    return values.reshape(values.shape[0] * values.shape[1], values.shape[2])


def proj_grad(hidden, grad_emb):
    return jnp.einsum("re,rf->ef", hidden, grad_emb, preferred_element_type=jnp.float32)


def conv_grad(columns, before, grad_emb, w_proj, w_conv):
    grad_hidden = jnp.einsum("rf,ef->re", grad_emb, w_proj, preferred_element_type=jnp.float32)
    grad_before = (grad_hidden * silu_slope(before)).astype(jnp.bfloat16)
    grad_conv = jnp.einsum("rk,re->ke", columns, grad_before, preferred_element_type=jnp.float32)
    return grad_conv.reshape(w_conv.shape)


def shards(
    audio_feats, lip_feats, lengths, labels, w_audio_conv, w_audio_proj, w_lip_conv, w_lip_proj
):
    clip_num, frame_num, chan_num = audio_feats.shape
    width = w_audio_proj.shape[1]
    offsets = 2 * SPAN + 1
    wide_len = frame_num + 2 * SPAN
    first_frame = lax.axis_index("tm") * frame_num
    stacked = jnp.stack([audio_feats, lip_feats])
    padded = padded_2(stacked, (("tm", 2),), 1)
    cols_a, pre_a, hid_a, emb_a = encoder(padded[0], w_audio_conv, w_audio_proj)
    cols_v, pre_v, hid_v, emb_v = encoder(padded[1], w_lip_conv, w_lip_proj)
    window = padded_2(emb_a, (("tm", 1),), SPAN)
    cols_a, pre_a, hid_a = (flatten_rows(cols_a), flatten_rows(pre_a), flatten_rows(hid_a))
    cols_v, pre_v, hid_v = (flatten_rows(cols_v), flatten_rows(pre_v), flatten_rows(hid_v))
    count_part = jnp.sum(lengths - jnp.abs(labels))
    count_block = jnp.zeros((8, 128), jnp.int32).at[0, 0].set(count_part)
    count = small_sum(count_block, ("y", "x", "h"), 1)[0, 0].astype(jnp.float32)
    inv_win = inverse_norm(window)
    reciprocal_visual_length = inverse_norm(emb_v)
    wide_pad = -(-wide_len // 128) * 128
    win_pad = jnp.pad(window, ((0, 0), (0, wide_pad - wide_len), (0, 0)))
    inv_pad = jnp.pad(inv_win, ((0, 0), (0, wide_pad - wide_len)))[:, None, :]
    dots_rev, strip_rev = corr_fwd(emb_v, win_pad[:, ::-1], inv_pad[:, :, ::-1])
    lagged_inner_terms = dots_rev[:, :, ::-1][:, :, :offsets]
    reciprocal_lag_strip = strip_rev[:, :, ::-1][:, :, :offsets]
    frame_ids = first_frame + jnp.arange(frame_num, dtype=jnp.int32)
    shifts = jnp.arange(offsets, dtype=jnp.int32) - SPAN
    positions = frame_ids[:, None] + shifts[None, :]
    inside = frame_ids[None, :] < lengths[:, None]
    valid = inside[:, :, None] & (positions[None] >= 0) & (positions[None] < lengths[:, None, None])
    target_pos = frame_ids[None, :] + labels[:, None]
    counted = inside & (target_pos >= 0) & (target_pos < lengths[:, None])
    correct_lag_position = (shifts[None, :] == labels[:, None]).astype(jnp.float32)
    lag_similarity_logits = (
        logit_sharpening_divisor
        * lagged_inner_terms
        * reciprocal_visual_length[:, :, None]
        * reciprocal_lag_strip
    )
    exponentiated_logits = jnp.where(valid, jnp.exp(lag_similarity_logits), 0.0)
    partition_sums = jnp.where(inside, jnp.sum(exponentiated_logits, axis=2), 1.0)
    picked = jnp.sum(lag_similarity_logits * correct_lag_position[:, None, :], axis=2)
    loss_local = jnp.sum(jnp.where(counted, jnp.log(partition_sums) - picked, 0.0))
    normalized_probabilities = jnp.where(counted, loss_scale / count, 0.0)
    logit_derivative = (
        logit_sharpening_divisor
        * normalized_probabilities[:, :, None]
        * (exponentiated_logits / partition_sums[:, :, None] - correct_lag_position[:, None, :])
    )
    grad_dots = (
        logit_derivative * reciprocal_visual_length[:, :, None] * reciprocal_lag_strip
    ).astype(jnp.bfloat16)
    grad_inv_v = jnp.sum(logit_derivative * lagged_inner_terms * reciprocal_lag_strip, axis=2)
    audio_term = logit_derivative * lagged_inner_terms * reciprocal_visual_length[:, :, None]
    band_pad = ((0, 0), (0, 0), (0, 128 - offsets))
    lip_sum, win_sum_pad, ginv_pad = corr_bwd(
        jnp.pad(grad_dots, band_pad), jnp.pad(audio_term, band_pad), emb_v, win_pad
    )
    grad_inv_win = ginv_pad[:, 0, :wide_len]
    lip_vals = emb_v.astype(jnp.float32)
    grad_lip = (
        lip_sum
        - (
            reciprocal_visual_length
            * reciprocal_visual_length
            * reciprocal_visual_length
            * grad_inv_v
        )[:, :, None]
        * lip_vals
    ).astype(jnp.bfloat16)
    win_sum = win_sum_pad[:, :wide_len]
    win_sum = win_sum - (inv_win * inv_win * inv_win * grad_inv_win)[:, :, None] * window.astype(
        jnp.float32
    )
    own_grad = win_sum[:, SPAN : SPAN + frame_num]
    from_after = from_behind(win_sum[:, :SPAN], "tm", -1)
    from_before = from_behind(win_sum[:, frame_num + SPAN :], "tm", 1)
    own_grad = own_grad.at[:, frame_num - SPAN :].add(from_after)
    own_grad = own_grad.at[:, :SPAN].add(from_before)
    grad_audio = own_grad.astype(jnp.bfloat16).reshape(clip_num * frame_num, width)
    grad_lip = grad_lip.reshape(clip_num * frame_num, width)
    grad_ap = proj_grad(hid_a, grad_audio)
    grad_vp = proj_grad(hid_v, grad_lip)
    grad_ac = conv_grad(cols_a, pre_a, grad_audio, w_audio_proj, w_audio_conv)
    grad_vc = conv_grad(cols_v, pre_v, grad_lip, w_lip_proj, w_lip_conv)
    parts = (grad_ac, grad_vc, grad_ap, grad_vp)
    lanes = grad_ap.shape[1]
    flat = jnp.concatenate([g.reshape(-1, lanes) for g in parts], axis=0)
    loss_block = jnp.zeros((8, 128), jnp.float32).at[0, 0].set(loss_local)
    total, loss_total = all_sum(flat, loss_block)
    outs = []
    start = 0
    for g in parts:
        rows = g.size // lanes
        outs.append(total[start : start + rows].reshape(g.shape))
        start += rows
    grad_ac, grad_vc, grad_ap, grad_vp = outs
    loss_sum = loss_total[0, 0]
    return (loss_sum / count, grad_ac, grad_ap, grad_vc, grad_vp)


def solution(mesh):
    placed = (
        P("clip", "tm", None),
        P("clip", "tm", None),
        P("clip"),
        P("clip"),
        P(),
        P(),
        P(),
        P(),
    )
    return jax.shard_map(
        shards, mesh=mesh, in_specs=placed, out_specs=(P(), P(), P(), P(), P()), check_vma=False
    )
```

```python
import jax
import jax.numpy as jnp
from jax import lax
from jax.sharding import PartitionSpec as P
import functools
from jax.experimental import pallas as pl
from jax.experimental.pallas import tpu as pltpu

SPAN = 15


MESH_ID = pl.DeviceIdType.MESH


def _coords():
    ci = lax.axis_index("clip")
    ti = lax.axis_index("tm")
    return ci, ti, ci % 4, (ci // 4) % 4, ci // 16, ti % 2, ti // 2


def _levels():
    ci, ti, y, x, zh, core, zl = _coords()
    z = zh * 4 + zl

    def at_y(v):
        return (zh * 16 + x * 4 + v % 4, ti)

    def at_x(v):
        return (zh * 16 + (v % 4) * 4 + y, ti)

    def at_z(v):
        w = v % 8
        return ((w // 4) * 16 + x * 4 + y, (w % 4) * 2 + core)

    def at_c(v):
        return (ci, zl * 2 + v % 2)

    def at_h(v):
        return ((v % 2) * 16 + x * 4 + y, ti)

    return {
        "c": (2, core, at_c, 1),
        "y": (4, y, at_y, 2),
        "x": (4, x, at_x, 2),
        "z": (8, z, at_z, 1),
        "h": (2, zh, at_h, 1),
    }


def _barrier(levels):
    barrier = pltpu.get_barrier_semaphore()
    peers = []
    for n, me, nbr, ndir in levels:
        peers.append(nbr(me + 1))
        if n > 2:
            peers.append(nbr(me - 1))
    for p in peers:
        pl.semaphore_signal(barrier, inc=1, device_id=p, device_id_type=MESH_ID)
    pl.semaphore_wait(barrier, len(peers))


def _small_start(n, me, nbr, s, tbuf, toff, tsend, trecv, tsem):
    at = toff + (me - s) % n
    c = pltpu.make_async_remote_copy(
        src_ref=tbuf.at[at],
        dst_ref=tbuf.at[at],
        send_sem=tsend.at[tsem],
        recv_sem=trecv.at[tsem],
        device_id=nbr(me + 1),
        device_id_type=MESH_ID,
    )
    c.start()
    return c


def _small_sum(n, tbuf, toff):
    acc = tbuf[toff]
    for k in range(1, n):
        acc = acc + tbuf[toff + k]
    return acc


def _small_kernel(names, t_ref, to_ref, tbuf, tsend, trecv):
    table = _levels()
    levels = [table[k] for k in names]
    barrier = pltpu.get_barrier_semaphore()
    peers = [nbr(me + j) for n, me, nbr, ndir in levels for j in range(1, n)]
    for p in peers:
        pl.semaphore_signal(barrier, inc=1, device_id=p, device_id_type=MESH_ID)
    pl.semaphore_wait(barrier, len(peers))
    toff = 0
    tsem = 0
    for li, (n, me, nbr, ndir) in enumerate(levels):
        tbuf[toff + me] = t_ref[...] if li == 0 else to_ref[...]
        copies = []
        for j in range(1, n):
            c = pltpu.make_async_remote_copy(
                src_ref=tbuf.at[toff + me],
                dst_ref=tbuf.at[toff + me],
                send_sem=tsend.at[tsem],
                recv_sem=trecv.at[tsem],
                device_id=nbr(me + j),
                device_id_type=MESH_ID,
            )
            c.start()
            copies.append(c)
            tsem += 1
        for c in copies:
            c.wait()
        to_ref[...] = _small_sum(n, tbuf, toff)
        toff += n


def small_sum(t, names, cid):
    table_n = {"c": 2, "y": 4, "x": 4, "z": 8, "h": 2}
    slots = sum(table_n[k] for k in names)
    sems = sum(table_n[k] - 1 for k in names)
    return pl.pallas_call(
        functools.partial(_small_kernel, names),
        out_shape=jax.ShapeDtypeStruct(t.shape, t.dtype),
        in_specs=[pl.BlockSpec(memory_space=pltpu.VMEM)],
        out_specs=pl.BlockSpec(memory_space=pltpu.VMEM),
        scratch_shapes=[
            pltpu.VMEM((slots,) + t.shape, t.dtype),
            pltpu.SemaphoreType.DMA((sems,)),
            pltpu.SemaphoreType.DMA((sems,)),
        ],
        compiler_params=pltpu.CompilerParams(collective_id=cid, has_side_effects=True),
    )(t)


def _rs_stage(tasks, work, rbuf, send_sem, recv_sem, slot, sem, rider=None):
    n = tasks[0][0]
    for s in range(n - 1):
        copies = []
        for tn, me, nbr, ndir, base, size, own in tasks:
            chunk = size // tn
            piece = chunk // ndir
            for d in range(ndir):
                sign = 1 if d == 0 else -1
                send_at = pl.multiple_of(base + ((me - sign * (s + 1)) % tn) * chunk + d * piece, 8)
                recv_at = pl.multiple_of(base + ((me - sign * (s + 2)) % tn) * chunk + d * piece, 8)
                src = own if s == 0 else work
                c = pltpu.make_async_remote_copy(
                    src_ref=src.at[pl.ds(send_at, piece)],
                    dst_ref=rbuf.at[pl.ds(slot, piece)],
                    send_sem=send_sem.at[sem],
                    recv_sem=recv_sem.at[sem],
                    device_id=nbr(me + sign),
                    device_id_type=MESH_ID,
                )
                c.start()
                copies.append((c, slot, recv_at, piece, own))
                slot += piece
                sem += 1
        ride = rider(s) if rider is not None else None
        for c, sl, recv_at, piece, own in copies:
            c.wait_recv()
            at = pl.ds(recv_at, piece)
            work[at] = rbuf[pl.ds(sl, piece)] + own[at]
        for c, sl, recv_at, piece, own in copies:
            c.wait_send()
        if ride is not None:
            ride.wait()
    return slot, sem


def _ag_stage(tasks, o_ref, send_sem, recv_sem, sem):
    n = tasks[0][0]
    for s in range(n - 1):
        copies = []
        for tn, me, nbr, ndir, base, size, own in tasks:
            chunk = size // tn
            piece = chunk // ndir
            for d in range(ndir):
                sign = 1 if d == 0 else -1
                at = pl.ds(pl.multiple_of(base + ((me - sign * s) % tn) * chunk + d * piece, 8), piece)
                c = pltpu.make_async_remote_copy(
                    src_ref=o_ref.at[at],
                    dst_ref=o_ref.at[at],
                    send_sem=send_sem.at[sem],
                    recv_sem=recv_sem.at[sem],
                    device_id=nbr(me + sign),
                    device_id_type=MESH_ID,
                )
                c.start()
                copies.append(c)
                sem += 1
        for c in copies:
            c.wait()
    return sem


def _pass_copy(buf, at, nbr, target, sems, idx):
    c = pltpu.make_async_remote_copy(
        src_ref=buf.at[at],
        dst_ref=buf.at[at],
        send_sem=sems[0].at[idx],
        recv_sem=sems[1].at[idx],
        device_id=nbr(target),
        device_id_type=MESH_ID,
    )
    c.start()
    return c


def _kernel(rows, x_ref, t_ref, o_ref, to_ref, work, rbuf, zbuf, send_sem, recv_sem, tbuf, tsend, trecv):
    table = _levels()
    lc, ly, lx, lz = (table[k] for k in ("c", "y", "x", "z"))
    _barrier([lc, ly, lx, lz])
    tsems = (tsend, trecv)
    state = {"toff": 0, "tsem": 0}

    def tiny_level(level, first):
        n, me, nbr, ndir = level
        toff = state["toff"]
        tbuf[toff + me] = t_ref[...] if first else to_ref[...]

        def rider(s):
            c = _pass_copy(tbuf, toff + (me - s) % n, nbr, me + 1, tsems, state["tsem"])
            state["tsem"] += 1
            return c

        return rider

    def tiny_done(n):
        to_ref[...] = _small_sum(n, tbuf, state["toff"])
        state["toff"] += n

    slot, sem = 0, 0
    half = rows // 2
    quarter = rows // 4
    nc, core, nbc, _ = lc
    ny, yi, nby, _ = ly
    nx, xi, nbx, _ = lx
    nz, zi, nbz, _ = lz

    rider = tiny_level(lc, True)
    slot, sem = _rs_stage([(nc, core, nbc, 1, 0, rows, x_ref)], work, rbuf, send_sem, recv_sem, slot, sem, rider)
    tiny_done(nc)
    r0 = core * half
    a1, b1 = r0, r0 + quarter
    rider = tiny_level(ly, False)
    slot, sem = _rs_stage(
        [(ny, yi, nby, 2, a1, quarter, work), (nx, xi, nbx, 2, b1, quarter, work)],
        work, rbuf, send_sem, recv_sem, slot, sem, rider,
    )
    tiny_done(ny)
    c1 = quarter // 4
    a2, b2 = a1 + yi * c1, b1 + xi * c1
    rider = tiny_level(lx, False)
    slot, sem = _rs_stage(
        [(nx, xi, nbx, 1, a2, c1, work), (ny, yi, nby, 1, b2, c1, work)],
        work, rbuf, send_sem, recv_sem, slot, sem, rider,
    )
    tiny_done(nx)
    c2 = c1 // 4
    a3, b3 = a2 + xi * c2, b2 + yi * c2
    zbuf[zi, 0] = work[pl.ds(pl.multiple_of(a3, 8), c2)]
    zbuf[zi, 1] = work[pl.ds(pl.multiple_of(b3, 8), c2)]
    toff = state["toff"]
    tbuf[toff + zi] = to_ref[...]
    right = nz // 2
    left = nz - 1 - right
    for s in range(right):
        cs = [
            _pass_copy(zbuf, (zi - s) % nz, nbz, zi + 1, (send_sem, recv_sem), sem),
            _pass_copy(tbuf, toff + (zi - s) % nz, nbz, zi + 1, tsems, state["tsem"]),
        ]
        sem += 1
        state["tsem"] += 1
        if s < left:
            cs.append(_pass_copy(zbuf, (zi + s) % nz, nbz, zi - 1, (send_sem, recv_sem), sem))
            cs.append(_pass_copy(tbuf, toff + (zi + s) % nz, nbz, zi - 1, tsems, state["tsem"]))
            sem += 1
            state["tsem"] += 1
        for c in cs:
            c.wait()
    for colour, at in ((0, a3), (1, b3)):
        acc = zbuf[0, colour]
        for k in range(1, nz):
            acc = acc + zbuf[k, colour]
        o_ref[pl.ds(pl.multiple_of(at, 8), c2)] = acc
    tiny_done(nz)
    sem = _ag_stage([(nx, xi, nbx, 1, a2, c1, None), (ny, yi, nby, 1, b2, c1, None)], o_ref, send_sem, recv_sem, sem)
    sem = _ag_stage([(ny, yi, nby, 2, a1, quarter, None), (nx, xi, nbx, 2, b1, quarter, None)], o_ref, send_sem, recv_sem, sem)
    sem = _ag_stage([(nc, core, nbc, 1, 0, rows, None)], o_ref, send_sem, recv_sem, sem)


def _counts(rows):
    half, quarter = rows // 2, rows // 4
    c1 = quarter // 4
    slots = half + 3 * 2 * quarter // 4 + 3 * 2 * c1 // 4
    sems = 1 + 3 * 4 + 3 * 2 + 7 + 3 * 2 + 3 * 4 + 1
    return slots, sems, 2 + 4 + 4 + 8, 1 + 3 + 3 + 7


def all_sum(flat, small):
    rows = flat.shape[0]
    slots, sems, tslots, tsems = _counts(rows)
    c2 = rows // 64
    return pl.pallas_call(
        functools.partial(_kernel, rows),
        out_shape=(
            jax.ShapeDtypeStruct(flat.shape, flat.dtype),
            jax.ShapeDtypeStruct(small.shape, small.dtype),
        ),
        in_specs=[pl.BlockSpec(memory_space=pltpu.VMEM)] * 2,
        out_specs=(pl.BlockSpec(memory_space=pltpu.VMEM),) * 2,
        scratch_shapes=[
            pltpu.VMEM(flat.shape, flat.dtype),
            pltpu.VMEM((slots, flat.shape[1]), flat.dtype),
            pltpu.VMEM((8, 2, c2, flat.shape[1]), flat.dtype),
            pltpu.SemaphoreType.DMA((sems,)),
            pltpu.SemaphoreType.DMA((sems,)),
            pltpu.VMEM((tslots,) + small.shape, small.dtype),
            pltpu.SemaphoreType.DMA((tsems,)),
            pltpu.SemaphoreType.DMA((tsems,)),
        ],
        compiler_params=pltpu.CompilerParams(
            collective_id=0, has_side_effects=True, vmem_limit_bytes=48 * 1024 * 1024
        ),
    )(flat, small)


def _corr_fwd_kernel(ev_ref, win_ref, inv_ref, dots_ref, strip_ref):
    wide = win_ref.shape[0]
    lanes = dots_ref.shape[1]
    rows = lax.broadcasted_iota(jnp.int32, (wide, wide), 0)
    cols = lax.broadcasted_iota(jnp.int32, (wide, wide), 1)
    flip = (rows + cols == wide - 1).astype(jnp.bfloat16)
    win_rev = jnp.dot(flip, win_ref[...], preferred_element_type=jnp.float32).astype(jnp.bfloat16)
    m = lax.dot_general(
        ev_ref[...], win_rev, (((1,), (1,)), ((), ())), preferred_element_type=jnp.float32
    )
    dots_ref[...] = pltpu.roll(m, 0, 1, stride=1, stride_axis=0)[:, wide - lanes :]
    inv = jnp.broadcast_to(inv_ref[...], m.shape)
    strip_ref[...] = pltpu.roll(inv, 0, 1, stride=1, stride_axis=0)[:, wide - lanes :]


def corr_fwd(emb_v, win_pad, inv_pad):
    clips, frames, width = emb_v.shape
    wide = win_pad.shape[1]
    lanes = 128
    return pl.pallas_call(
        _corr_fwd_kernel,
        grid=(clips,),
        in_specs=[
            pl.BlockSpec((None, frames, width), lambda c: (c, 0, 0)),
            pl.BlockSpec((None, wide, width), lambda c: (c, 0, 0)),
            pl.BlockSpec((None, 1, wide), lambda c: (c, 0, 0)),
        ],
        out_specs=[
            pl.BlockSpec((None, frames, lanes), lambda c: (c, 0, 0)),
            pl.BlockSpec((None, frames, lanes), lambda c: (c, 0, 0)),
        ],
        out_shape=[
            jax.ShapeDtypeStruct((clips, frames, lanes), jnp.float32),
            jax.ShapeDtypeStruct((clips, frames, lanes), jnp.float32),
        ],
    )(emb_v, win_pad, inv_pad)


def _corr_bwd_kernel(gd_ref, at_ref, ev_ref, win_ref, lip_ref, wsum_ref, ginv_ref):
    frames, lanes = gd_ref.shape
    wide = win_ref.shape[0]
    pad = jnp.zeros((frames, wide - lanes), jnp.float32)
    g = jnp.concatenate([gd_ref[...].astype(jnp.float32), pad], axis=1)
    band = pltpu.roll(g, 0, 1, stride=1, stride_axis=0)
    lip_ref[...] = jnp.dot(band.astype(jnp.bfloat16), win_ref[...], preferred_element_type=jnp.float32)
    band_t = band.T.astype(jnp.bfloat16)
    wsum_ref[...] = jnp.dot(band_t, ev_ref[...], preferred_element_type=jnp.float32)
    a = jnp.concatenate([at_ref[...], pad], axis=1)
    spread = pltpu.roll(a, 0, 1, stride=1, stride_axis=0)
    ginv_ref[...] = jnp.sum(spread, axis=0, keepdims=True)


def corr_bwd(gd_pad, at_pad, emb_v, win_pad):
    clips, frames, width = emb_v.shape
    wide = win_pad.shape[1]
    lanes = gd_pad.shape[2]
    return pl.pallas_call(
        _corr_bwd_kernel,
        grid=(clips,),
        in_specs=[
            pl.BlockSpec((None, frames, lanes), lambda c: (c, 0, 0)),
            pl.BlockSpec((None, frames, lanes), lambda c: (c, 0, 0)),
            pl.BlockSpec((None, frames, width), lambda c: (c, 0, 0)),
            pl.BlockSpec((None, wide, width), lambda c: (c, 0, 0)),
        ],
        out_specs=[
            pl.BlockSpec((None, frames, width), lambda c: (c, 0, 0)),
            pl.BlockSpec((None, wide, width), lambda c: (c, 0, 0)),
            pl.BlockSpec((None, 1, wide), lambda c: (c, 0, 0)),
        ],
        out_shape=[
            jax.ShapeDtypeStruct((clips, frames, width), jnp.float32),
            jax.ShapeDtypeStruct((clips, wide, width), jnp.float32),
            jax.ShapeDtypeStruct((clips, 1, wide), jnp.float32),
        ],
    )(gd_pad, at_pad, emb_v, win_pad)


logit_sharpening_divisor = 10.0
loss_scale = 1024.0
epsilon = 1e-06


def padded_2(cells, sides, width):
    for axis, dim in sides:
        count = lax.axis_size(axis)
        ends = count - 1
        head = lax.slice_in_dim(cells, 0, width, axis=dim)
        tail = lax.slice_in_dim(cells, cells.shape[dim] - width, cells.shape[dim], axis=dim)
        cells = jnp.concatenate(
            [
                lax.ppermute(tail, axis, [(i, (i + 1) % count) for i in range(ends)]),
                cells,
                lax.ppermute(head, axis, [((i + 1) % count, i) for i in range(ends)]),
            ],
            axis=dim,
        )
    return cells


def from_behind(value, axis, steps):
    count = lax.axis_size(axis)
    initial, last = (max(0, -steps), min(count, count - steps))
    return lax.ppermute(value, axis, [(source, source + steps) for source in range(initial, last)])


def silu_slope(values):
    sigma = jax.nn.sigmoid(values)
    return sigma * (1.0 + values * (1.0 - sigma))


def encoder(padded, w_conv, w_proj):
    clip_num, frame_pad, chan_num = padded.shape
    frame_num = frame_pad - 2
    columns = jnp.concatenate(
        [padded[:, 0:frame_num], padded[:, 1 : frame_num + 1], padded[:, 2 : frame_num + 2]], axis=2
    )
    before = jnp.einsum(
        "cfk,ke->cfe",
        columns,
        w_conv.reshape(3 * chan_num, w_conv.shape[2]),
        preferred_element_type=jnp.float32,
    )
    hidden = jax.nn.silu(before).astype(jnp.bfloat16)
    embedded = jnp.einsum("cfe,eg->cfg", hidden, w_proj, preferred_element_type=jnp.float32).astype(
        jnp.bfloat16
    )
    return (columns, before, hidden, embedded)


def inverse_norm(embedded):
    values = embedded.astype(jnp.float32)
    return lax.rsqrt(jnp.sum(values * values, axis=-1) + epsilon)


def spread_band(band, wide_len):
    clip_num, row_num, band_len = band.shape
    full_band = jnp.pad(band, ((0, 0), (0, 0), (0, wide_len + 1 - band_len)))
    flat_band = full_band.reshape(clip_num, row_num * (wide_len + 1))[:, : row_num * wide_len]
    return flat_band.reshape(clip_num, row_num, wide_len)


def narrow_band(matrix, band_len):
    clip_num, row_num, wide_len = matrix.shape
    flat_mat = jnp.pad(matrix.reshape(clip_num, row_num * wide_len), ((0, 0), (0, row_num)))
    return flat_mat.reshape(clip_num, row_num, wide_len + 1)[:, :, :band_len]


def flatten_rows(values):
    return values.reshape(values.shape[0] * values.shape[1], values.shape[2])


def proj_grad(hidden, grad_emb):
    return jnp.einsum("re,rf->ef", hidden, grad_emb, preferred_element_type=jnp.float32)


def conv_grad(columns, before, grad_emb, w_proj, w_conv):
    grad_hidden = jnp.einsum("rf,ef->re", grad_emb, w_proj, preferred_element_type=jnp.float32)
    grad_before = (grad_hidden * silu_slope(before)).astype(jnp.bfloat16)
    grad_conv = jnp.einsum("rk,re->ke", columns, grad_before, preferred_element_type=jnp.float32)
    return grad_conv.reshape(w_conv.shape)


def shards(
    audio_feats, lip_feats, lengths, labels, w_audio_conv, w_audio_proj, w_lip_conv, w_lip_proj
):
    clip_num, frame_num, chan_num = audio_feats.shape
    width = w_audio_proj.shape[1]
    offsets = 2 * SPAN + 1
    wide_len = frame_num + 2 * SPAN
    first_frame = lax.axis_index("tm") * frame_num
    stacked = jnp.stack([audio_feats, lip_feats])
    padded = padded_2(stacked, (("tm", 2),), 1)
    cols_a, pre_a, hid_a, emb_a = encoder(padded[0], w_audio_conv, w_audio_proj)
    cols_v, pre_v, hid_v, emb_v = encoder(padded[1], w_lip_conv, w_lip_proj)
    window = padded_2(emb_a, (("tm", 1),), SPAN)
    cols_a, pre_a, hid_a = (flatten_rows(cols_a), flatten_rows(pre_a), flatten_rows(hid_a))
    cols_v, pre_v, hid_v = (flatten_rows(cols_v), flatten_rows(pre_v), flatten_rows(hid_v))
    count_part = jnp.sum(lengths - jnp.abs(labels))
    count_block = jnp.zeros((8, 128), jnp.int32).at[0, 0].set(count_part)
    count = small_sum(count_block, ("y", "x", "h"), 1)[0, 0].astype(jnp.float32)
    inv_win = inverse_norm(window)
    reciprocal_visual_length = inverse_norm(emb_v)
    wide_pad = -(-wide_len // 128) * 128
    win_pad = jnp.pad(window, ((0, 0), (0, wide_pad - wide_len), (0, 0)))
    inv_pad = jnp.pad(inv_win, ((0, 0), (0, wide_pad - wide_len)))[:, None, :]
    dots_rev, strip_rev = corr_fwd(emb_v, win_pad, inv_pad[:, :, ::-1])
    lagged_inner_terms = dots_rev[:, :, ::-1][:, :, :offsets]
    reciprocal_lag_strip = strip_rev[:, :, ::-1][:, :, :offsets]
    frame_ids = first_frame + jnp.arange(frame_num, dtype=jnp.int32)
    shifts = jnp.arange(offsets, dtype=jnp.int32) - SPAN
    positions = frame_ids[:, None] + shifts[None, :]
    inside = frame_ids[None, :] < lengths[:, None]
    valid = inside[:, :, None] & (positions[None] >= 0) & (positions[None] < lengths[:, None, None])
    target_pos = frame_ids[None, :] + labels[:, None]
    counted = inside & (target_pos >= 0) & (target_pos < lengths[:, None])
    correct_lag_position = (shifts[None, :] == labels[:, None]).astype(jnp.float32)
    lag_similarity_logits = (
        logit_sharpening_divisor
        * lagged_inner_terms
        * reciprocal_visual_length[:, :, None]
        * reciprocal_lag_strip
    )
    exponentiated_logits = jnp.where(valid, jnp.exp(lag_similarity_logits), 0.0)
    partition_sums = jnp.where(inside, jnp.sum(exponentiated_logits, axis=2), 1.0)
    picked = jnp.sum(lag_similarity_logits * correct_lag_position[:, None, :], axis=2)
    loss_local = jnp.sum(jnp.where(counted, jnp.log(partition_sums) - picked, 0.0))
    normalized_probabilities = jnp.where(counted, loss_scale / count, 0.0)
    logit_derivative = (
        logit_sharpening_divisor
        * normalized_probabilities[:, :, None]
        * (exponentiated_logits / partition_sums[:, :, None] - correct_lag_position[:, None, :])
    )
    grad_dots = (
        logit_derivative * reciprocal_visual_length[:, :, None] * reciprocal_lag_strip
    ).astype(jnp.bfloat16)
    grad_inv_v = jnp.sum(logit_derivative * lagged_inner_terms * reciprocal_lag_strip, axis=2)
    audio_term = logit_derivative * lagged_inner_terms * reciprocal_visual_length[:, :, None]
    band_pad = ((0, 0), (0, 0), (0, 128 - offsets))
    lip_sum, win_sum_pad, ginv_pad = corr_bwd(
        jnp.pad(grad_dots, band_pad), jnp.pad(audio_term, band_pad), emb_v, win_pad
    )
    grad_inv_win = ginv_pad[:, 0, :wide_len]
    lip_vals = emb_v.astype(jnp.float32)
    grad_lip = (
        lip_sum
        - (
            reciprocal_visual_length
            * reciprocal_visual_length
            * reciprocal_visual_length
            * grad_inv_v
        )[:, :, None]
        * lip_vals
    ).astype(jnp.bfloat16)
    win_sum = win_sum_pad[:, :wide_len]
    win_sum = win_sum - (inv_win * inv_win * inv_win * grad_inv_win)[:, :, None] * window.astype(
        jnp.float32
    )
    own_grad = win_sum[:, SPAN : SPAN + frame_num]
    from_after = from_behind(win_sum[:, :SPAN], "tm", -1)
    from_before = from_behind(win_sum[:, frame_num + SPAN :], "tm", 1)
    own_grad = own_grad.at[:, frame_num - SPAN :].add(from_after)
    own_grad = own_grad.at[:, :SPAN].add(from_before)
    grad_audio = own_grad.astype(jnp.bfloat16).reshape(clip_num * frame_num, width)
    grad_lip = grad_lip.reshape(clip_num * frame_num, width)
    grad_ap = proj_grad(hid_a, grad_audio)
    grad_vp = proj_grad(hid_v, grad_lip)
    grad_ac = conv_grad(cols_a, pre_a, grad_audio, w_audio_proj, w_audio_conv)
    grad_vc = conv_grad(cols_v, pre_v, grad_lip, w_lip_proj, w_lip_conv)
    parts = (grad_ac, grad_vc, grad_ap, grad_vp)
    lanes = grad_ap.shape[1]
    flat = jnp.concatenate([g.reshape(-1, lanes) for g in parts], axis=0)
    loss_block = jnp.zeros((8, 128), jnp.float32).at[0, 0].set(loss_local)
    total, loss_total = all_sum(flat, loss_block)
    outs = []
    start = 0
    for g in parts:
        rows = g.size // lanes
        outs.append(total[start : start + rows].reshape(g.shape))
        start += rows
    grad_ac, grad_vc, grad_ap, grad_vp = outs
    loss_sum = loss_total[0, 0]
    return (loss_sum / count, grad_ac, grad_ap, grad_vc, grad_vp)


def solution(mesh):
    placed = (
        P("clip", "tm", None),
        P("clip", "tm", None),
        P("clip"),
        P("clip"),
        P(),
        P(),
        P(),
        P(),
    )
    return jax.shard_map(
        shards, mesh=mesh, in_specs=placed, out_specs=(P(), P(), P(), P(), P()), check_vma=False
    )
```

```python
import jax
import jax.numpy as jnp
from jax import lax
from jax.sharding import PartitionSpec as P
import functools
from jax.experimental import pallas as pl
from jax.experimental.pallas import tpu as pltpu

SPAN = 15


MESH_ID = pl.DeviceIdType.MESH


def _coords():
    ci = lax.axis_index("clip")
    ti = lax.axis_index("tm")
    return ci, ti, ci % 4, (ci // 4) % 4, ci // 16, ti % 2, ti // 2


def _levels():
    ci, ti, y, x, zh, core, zl = _coords()
    z = zh * 4 + zl

    def at_y(v):
        return (zh * 16 + x * 4 + v % 4, ti)

    def at_x(v):
        return (zh * 16 + (v % 4) * 4 + y, ti)

    def at_z(v):
        w = v % 8
        return ((w // 4) * 16 + x * 4 + y, (w % 4) * 2 + core)

    def at_c(v):
        return (ci, zl * 2 + v % 2)

    def at_h(v):
        return ((v % 2) * 16 + x * 4 + y, ti)

    return {
        "c": (2, core, at_c, 1),
        "y": (4, y, at_y, 2),
        "x": (4, x, at_x, 2),
        "z": (8, z, at_z, 1),
        "h": (2, zh, at_h, 1),
    }


def _barrier(levels):
    barrier = pltpu.get_barrier_semaphore()
    peers = []
    for n, me, nbr, ndir in levels:
        peers.append(nbr(me + 1))
        if n > 2:
            peers.append(nbr(me - 1))
    for p in peers:
        pl.semaphore_signal(barrier, inc=1, device_id=p, device_id_type=MESH_ID)
    pl.semaphore_wait(barrier, len(peers))


def _small_start(n, me, nbr, s, tbuf, toff, tsend, trecv, tsem):
    at = toff + (me - s) % n
    c = pltpu.make_async_remote_copy(
        src_ref=tbuf.at[at],
        dst_ref=tbuf.at[at],
        send_sem=tsend.at[tsem],
        recv_sem=trecv.at[tsem],
        device_id=nbr(me + 1),
        device_id_type=MESH_ID,
    )
    c.start()
    return c


def _small_sum(n, tbuf, toff):
    acc = tbuf[toff]
    for k in range(1, n):
        acc = acc + tbuf[toff + k]
    return acc


def _small_kernel(names, t_ref, to_ref, tbuf, tsend, trecv):
    table = _levels()
    levels = [table[k] for k in names]
    barrier = pltpu.get_barrier_semaphore()
    peers = [nbr(me + j) for n, me, nbr, ndir in levels for j in range(1, n)]
    for p in peers:
        pl.semaphore_signal(barrier, inc=1, device_id=p, device_id_type=MESH_ID)
    pl.semaphore_wait(barrier, len(peers))
    toff = 0
    tsem = 0
    for li, (n, me, nbr, ndir) in enumerate(levels):
        tbuf[toff + me] = t_ref[...] if li == 0 else to_ref[...]
        copies = []
        for j in range(1, n):
            c = pltpu.make_async_remote_copy(
                src_ref=tbuf.at[toff + me],
                dst_ref=tbuf.at[toff + me],
                send_sem=tsend.at[tsem],
                recv_sem=trecv.at[tsem],
                device_id=nbr(me + j),
                device_id_type=MESH_ID,
            )
            c.start()
            copies.append(c)
            tsem += 1
        for c in copies:
            c.wait()
        to_ref[...] = _small_sum(n, tbuf, toff)
        toff += n


def small_sum(t, names, cid):
    table_n = {"c": 2, "y": 4, "x": 4, "z": 8, "h": 2}
    slots = sum(table_n[k] for k in names)
    sems = sum(table_n[k] - 1 for k in names)
    return pl.pallas_call(
        functools.partial(_small_kernel, names),
        out_shape=jax.ShapeDtypeStruct(t.shape, t.dtype),
        in_specs=[pl.BlockSpec(memory_space=pltpu.VMEM)],
        out_specs=pl.BlockSpec(memory_space=pltpu.VMEM),
        scratch_shapes=[
            pltpu.VMEM((slots,) + t.shape, t.dtype),
            pltpu.SemaphoreType.DMA((sems,)),
            pltpu.SemaphoreType.DMA((sems,)),
        ],
        compiler_params=pltpu.CompilerParams(collective_id=cid, has_side_effects=True),
    )(t)


def _rs_stage(tasks, work, rbuf, send_sem, recv_sem, slot, sem, rider=None):
    n = tasks[0][0]
    for s in range(n - 1):
        copies = []
        for tn, me, nbr, ndir, base, size, own in tasks:
            chunk = size // tn
            piece = chunk // ndir
            for d in range(ndir):
                sign = 1 if d == 0 else -1
                send_at = pl.multiple_of(base + ((me - sign * (s + 1)) % tn) * chunk + d * piece, 8)
                recv_at = pl.multiple_of(base + ((me - sign * (s + 2)) % tn) * chunk + d * piece, 8)
                src = own if s == 0 else work
                c = pltpu.make_async_remote_copy(
                    src_ref=src.at[pl.ds(send_at, piece)],
                    dst_ref=rbuf.at[pl.ds(slot, piece)],
                    send_sem=send_sem.at[sem],
                    recv_sem=recv_sem.at[sem],
                    device_id=nbr(me + sign),
                    device_id_type=MESH_ID,
                )
                c.start()
                copies.append((c, slot, recv_at, piece, own))
                slot += piece
                sem += 1
        ride = rider(s) if rider is not None else None
        for c, sl, recv_at, piece, own in copies:
            c.wait_recv()
            at = pl.ds(recv_at, piece)
            work[at] = rbuf[pl.ds(sl, piece)] + own[at]
        for c, sl, recv_at, piece, own in copies:
            c.wait_send()
        if ride is not None:
            ride.wait()
    return slot, sem


def _ag_stage(tasks, o_ref, send_sem, recv_sem, sem):
    n = tasks[0][0]
    for s in range(n - 1):
        copies = []
        for tn, me, nbr, ndir, base, size, own in tasks:
            chunk = size // tn
            piece = chunk // ndir
            for d in range(ndir):
                sign = 1 if d == 0 else -1
                at = pl.ds(pl.multiple_of(base + ((me - sign * s) % tn) * chunk + d * piece, 8), piece)
                c = pltpu.make_async_remote_copy(
                    src_ref=o_ref.at[at],
                    dst_ref=o_ref.at[at],
                    send_sem=send_sem.at[sem],
                    recv_sem=recv_sem.at[sem],
                    device_id=nbr(me + sign),
                    device_id_type=MESH_ID,
                )
                c.start()
                copies.append(c)
                sem += 1
        for c in copies:
            c.wait()
    return sem


def _pass_copy(buf, at, nbr, target, sems, idx):
    c = pltpu.make_async_remote_copy(
        src_ref=buf.at[at],
        dst_ref=buf.at[at],
        send_sem=sems[0].at[idx],
        recv_sem=sems[1].at[idx],
        device_id=nbr(target),
        device_id_type=MESH_ID,
    )
    c.start()
    return c


def _kernel(rows, x_ref, t_ref, o_ref, to_ref, work, rbuf, zbuf, send_sem, recv_sem, tbuf, tsend, trecv, half_ref, hsend, hrecv):
    table = _levels()
    lc, ly, lx, lz = (table[k] for k in ("c", "y", "x", "z"))
    _barrier([lc, ly, lx, lz])
    tsems = (tsend, trecv)
    state = {"toff": 0, "tsem": 0}

    def tiny_level(level, first):
        n, me, nbr, ndir = level
        toff = state["toff"]
        tbuf[toff + me] = t_ref[...] if first else to_ref[...]

        def rider(s):
            c = _pass_copy(tbuf, toff + (me - s) % n, nbr, me + 1, tsems, state["tsem"])
            state["tsem"] += 1
            return c

        return rider

    def tiny_done(n):
        to_ref[...] = _small_sum(n, tbuf, state["toff"])
        state["toff"] += n

    slot, sem = 0, 0
    half = rows // 2
    quarter = rows // 4
    nc, core, nbc, _ = lc
    ny, yi, nby, _ = ly
    nx, xi, nbx, _ = lx
    nz, zi, nbz, _ = lz

    rider = tiny_level(lc, True)
    slot, sem = _rs_stage([(nc, core, nbc, 1, 0, rows, x_ref)], work, rbuf, send_sem, recv_sem, slot, sem, rider)
    tiny_done(nc)
    r0 = core * half
    a1, b1 = r0, r0 + quarter
    rider = tiny_level(ly, False)
    slot, sem = _rs_stage(
        [(ny, yi, nby, 2, a1, quarter, work), (nx, xi, nbx, 2, b1, quarter, work)],
        work, rbuf, send_sem, recv_sem, slot, sem, rider,
    )
    tiny_done(ny)
    c1 = quarter // 4
    a2, b2 = a1 + yi * c1, b1 + xi * c1
    rider = tiny_level(lx, False)
    slot, sem = _rs_stage(
        [(nx, xi, nbx, 1, a2, c1, work), (ny, yi, nby, 1, b2, c1, work)],
        work, rbuf, send_sem, recv_sem, slot, sem, rider,
    )
    tiny_done(nx)
    c2 = c1 // 4
    a3, b3 = a2 + xi * c2, b2 + yi * c2
    zbuf[zi, 0] = work[pl.ds(pl.multiple_of(a3, 8), c2)]
    zbuf[zi, 1] = work[pl.ds(pl.multiple_of(b3, 8), c2)]
    toff = state["toff"]
    tbuf[toff + zi] = to_ref[...]
    right = nz // 2
    left = nz - 1 - right
    for s in range(right):
        cs = [
            _pass_copy(zbuf, (zi - s) % nz, nbz, zi + 1, (send_sem, recv_sem), sem),
            _pass_copy(tbuf, toff + (zi - s) % nz, nbz, zi + 1, tsems, state["tsem"]),
        ]
        sem += 1
        state["tsem"] += 1
        if s < left:
            cs.append(_pass_copy(zbuf, (zi + s) % nz, nbz, zi - 1, (send_sem, recv_sem), sem))
            cs.append(_pass_copy(tbuf, toff + (zi + s) % nz, nbz, zi - 1, tsems, state["tsem"]))
            sem += 1
            state["tsem"] += 1
        for c in cs:
            c.wait()
    for colour, at in ((0, a3), (1, b3)):
        acc = zbuf[0, colour]
        for k in range(1, nz):
            acc = acc + zbuf[k, colour]
        o_ref[pl.ds(pl.multiple_of(at, 8), c2)] = acc
    tiny_done(nz)
    sem = _ag_stage([(nx, xi, nbx, 1, a2, c1, None), (ny, yi, nby, 1, b2, c1, None)], o_ref, send_sem, recv_sem, sem)
    for at in (a2, b2):
        region = pl.ds(pl.multiple_of(at, 16), c1)
        half_ref[region] = o_ref[region].astype(half_ref.dtype)
    sem = _ag_stage([(ny, yi, nby, 2, a1, quarter, None), (nx, xi, nbx, 2, b1, quarter, None)], half_ref, hsend, hrecv, 0)
    _ag_stage([(nc, core, nbc, 1, 0, rows, None)], half_ref, hsend, hrecv, sem)
    o_ref[...] = half_ref[...].astype(o_ref.dtype)


def _counts(rows):
    half, quarter = rows // 2, rows // 4
    c1 = quarter // 4
    slots = half + 3 * 2 * quarter // 4 + 3 * 2 * c1 // 4
    sems = 1 + 3 * 4 + 3 * 2 + 7 + 3 * 2
    return slots, sems, 2 + 4 + 4 + 8, 1 + 3 + 3 + 7


def all_sum(flat, small):
    rows = flat.shape[0]
    slots, sems, tslots, tsems = _counts(rows)
    c2 = rows // 64
    return pl.pallas_call(
        functools.partial(_kernel, rows),
        out_shape=(
            jax.ShapeDtypeStruct(flat.shape, flat.dtype),
            jax.ShapeDtypeStruct(small.shape, small.dtype),
        ),
        in_specs=[pl.BlockSpec(memory_space=pltpu.VMEM)] * 2,
        out_specs=(pl.BlockSpec(memory_space=pltpu.VMEM),) * 2,
        scratch_shapes=[
            pltpu.VMEM(flat.shape, flat.dtype),
            pltpu.VMEM((slots, flat.shape[1]), flat.dtype),
            pltpu.VMEM((8, 2, c2, flat.shape[1]), flat.dtype),
            pltpu.SemaphoreType.DMA((sems,)),
            pltpu.SemaphoreType.DMA((sems,)),
            pltpu.VMEM((tslots,) + small.shape, small.dtype),
            pltpu.SemaphoreType.DMA((tsems,)),
            pltpu.SemaphoreType.DMA((tsems,)),
            pltpu.VMEM(flat.shape, jnp.bfloat16),
            pltpu.SemaphoreType.DMA((13,)),
            pltpu.SemaphoreType.DMA((13,)),
        ],
        compiler_params=pltpu.CompilerParams(
            collective_id=0, has_side_effects=True, vmem_limit_bytes=48 * 1024 * 1024
        ),
    )(flat, small)


def _corr_fwd_kernel(ev_ref, win_ref, inv_ref, dots_ref, strip_ref):
    wide = win_ref.shape[0]
    lanes = dots_ref.shape[1]
    rows = lax.broadcasted_iota(jnp.int32, (wide, wide), 0)
    cols = lax.broadcasted_iota(jnp.int32, (wide, wide), 1)
    flip = (rows + cols == wide - 1).astype(jnp.bfloat16)
    win_rev = jnp.dot(flip, win_ref[...], preferred_element_type=jnp.float32).astype(jnp.bfloat16)
    m = lax.dot_general(
        ev_ref[...], win_rev, (((1,), (1,)), ((), ())), preferred_element_type=jnp.float32
    )
    dots_ref[...] = pltpu.roll(m, 0, 1, stride=1, stride_axis=0)[:, wide - lanes :]
    inv = jnp.broadcast_to(inv_ref[...], m.shape)
    strip_ref[...] = pltpu.roll(inv, 0, 1, stride=1, stride_axis=0)[:, wide - lanes :]


def corr_fwd(emb_v, win_pad, inv_pad):
    clips, frames, width = emb_v.shape
    wide = win_pad.shape[1]
    lanes = 128
    return pl.pallas_call(
        _corr_fwd_kernel,
        grid=(clips,),
        in_specs=[
            pl.BlockSpec((None, frames, width), lambda c: (c, 0, 0)),
            pl.BlockSpec((None, wide, width), lambda c: (c, 0, 0)),
            pl.BlockSpec((None, 1, wide), lambda c: (c, 0, 0)),
        ],
        out_specs=[
            pl.BlockSpec((None, frames, lanes), lambda c: (c, 0, 0)),
            pl.BlockSpec((None, frames, lanes), lambda c: (c, 0, 0)),
        ],
        out_shape=[
            jax.ShapeDtypeStruct((clips, frames, lanes), jnp.float32),
            jax.ShapeDtypeStruct((clips, frames, lanes), jnp.float32),
        ],
    )(emb_v, win_pad, inv_pad)


def _corr_bwd_kernel(gd_ref, at_ref, ev_ref, win_ref, lip_ref, wsum_ref, ginv_ref):
    frames, lanes = gd_ref.shape
    wide = win_ref.shape[0]
    pad = jnp.zeros((frames, wide - lanes), jnp.float32)
    g = jnp.concatenate([gd_ref[...].astype(jnp.float32), pad], axis=1)
    band = pltpu.roll(g, 0, 1, stride=1, stride_axis=0)
    lip_ref[...] = jnp.dot(band.astype(jnp.bfloat16), win_ref[...], preferred_element_type=jnp.float32)
    band_t = band.T.astype(jnp.bfloat16)
    wsum_ref[...] = jnp.dot(band_t, ev_ref[...], preferred_element_type=jnp.float32)
    a = jnp.concatenate([at_ref[...], pad], axis=1)
    spread = pltpu.roll(a, 0, 1, stride=1, stride_axis=0)
    ginv_ref[...] = jnp.sum(spread, axis=0, keepdims=True)


def corr_bwd(gd_pad, at_pad, emb_v, win_pad):
    clips, frames, width = emb_v.shape
    wide = win_pad.shape[1]
    lanes = gd_pad.shape[2]
    return pl.pallas_call(
        _corr_bwd_kernel,
        grid=(clips,),
        in_specs=[
            pl.BlockSpec((None, frames, lanes), lambda c: (c, 0, 0)),
            pl.BlockSpec((None, frames, lanes), lambda c: (c, 0, 0)),
            pl.BlockSpec((None, frames, width), lambda c: (c, 0, 0)),
            pl.BlockSpec((None, wide, width), lambda c: (c, 0, 0)),
        ],
        out_specs=[
            pl.BlockSpec((None, frames, width), lambda c: (c, 0, 0)),
            pl.BlockSpec((None, wide, width), lambda c: (c, 0, 0)),
            pl.BlockSpec((None, 1, wide), lambda c: (c, 0, 0)),
        ],
        out_shape=[
            jax.ShapeDtypeStruct((clips, frames, width), jnp.float32),
            jax.ShapeDtypeStruct((clips, wide, width), jnp.float32),
            jax.ShapeDtypeStruct((clips, 1, wide), jnp.float32),
        ],
    )(gd_pad, at_pad, emb_v, win_pad)


logit_sharpening_divisor = 10.0
loss_scale = 1024.0
epsilon = 1e-06


def padded_2(cells, sides, width):
    for axis, dim in sides:
        count = lax.axis_size(axis)
        ends = count - 1
        head = lax.slice_in_dim(cells, 0, width, axis=dim)
        tail = lax.slice_in_dim(cells, cells.shape[dim] - width, cells.shape[dim], axis=dim)
        cells = jnp.concatenate(
            [
                lax.ppermute(tail, axis, [(i, (i + 1) % count) for i in range(ends)]),
                cells,
                lax.ppermute(head, axis, [((i + 1) % count, i) for i in range(ends)]),
            ],
            axis=dim,
        )
    return cells


def from_behind(value, axis, steps):
    count = lax.axis_size(axis)
    initial, last = (max(0, -steps), min(count, count - steps))
    return lax.ppermute(value, axis, [(source, source + steps) for source in range(initial, last)])


def silu_slope(values):
    sigma = jax.nn.sigmoid(values)
    return sigma * (1.0 + values * (1.0 - sigma))


def encoder(padded, w_conv, w_proj):
    clip_num, frame_pad, chan_num = padded.shape
    frame_num = frame_pad - 2
    columns = jnp.concatenate(
        [padded[:, 0:frame_num], padded[:, 1 : frame_num + 1], padded[:, 2 : frame_num + 2]], axis=2
    )
    before = jnp.einsum(
        "cfk,ke->cfe",
        columns,
        w_conv.reshape(3 * chan_num, w_conv.shape[2]),
        preferred_element_type=jnp.float32,
    )
    hidden = jax.nn.silu(before).astype(jnp.bfloat16)
    embedded = jnp.einsum("cfe,eg->cfg", hidden, w_proj, preferred_element_type=jnp.float32).astype(
        jnp.bfloat16
    )
    return (columns, before, hidden, embedded)


def inverse_norm(embedded):
    values = embedded.astype(jnp.float32)
    return lax.rsqrt(jnp.sum(values * values, axis=-1) + epsilon)


def spread_band(band, wide_len):
    clip_num, row_num, band_len = band.shape
    full_band = jnp.pad(band, ((0, 0), (0, 0), (0, wide_len + 1 - band_len)))
    flat_band = full_band.reshape(clip_num, row_num * (wide_len + 1))[:, : row_num * wide_len]
    return flat_band.reshape(clip_num, row_num, wide_len)


def narrow_band(matrix, band_len):
    clip_num, row_num, wide_len = matrix.shape
    flat_mat = jnp.pad(matrix.reshape(clip_num, row_num * wide_len), ((0, 0), (0, row_num)))
    return flat_mat.reshape(clip_num, row_num, wide_len + 1)[:, :, :band_len]


def flatten_rows(values):
    return values.reshape(values.shape[0] * values.shape[1], values.shape[2])


def proj_grad(hidden, grad_emb):
    return jnp.einsum("re,rf->ef", hidden, grad_emb, preferred_element_type=jnp.float32)


def conv_grad(columns, before, grad_emb, w_proj, w_conv):
    grad_hidden = jnp.einsum("rf,ef->re", grad_emb, w_proj, preferred_element_type=jnp.float32)
    grad_before = (grad_hidden * silu_slope(before)).astype(jnp.bfloat16)
    grad_conv = jnp.einsum("rk,re->ke", columns, grad_before, preferred_element_type=jnp.float32)
    return grad_conv.reshape(w_conv.shape)


def shards(
    audio_feats, lip_feats, lengths, labels, w_audio_conv, w_audio_proj, w_lip_conv, w_lip_proj
):
    clip_num, frame_num, chan_num = audio_feats.shape
    width = w_audio_proj.shape[1]
    offsets = 2 * SPAN + 1
    wide_len = frame_num + 2 * SPAN
    first_frame = lax.axis_index("tm") * frame_num
    stacked = jnp.stack([audio_feats, lip_feats])
    padded = padded_2(stacked, (("tm", 2),), 1)
    cols_a, pre_a, hid_a, emb_a = encoder(padded[0], w_audio_conv, w_audio_proj)
    cols_v, pre_v, hid_v, emb_v = encoder(padded[1], w_lip_conv, w_lip_proj)
    window = padded_2(emb_a, (("tm", 1),), SPAN)
    cols_a, pre_a, hid_a = (flatten_rows(cols_a), flatten_rows(pre_a), flatten_rows(hid_a))
    cols_v, pre_v, hid_v = (flatten_rows(cols_v), flatten_rows(pre_v), flatten_rows(hid_v))
    count_part = jnp.sum(lengths - jnp.abs(labels))
    count_block = jnp.zeros((8, 128), jnp.int32).at[0, 0].set(count_part)
    count = small_sum(count_block, ("y", "x", "h"), 1)[0, 0].astype(jnp.float32)
    inv_win = inverse_norm(window)
    reciprocal_visual_length = inverse_norm(emb_v)
    wide_pad = -(-wide_len // 128) * 128
    win_pad = jnp.pad(window, ((0, 0), (0, wide_pad - wide_len), (0, 0)))
    inv_pad = jnp.pad(inv_win, ((0, 0), (0, wide_pad - wide_len)))[:, None, :]
    dots_rev, strip_rev = corr_fwd(emb_v, win_pad, inv_pad[:, :, ::-1])
    lagged_inner_terms = dots_rev[:, :, ::-1][:, :, :offsets]
    reciprocal_lag_strip = strip_rev[:, :, ::-1][:, :, :offsets]
    frame_ids = first_frame + jnp.arange(frame_num, dtype=jnp.int32)
    shifts = jnp.arange(offsets, dtype=jnp.int32) - SPAN
    positions = frame_ids[:, None] + shifts[None, :]
    inside = frame_ids[None, :] < lengths[:, None]
    valid = inside[:, :, None] & (positions[None] >= 0) & (positions[None] < lengths[:, None, None])
    target_pos = frame_ids[None, :] + labels[:, None]
    counted = inside & (target_pos >= 0) & (target_pos < lengths[:, None])
    correct_lag_position = (shifts[None, :] == labels[:, None]).astype(jnp.float32)
    lag_similarity_logits = (
        logit_sharpening_divisor
        * lagged_inner_terms
        * reciprocal_visual_length[:, :, None]
        * reciprocal_lag_strip
    )
    exponentiated_logits = jnp.where(valid, jnp.exp(lag_similarity_logits), 0.0)
    partition_sums = jnp.where(inside, jnp.sum(exponentiated_logits, axis=2), 1.0)
    picked = jnp.sum(lag_similarity_logits * correct_lag_position[:, None, :], axis=2)
    loss_local = jnp.sum(jnp.where(counted, jnp.log(partition_sums) - picked, 0.0))
    normalized_probabilities = jnp.where(counted, loss_scale / count, 0.0)
    logit_derivative = (
        logit_sharpening_divisor
        * normalized_probabilities[:, :, None]
        * (exponentiated_logits / partition_sums[:, :, None] - correct_lag_position[:, None, :])
    )
    grad_dots = (
        logit_derivative * reciprocal_visual_length[:, :, None] * reciprocal_lag_strip
    ).astype(jnp.bfloat16)
    grad_inv_v = jnp.sum(logit_derivative * lagged_inner_terms * reciprocal_lag_strip, axis=2)
    audio_term = logit_derivative * lagged_inner_terms * reciprocal_visual_length[:, :, None]
    band_pad = ((0, 0), (0, 0), (0, 128 - offsets))
    lip_sum, win_sum_pad, ginv_pad = corr_bwd(
        jnp.pad(grad_dots, band_pad), jnp.pad(audio_term, band_pad), emb_v, win_pad
    )
    grad_inv_win = ginv_pad[:, 0, :wide_len]
    lip_vals = emb_v.astype(jnp.float32)
    grad_lip = (
        lip_sum
        - (
            reciprocal_visual_length
            * reciprocal_visual_length
            * reciprocal_visual_length
            * grad_inv_v
        )[:, :, None]
        * lip_vals
    ).astype(jnp.bfloat16)
    win_sum = win_sum_pad[:, :wide_len]
    win_sum = win_sum - (inv_win * inv_win * inv_win * grad_inv_win)[:, :, None] * window.astype(
        jnp.float32
    )
    own_grad = win_sum[:, SPAN : SPAN + frame_num]
    from_after = from_behind(win_sum[:, :SPAN], "tm", -1)
    from_before = from_behind(win_sum[:, frame_num + SPAN :], "tm", 1)
    own_grad = own_grad.at[:, frame_num - SPAN :].add(from_after)
    own_grad = own_grad.at[:, :SPAN].add(from_before)
    grad_audio = own_grad.astype(jnp.bfloat16).reshape(clip_num * frame_num, width)
    grad_lip = grad_lip.reshape(clip_num * frame_num, width)
    grad_ap = proj_grad(hid_a, grad_audio)
    grad_vp = proj_grad(hid_v, grad_lip)
    grad_ac = conv_grad(cols_a, pre_a, grad_audio, w_audio_proj, w_audio_conv)
    grad_vc = conv_grad(cols_v, pre_v, grad_lip, w_lip_proj, w_lip_conv)
    parts = (grad_ac, grad_vc, grad_ap, grad_vp)
    lanes = grad_ap.shape[1]
    flat = jnp.concatenate([g.reshape(-1, lanes) for g in parts], axis=0)
    loss_block = jnp.zeros((8, 128), jnp.float32).at[0, 0].set(loss_local)
    total, loss_total = all_sum(flat, loss_block)
    outs = []
    start = 0
    for g in parts:
        rows = g.size // lanes
        outs.append(total[start : start + rows].reshape(g.shape))
        start += rows
    grad_ac, grad_vc, grad_ap, grad_vp = outs
    loss_sum = loss_total[0, 0]
    return (loss_sum / count, grad_ac, grad_ap, grad_vc, grad_vp)


def solution(mesh):
    placed = (
        P("clip", "tm", None),
        P("clip", "tm", None),
        P("clip"),
        P("clip"),
        P(),
        P(),
        P(),
        P(),
    )
    return jax.shard_map(
        shards, mesh=mesh, in_specs=placed, out_specs=(P(), P(), P(), P(), P()), check_vma=False
    )
```

```python
import jax
import jax.numpy as jnp
from jax import lax
from jax.sharding import PartitionSpec as P
import functools
from jax.experimental import pallas as pl
from jax.experimental.pallas import tpu as pltpu

SPAN = 15


MESH_ID = pl.DeviceIdType.MESH


def _coords():
    ci = lax.axis_index("clip")
    ti = lax.axis_index("tm")
    return ci, ti, ci % 4, (ci // 4) % 4, ci // 16, ti % 2, ti // 2


def _levels():
    ci, ti, y, x, zh, core, zl = _coords()
    z = zh * 4 + zl

    def at_y(v):
        return (zh * 16 + x * 4 + v % 4, ti)

    def at_x(v):
        return (zh * 16 + (v % 4) * 4 + y, ti)

    def at_z(v):
        w = v % 8
        return ((w // 4) * 16 + x * 4 + y, (w % 4) * 2 + core)

    def at_c(v):
        return (ci, zl * 2 + v % 2)

    def at_h(v):
        return ((v % 2) * 16 + x * 4 + y, ti)

    return {
        "c": (2, core, at_c, 1),
        "y": (4, y, at_y, 2),
        "x": (4, x, at_x, 2),
        "z": (8, z, at_z, 1),
        "h": (2, zh, at_h, 1),
    }


def _barrier(levels):
    barrier = pltpu.get_barrier_semaphore()
    peers = []
    for n, me, nbr, ndir in levels:
        peers.append(nbr(me + 1))
        if n > 2:
            peers.append(nbr(me - 1))
    for p in peers:
        pl.semaphore_signal(barrier, inc=1, device_id=p, device_id_type=MESH_ID)
    pl.semaphore_wait(barrier, len(peers))


def _small_start(n, me, nbr, s, tbuf, toff, tsend, trecv, tsem):
    at = toff + (me - s) % n
    c = pltpu.make_async_remote_copy(
        src_ref=tbuf.at[at],
        dst_ref=tbuf.at[at],
        send_sem=tsend.at[tsem],
        recv_sem=trecv.at[tsem],
        device_id=nbr(me + 1),
        device_id_type=MESH_ID,
    )
    c.start()
    return c


def _small_sum(n, tbuf, toff):
    acc = tbuf[toff]
    for k in range(1, n):
        acc = acc + tbuf[toff + k]
    return acc


def _small_kernel(names, t_ref, to_ref, tbuf, tsend, trecv):
    table = _levels()
    levels = [table[k] for k in names]
    barrier = pltpu.get_barrier_semaphore()
    peers = [nbr(me + j) for n, me, nbr, ndir in levels for j in range(1, n)]
    for p in peers:
        pl.semaphore_signal(barrier, inc=1, device_id=p, device_id_type=MESH_ID)
    pl.semaphore_wait(barrier, len(peers))
    toff = 0
    tsem = 0
    for li, (n, me, nbr, ndir) in enumerate(levels):
        tbuf[toff + me] = t_ref[...] if li == 0 else to_ref[...]
        copies = []
        for j in range(1, n):
            c = pltpu.make_async_remote_copy(
                src_ref=tbuf.at[toff + me],
                dst_ref=tbuf.at[toff + me],
                send_sem=tsend.at[tsem],
                recv_sem=trecv.at[tsem],
                device_id=nbr(me + j),
                device_id_type=MESH_ID,
            )
            c.start()
            copies.append(c)
            tsem += 1
        for c in copies:
            c.wait()
        to_ref[...] = _small_sum(n, tbuf, toff)
        toff += n


def small_sum(t, names, cid):
    table_n = {"c": 2, "y": 4, "x": 4, "z": 8, "h": 2}
    slots = sum(table_n[k] for k in names)
    sems = sum(table_n[k] - 1 for k in names)
    return pl.pallas_call(
        functools.partial(_small_kernel, names),
        out_shape=jax.ShapeDtypeStruct(t.shape, t.dtype),
        in_specs=[pl.BlockSpec(memory_space=pltpu.VMEM)],
        out_specs=pl.BlockSpec(memory_space=pltpu.VMEM),
        scratch_shapes=[
            pltpu.VMEM((slots,) + t.shape, t.dtype),
            pltpu.SemaphoreType.DMA((sems,)),
            pltpu.SemaphoreType.DMA((sems,)),
        ],
        compiler_params=pltpu.CompilerParams(collective_id=cid, has_side_effects=True),
    )(t)


def _rs_stage(tasks, work, rbuf, send_sem, recv_sem, slot, sem, rider=None):
    n = tasks[0][0]
    for s in range(n - 1):
        copies = []
        for tn, me, nbr, ndir, base, size, own in tasks:
            chunk = size // tn
            piece = chunk // ndir
            for d in range(ndir):
                sign = 1 if d == 0 else -1
                send_at = pl.multiple_of(base + ((me - sign * (s + 1)) % tn) * chunk + d * piece, 8)
                recv_at = pl.multiple_of(base + ((me - sign * (s + 2)) % tn) * chunk + d * piece, 8)
                src = own if s == 0 else work
                c = pltpu.make_async_remote_copy(
                    src_ref=src.at[pl.ds(send_at, piece)],
                    dst_ref=rbuf.at[pl.ds(slot, piece)],
                    send_sem=send_sem.at[sem],
                    recv_sem=recv_sem.at[sem],
                    device_id=nbr(me + sign),
                    device_id_type=MESH_ID,
                )
                c.start()
                copies.append((c, slot, recv_at, piece, own))
                slot += piece
                sem += 1
        ride = rider(s) if rider is not None else None
        for c, sl, recv_at, piece, own in copies:
            c.wait_recv()
            at = pl.ds(recv_at, piece)
            work[at] = rbuf[pl.ds(sl, piece)] + own[at]
        for c, sl, recv_at, piece, own in copies:
            c.wait_send()
        if ride is not None:
            ride.wait()
    return slot, sem


def _ag_stage(tasks, o_ref, send_sem, recv_sem, sem):
    n = tasks[0][0]
    for s in range(n - 1):
        copies = []
        for tn, me, nbr, ndir, base, size, own in tasks:
            chunk = size // tn
            piece = chunk // ndir
            for d in range(ndir):
                sign = 1 if d == 0 else -1
                at = pl.ds(pl.multiple_of(base + ((me - sign * s) % tn) * chunk + d * piece, 8), piece)
                c = pltpu.make_async_remote_copy(
                    src_ref=o_ref.at[at],
                    dst_ref=o_ref.at[at],
                    send_sem=send_sem.at[sem],
                    recv_sem=recv_sem.at[sem],
                    device_id=nbr(me + sign),
                    device_id_type=MESH_ID,
                )
                c.start()
                copies.append(c)
                sem += 1
        for c in copies:
            c.wait()
    return sem


def _pass_copy(buf, at, nbr, target, sems, idx):
    c = pltpu.make_async_remote_copy(
        src_ref=buf.at[at],
        dst_ref=buf.at[at],
        send_sem=sems[0].at[idx],
        recv_sem=sems[1].at[idx],
        device_id=nbr(target),
        device_id_type=MESH_ID,
    )
    c.start()
    return c


def _kernel(sizes, *refs):
    parts = len(sizes)
    ins, t_ref = refs[:parts], refs[parts]
    outs, to_ref = refs[parts + 1 : 2 * parts + 1], refs[2 * parts + 1]
    work, rbuf, zbuf, send_sem, recv_sem, tbuf, tsend, trecv, half_ref, hsend, hrecv, o_ref = refs[2 * parts + 2 :]
    rows = sum(sizes)
    start = 0
    for size, in_ref in zip(sizes, ins):
        work[start : start + size] = in_ref[...]
        start += size
    table = _levels()
    lc, ly, lx, lz = (table[k] for k in ("c", "y", "x", "z"))
    _barrier([lc, ly, lx, lz])
    tsems = (tsend, trecv)
    state = {"toff": 0, "tsem": 0}

    def tiny_level(level, first):
        n, me, nbr, ndir = level
        toff = state["toff"]
        tbuf[toff + me] = t_ref[...] if first else to_ref[...]

        def rider(s):
            c = _pass_copy(tbuf, toff + (me - s) % n, nbr, me + 1, tsems, state["tsem"])
            state["tsem"] += 1
            return c

        return rider

    def tiny_done(n):
        to_ref[...] = _small_sum(n, tbuf, state["toff"])
        state["toff"] += n

    slot, sem = 0, 0
    half = rows // 2
    quarter = rows // 4
    nc, core, nbc, _ = lc
    ny, yi, nby, _ = ly
    nx, xi, nbx, _ = lx
    nz, zi, nbz, _ = lz

    rider = tiny_level(lc, True)
    slot, sem = _rs_stage([(nc, core, nbc, 1, 0, rows, work)], work, rbuf, send_sem, recv_sem, slot, sem, rider)
    tiny_done(nc)
    r0 = core * half
    a1, b1 = r0, r0 + quarter
    rider = tiny_level(ly, False)
    slot, sem = _rs_stage(
        [(ny, yi, nby, 2, a1, quarter, work), (nx, xi, nbx, 2, b1, quarter, work)],
        work, rbuf, send_sem, recv_sem, slot, sem, rider,
    )
    tiny_done(ny)
    c1 = quarter // 4
    a2, b2 = a1 + yi * c1, b1 + xi * c1
    rider = tiny_level(lx, False)
    slot, sem = _rs_stage(
        [(nx, xi, nbx, 1, a2, c1, work), (ny, yi, nby, 1, b2, c1, work)],
        work, rbuf, send_sem, recv_sem, slot, sem, rider,
    )
    tiny_done(nx)
    c2 = c1 // 4
    a3, b3 = a2 + xi * c2, b2 + yi * c2
    zbuf[zi, 0] = work[pl.ds(pl.multiple_of(a3, 8), c2)]
    zbuf[zi, 1] = work[pl.ds(pl.multiple_of(b3, 8), c2)]
    toff = state["toff"]
    tbuf[toff + zi] = to_ref[...]
    right = nz // 2
    left = nz - 1 - right
    for s in range(right):
        cs = [
            _pass_copy(zbuf, (zi - s) % nz, nbz, zi + 1, (send_sem, recv_sem), sem),
            _pass_copy(tbuf, toff + (zi - s) % nz, nbz, zi + 1, tsems, state["tsem"]),
        ]
        sem += 1
        state["tsem"] += 1
        if s < left:
            cs.append(_pass_copy(zbuf, (zi + s) % nz, nbz, zi - 1, (send_sem, recv_sem), sem))
            cs.append(_pass_copy(tbuf, toff + (zi + s) % nz, nbz, zi - 1, tsems, state["tsem"]))
            sem += 1
            state["tsem"] += 1
        for c in cs:
            c.wait()
    for colour, at in ((0, a3), (1, b3)):
        acc = zbuf[0, colour]
        for k in range(1, nz):
            acc = acc + zbuf[k, colour]
        o_ref[pl.ds(pl.multiple_of(at, 8), c2)] = acc
    tiny_done(nz)
    sem = _ag_stage([(nx, xi, nbx, 1, a2, c1, None), (ny, yi, nby, 1, b2, c1, None)], o_ref, send_sem, recv_sem, sem)
    for at in (a2, b2):
        region = pl.ds(pl.multiple_of(at, 16), c1)
        half_ref[region] = o_ref[region].astype(half_ref.dtype)
    sem = _ag_stage([(ny, yi, nby, 2, a1, quarter, None), (nx, xi, nbx, 2, b1, quarter, None)], half_ref, hsend, hrecv, 0)
    _ag_stage([(nc, core, nbc, 1, 0, rows, None)], half_ref, hsend, hrecv, sem)
    start = 0
    for size, out_ref in zip(sizes, outs):
        out_ref[...] = half_ref[start : start + size].astype(out_ref.dtype)
        start += size


def _counts(rows):
    half, quarter = rows // 2, rows // 4
    c1 = quarter // 4
    slots = half + 3 * 2 * quarter // 4 + 3 * 2 * c1 // 4
    sems = 1 + 3 * 4 + 3 * 2 + 7 + 3 * 2
    return slots, sems, 2 + 4 + 4 + 8, 1 + 3 + 3 + 7


def all_sum(parts, small):
    sizes = tuple(p.shape[0] for p in parts)
    lanes = parts[0].shape[1]
    rows = sum(sizes)
    slots, sems, tslots, tsems = _counts(rows)
    c2 = rows // 64
    vmem = pl.BlockSpec(memory_space=pltpu.VMEM)
    return pl.pallas_call(
        functools.partial(_kernel, sizes),
        out_shape=tuple(jax.ShapeDtypeStruct(p.shape, p.dtype) for p in parts)
        + (jax.ShapeDtypeStruct(small.shape, small.dtype),),
        in_specs=[vmem] * (len(parts) + 1),
        out_specs=(vmem,) * (len(parts) + 1),
        scratch_shapes=[
            pltpu.VMEM((rows, lanes), jnp.float32),
            pltpu.VMEM((slots, lanes), jnp.float32),
            pltpu.VMEM((8, 2, c2, lanes), jnp.float32),
            pltpu.SemaphoreType.DMA((sems,)),
            pltpu.SemaphoreType.DMA((sems,)),
            pltpu.VMEM((tslots,) + small.shape, small.dtype),
            pltpu.SemaphoreType.DMA((tsems,)),
            pltpu.SemaphoreType.DMA((tsems,)),
            pltpu.VMEM((rows, lanes), jnp.bfloat16),
            pltpu.SemaphoreType.DMA((13,)),
            pltpu.SemaphoreType.DMA((13,)),
            pltpu.VMEM((rows, lanes), jnp.float32),
        ],
        compiler_params=pltpu.CompilerParams(
            collective_id=0, has_side_effects=True, vmem_limit_bytes=48 * 1024 * 1024
        ),
    )(*parts, small)


def _corr_fwd_kernel(ev_ref, win_ref, inv_ref, dots_ref, strip_ref):
    wide = win_ref.shape[0]
    lanes = dots_ref.shape[1]
    rows = lax.broadcasted_iota(jnp.int32, (wide, wide), 0)
    cols = lax.broadcasted_iota(jnp.int32, (wide, wide), 1)
    flip = (rows + cols == wide - 1).astype(jnp.bfloat16)
    win_rev = jnp.dot(flip, win_ref[...], preferred_element_type=jnp.float32).astype(jnp.bfloat16)
    m = lax.dot_general(
        ev_ref[...], win_rev, (((1,), (1,)), ((), ())), preferred_element_type=jnp.float32
    )
    dots_ref[...] = pltpu.roll(m, 0, 1, stride=1, stride_axis=0)[:, wide - lanes :]
    inv = jnp.broadcast_to(inv_ref[...], m.shape)
    strip_ref[...] = pltpu.roll(inv, 0, 1, stride=1, stride_axis=0)[:, wide - lanes :]


def corr_fwd(emb_v, win_pad, inv_pad):
    clips, frames, width = emb_v.shape
    wide = win_pad.shape[1]
    lanes = 128
    return pl.pallas_call(
        _corr_fwd_kernel,
        grid=(clips,),
        in_specs=[
            pl.BlockSpec((None, frames, width), lambda c: (c, 0, 0)),
            pl.BlockSpec((None, wide, width), lambda c: (c, 0, 0)),
            pl.BlockSpec((None, 1, wide), lambda c: (c, 0, 0)),
        ],
        out_specs=[
            pl.BlockSpec((None, frames, lanes), lambda c: (c, 0, 0)),
            pl.BlockSpec((None, frames, lanes), lambda c: (c, 0, 0)),
        ],
        out_shape=[
            jax.ShapeDtypeStruct((clips, frames, lanes), jnp.float32),
            jax.ShapeDtypeStruct((clips, frames, lanes), jnp.float32),
        ],
    )(emb_v, win_pad, inv_pad)


def _corr_bwd_kernel(gd_ref, at_ref, ev_ref, win_ref, lip_ref, wsum_ref, ginv_ref):
    frames, lanes = gd_ref.shape
    wide = win_ref.shape[0]
    pad = jnp.zeros((frames, wide - lanes), jnp.float32)
    g = jnp.concatenate([gd_ref[...].astype(jnp.float32), pad], axis=1)
    band = pltpu.roll(g, 0, 1, stride=1, stride_axis=0)
    lip_ref[...] = jnp.dot(band.astype(jnp.bfloat16), win_ref[...], preferred_element_type=jnp.float32)
    band_t = band.T.astype(jnp.bfloat16)
    wsum_ref[...] = jnp.dot(band_t, ev_ref[...], preferred_element_type=jnp.float32)
    a = jnp.concatenate([at_ref[...], pad], axis=1)
    spread = pltpu.roll(a, 0, 1, stride=1, stride_axis=0)
    ginv_ref[...] = jnp.sum(spread, axis=0, keepdims=True)


def corr_bwd(gd_pad, at_pad, emb_v, win_pad):
    clips, frames, width = emb_v.shape
    wide = win_pad.shape[1]
    lanes = gd_pad.shape[2]
    return pl.pallas_call(
        _corr_bwd_kernel,
        grid=(clips,),
        in_specs=[
            pl.BlockSpec((None, frames, lanes), lambda c: (c, 0, 0)),
            pl.BlockSpec((None, frames, lanes), lambda c: (c, 0, 0)),
            pl.BlockSpec((None, frames, width), lambda c: (c, 0, 0)),
            pl.BlockSpec((None, wide, width), lambda c: (c, 0, 0)),
        ],
        out_specs=[
            pl.BlockSpec((None, frames, width), lambda c: (c, 0, 0)),
            pl.BlockSpec((None, wide, width), lambda c: (c, 0, 0)),
            pl.BlockSpec((None, 1, wide), lambda c: (c, 0, 0)),
        ],
        out_shape=[
            jax.ShapeDtypeStruct((clips, frames, width), jnp.float32),
            jax.ShapeDtypeStruct((clips, wide, width), jnp.float32),
            jax.ShapeDtypeStruct((clips, 1, wide), jnp.float32),
        ],
    )(gd_pad, at_pad, emb_v, win_pad)


logit_sharpening_divisor = 10.0
loss_scale = 1024.0
epsilon = 1e-06


def padded_2(cells, sides, width):
    for axis, dim in sides:
        count = lax.axis_size(axis)
        ends = count - 1
        head = lax.slice_in_dim(cells, 0, width, axis=dim)
        tail = lax.slice_in_dim(cells, cells.shape[dim] - width, cells.shape[dim], axis=dim)
        cells = jnp.concatenate(
            [
                lax.ppermute(tail, axis, [(i, (i + 1) % count) for i in range(ends)]),
                cells,
                lax.ppermute(head, axis, [((i + 1) % count, i) for i in range(ends)]),
            ],
            axis=dim,
        )
    return cells


def from_behind(value, axis, steps):
    count = lax.axis_size(axis)
    initial, last = (max(0, -steps), min(count, count - steps))
    return lax.ppermute(value, axis, [(source, source + steps) for source in range(initial, last)])


def silu_slope(values):
    sigma = jax.nn.sigmoid(values)
    return sigma * (1.0 + values * (1.0 - sigma))


def encoder(padded, w_conv, w_proj):
    clip_num, frame_pad, chan_num = padded.shape
    frame_num = frame_pad - 2
    columns = jnp.concatenate(
        [padded[:, 0:frame_num], padded[:, 1 : frame_num + 1], padded[:, 2 : frame_num + 2]], axis=2
    )
    before = jnp.einsum(
        "cfk,ke->cfe",
        columns,
        w_conv.reshape(3 * chan_num, w_conv.shape[2]),
        preferred_element_type=jnp.float32,
    )
    hidden = jax.nn.silu(before).astype(jnp.bfloat16)
    embedded = jnp.einsum("cfe,eg->cfg", hidden, w_proj, preferred_element_type=jnp.float32).astype(
        jnp.bfloat16
    )
    return (columns, before, hidden, embedded)


def inverse_norm(embedded):
    values = embedded.astype(jnp.float32)
    return lax.rsqrt(jnp.sum(values * values, axis=-1) + epsilon)


def spread_band(band, wide_len):
    clip_num, row_num, band_len = band.shape
    full_band = jnp.pad(band, ((0, 0), (0, 0), (0, wide_len + 1 - band_len)))
    flat_band = full_band.reshape(clip_num, row_num * (wide_len + 1))[:, : row_num * wide_len]
    return flat_band.reshape(clip_num, row_num, wide_len)


def narrow_band(matrix, band_len):
    clip_num, row_num, wide_len = matrix.shape
    flat_mat = jnp.pad(matrix.reshape(clip_num, row_num * wide_len), ((0, 0), (0, row_num)))
    return flat_mat.reshape(clip_num, row_num, wide_len + 1)[:, :, :band_len]


def flatten_rows(values):
    return values.reshape(values.shape[0] * values.shape[1], values.shape[2])


def proj_grad(hidden, grad_emb):
    return jnp.einsum("re,rf->ef", hidden, grad_emb, preferred_element_type=jnp.float32)


def conv_grad(columns, before, grad_emb, w_proj, w_conv):
    grad_hidden = jnp.einsum("rf,ef->re", grad_emb, w_proj, preferred_element_type=jnp.float32)
    grad_before = (grad_hidden * silu_slope(before)).astype(jnp.bfloat16)
    grad_conv = jnp.einsum("rk,re->ke", columns, grad_before, preferred_element_type=jnp.float32)
    return grad_conv.reshape(w_conv.shape)


def shards(
    audio_feats, lip_feats, lengths, labels, w_audio_conv, w_audio_proj, w_lip_conv, w_lip_proj
):
    clip_num, frame_num, chan_num = audio_feats.shape
    width = w_audio_proj.shape[1]
    offsets = 2 * SPAN + 1
    wide_len = frame_num + 2 * SPAN
    first_frame = lax.axis_index("tm") * frame_num
    stacked = jnp.stack([audio_feats, lip_feats])
    padded = padded_2(stacked, (("tm", 2),), 1)
    cols_a, pre_a, hid_a, emb_a = encoder(padded[0], w_audio_conv, w_audio_proj)
    cols_v, pre_v, hid_v, emb_v = encoder(padded[1], w_lip_conv, w_lip_proj)
    window = padded_2(emb_a, (("tm", 1),), SPAN)
    cols_a, pre_a, hid_a = (flatten_rows(cols_a), flatten_rows(pre_a), flatten_rows(hid_a))
    cols_v, pre_v, hid_v = (flatten_rows(cols_v), flatten_rows(pre_v), flatten_rows(hid_v))
    count_part = jnp.sum(lengths - jnp.abs(labels))
    count_block = jnp.zeros((8, 128), jnp.int32).at[0, 0].set(count_part)
    count = small_sum(count_block, ("y", "x", "h"), 1)[0, 0].astype(jnp.float32)
    inv_win = inverse_norm(window)
    reciprocal_visual_length = inverse_norm(emb_v)
    wide_pad = -(-wide_len // 128) * 128
    win_pad = jnp.pad(window, ((0, 0), (0, wide_pad - wide_len), (0, 0)))
    inv_pad = jnp.pad(inv_win, ((0, 0), (0, wide_pad - wide_len)))[:, None, :]
    dots_rev, strip_rev = corr_fwd(emb_v, win_pad, inv_pad[:, :, ::-1])
    lagged_inner_terms = dots_rev[:, :, ::-1][:, :, :offsets]
    reciprocal_lag_strip = strip_rev[:, :, ::-1][:, :, :offsets]
    frame_ids = first_frame + jnp.arange(frame_num, dtype=jnp.int32)
    shifts = jnp.arange(offsets, dtype=jnp.int32) - SPAN
    positions = frame_ids[:, None] + shifts[None, :]
    inside = frame_ids[None, :] < lengths[:, None]
    valid = inside[:, :, None] & (positions[None] >= 0) & (positions[None] < lengths[:, None, None])
    target_pos = frame_ids[None, :] + labels[:, None]
    counted = inside & (target_pos >= 0) & (target_pos < lengths[:, None])
    correct_lag_position = (shifts[None, :] == labels[:, None]).astype(jnp.float32)
    lag_similarity_logits = (
        logit_sharpening_divisor
        * lagged_inner_terms
        * reciprocal_visual_length[:, :, None]
        * reciprocal_lag_strip
    )
    exponentiated_logits = jnp.where(valid, jnp.exp(lag_similarity_logits), 0.0)
    partition_sums = jnp.where(inside, jnp.sum(exponentiated_logits, axis=2), 1.0)
    picked = jnp.sum(lag_similarity_logits * correct_lag_position[:, None, :], axis=2)
    loss_local = jnp.sum(jnp.where(counted, jnp.log(partition_sums) - picked, 0.0))
    normalized_probabilities = jnp.where(counted, loss_scale / count, 0.0)
    logit_derivative = (
        logit_sharpening_divisor
        * normalized_probabilities[:, :, None]
        * (exponentiated_logits / partition_sums[:, :, None] - correct_lag_position[:, None, :])
    )
    grad_dots = (
        logit_derivative * reciprocal_visual_length[:, :, None] * reciprocal_lag_strip
    ).astype(jnp.bfloat16)
    grad_inv_v = jnp.sum(logit_derivative * lagged_inner_terms * reciprocal_lag_strip, axis=2)
    audio_term = logit_derivative * lagged_inner_terms * reciprocal_visual_length[:, :, None]
    band_pad = ((0, 0), (0, 0), (0, 128 - offsets))
    lip_sum, win_sum_pad, ginv_pad = corr_bwd(
        jnp.pad(grad_dots, band_pad), jnp.pad(audio_term, band_pad), emb_v, win_pad
    )
    grad_inv_win = ginv_pad[:, 0, :wide_len]
    lip_vals = emb_v.astype(jnp.float32)
    grad_lip = (
        lip_sum
        - (
            reciprocal_visual_length
            * reciprocal_visual_length
            * reciprocal_visual_length
            * grad_inv_v
        )[:, :, None]
        * lip_vals
    ).astype(jnp.bfloat16)
    win_sum = win_sum_pad[:, :wide_len]
    win_sum = win_sum - (inv_win * inv_win * inv_win * grad_inv_win)[:, :, None] * window.astype(
        jnp.float32
    )
    own_grad = win_sum[:, SPAN : SPAN + frame_num]
    from_after = from_behind(win_sum[:, :SPAN], "tm", -1)
    from_before = from_behind(win_sum[:, frame_num + SPAN :], "tm", 1)
    own_grad = own_grad.at[:, frame_num - SPAN :].add(from_after)
    own_grad = own_grad.at[:, :SPAN].add(from_before)
    grad_audio = own_grad.astype(jnp.bfloat16).reshape(clip_num * frame_num, width)
    grad_lip = grad_lip.reshape(clip_num * frame_num, width)
    grad_ap = proj_grad(hid_a, grad_audio)
    grad_vp = proj_grad(hid_v, grad_lip)
    grad_ac = conv_grad(cols_a, pre_a, grad_audio, w_audio_proj, w_audio_conv)
    grad_vc = conv_grad(cols_v, pre_v, grad_lip, w_lip_proj, w_lip_conv)
    parts = (grad_ac, grad_vc, grad_ap, grad_vp)
    lanes = grad_ap.shape[1]
    loss_block = jnp.zeros((8, 128), jnp.float32).at[0, 0].set(loss_local)
    *sums, loss_total = all_sum([g.reshape(-1, lanes) for g in parts], loss_block)
    grad_ac, grad_vc, grad_ap, grad_vp = (t.reshape(g.shape) for t, g in zip(sums, parts))
    loss_sum = loss_total[0, 0]
    return (loss_sum / count, grad_ac, grad_ap, grad_vc, grad_vp)


def solution(mesh):
    placed = (
        P("clip", "tm", None),
        P("clip", "tm", None),
        P("clip"),
        P("clip"),
        P(),
        P(),
        P(),
        P(),
    )
    return jax.shard_map(
        shards, mesh=mesh, in_specs=placed, out_specs=(P(), P(), P(), P(), P()), check_vma=False
    )
```

```python
import jax
import jax.numpy as jnp
from jax import lax
from jax.sharding import PartitionSpec as P
import functools
from jax.experimental import pallas as pl
from jax.experimental.pallas import tpu as pltpu

SPAN = 15


MESH_ID = pl.DeviceIdType.MESH


def _coords():
    ci = lax.axis_index("clip")
    ti = lax.axis_index("tm")
    return ci, ti, ci % 4, (ci // 4) % 4, ci // 16, ti % 2, ti // 2


def _levels():
    ci, ti, y, x, zh, core, zl = _coords()
    z = zh * 4 + zl

    def at_y(v):
        return (zh * 16 + x * 4 + v % 4, ti)

    def at_x(v):
        return (zh * 16 + (v % 4) * 4 + y, ti)

    def at_z(v):
        w = v % 8
        return ((w // 4) * 16 + x * 4 + y, (w % 4) * 2 + core)

    def at_c(v):
        return (ci, zl * 2 + v % 2)

    def at_h(v):
        return ((v % 2) * 16 + x * 4 + y, ti)

    def at_k(v):
        return (v % 32, ti)

    return {
        "c": (2, core, at_c, 1),
        "y": (4, y, at_y, 2),
        "x": (4, x, at_x, 2),
        "z": (8, z, at_z, 1),
        "h": (2, zh, at_h, 1),
        "k": (32, ci, at_k, 1),
    }


def _barrier(levels):
    barrier = pltpu.get_barrier_semaphore()
    peers = []
    for n, me, nbr, ndir in levels:
        peers.append(nbr(me + 1))
        if n > 2:
            peers.append(nbr(me - 1))
    for p in peers:
        pl.semaphore_signal(barrier, inc=1, device_id=p, device_id_type=MESH_ID)
    pl.semaphore_wait(barrier, len(peers))


def _small_start(n, me, nbr, s, tbuf, toff, tsend, trecv, tsem):
    at = toff + (me - s) % n
    c = pltpu.make_async_remote_copy(
        src_ref=tbuf.at[at],
        dst_ref=tbuf.at[at],
        send_sem=tsend.at[tsem],
        recv_sem=trecv.at[tsem],
        device_id=nbr(me + 1),
        device_id_type=MESH_ID,
    )
    c.start()
    return c


def _small_sum(n, tbuf, toff):
    acc = tbuf[toff]
    for k in range(1, n):
        acc = acc + tbuf[toff + k]
    return acc


def _small_kernel(names, t_ref, to_ref, tbuf, tsend, trecv):
    table = _levels()
    levels = [table[k] for k in names]
    barrier = pltpu.get_barrier_semaphore()
    peers = [nbr(me + j) for n, me, nbr, ndir in levels for j in range(1, n)]
    for p in peers:
        pl.semaphore_signal(barrier, inc=1, device_id=p, device_id_type=MESH_ID)
    pl.semaphore_wait(barrier, len(peers))
    toff = 0
    tsem = 0
    for li, (n, me, nbr, ndir) in enumerate(levels):
        tbuf[toff + me] = t_ref[...] if li == 0 else to_ref[...]
        copies = []
        for j in range(1, n):
            c = pltpu.make_async_remote_copy(
                src_ref=tbuf.at[toff + me],
                dst_ref=tbuf.at[toff + me],
                send_sem=tsend.at[tsem],
                recv_sem=trecv.at[tsem],
                device_id=nbr(me + j),
                device_id_type=MESH_ID,
            )
            c.start()
            copies.append(c)
            tsem += 1
        for c in copies:
            c.wait()
        to_ref[...] = _small_sum(n, tbuf, toff)
        toff += n


def small_sum(t, names, cid):
    table_n = {"c": 2, "y": 4, "x": 4, "z": 8, "h": 2, "k": 32}
    slots = sum(table_n[k] for k in names)
    sems = sum(table_n[k] - 1 for k in names)
    return pl.pallas_call(
        functools.partial(_small_kernel, names),
        out_shape=jax.ShapeDtypeStruct(t.shape, t.dtype),
        in_specs=[pl.BlockSpec(memory_space=pltpu.VMEM)],
        out_specs=pl.BlockSpec(memory_space=pltpu.VMEM),
        scratch_shapes=[
            pltpu.VMEM((slots,) + t.shape, t.dtype),
            pltpu.SemaphoreType.DMA((sems,)),
            pltpu.SemaphoreType.DMA((sems,)),
        ],
        compiler_params=pltpu.CompilerParams(collective_id=cid, has_side_effects=True),
    )(t)


def _rs_stage(tasks, work, rbuf, send_sem, recv_sem, slot, sem, rider=None):
    n = tasks[0][0]
    for s in range(n - 1):
        copies = []
        for tn, me, nbr, ndir, base, size, own in tasks:
            chunk = size // tn
            piece = chunk // ndir
            for d in range(ndir):
                sign = 1 if d == 0 else -1
                send_at = pl.multiple_of(base + ((me - sign * (s + 1)) % tn) * chunk + d * piece, 8)
                recv_at = pl.multiple_of(base + ((me - sign * (s + 2)) % tn) * chunk + d * piece, 8)
                src = own if s == 0 else work
                c = pltpu.make_async_remote_copy(
                    src_ref=src.at[pl.ds(send_at, piece)],
                    dst_ref=rbuf.at[pl.ds(slot, piece)],
                    send_sem=send_sem.at[sem],
                    recv_sem=recv_sem.at[sem],
                    device_id=nbr(me + sign),
                    device_id_type=MESH_ID,
                )
                c.start()
                copies.append((c, slot, recv_at, piece, own))
                slot += piece
                sem += 1
        ride = rider(s) if rider is not None else None
        for c, sl, recv_at, piece, own in copies:
            c.wait_recv()
            at = pl.ds(recv_at, piece)
            work[at] = rbuf[pl.ds(sl, piece)] + own[at]
        for c, sl, recv_at, piece, own in copies:
            c.wait_send()
        if ride is not None:
            ride.wait()
    return slot, sem


def _ag_stage(tasks, o_ref, send_sem, recv_sem, sem):
    n = tasks[0][0]
    for s in range(n - 1):
        copies = []
        for tn, me, nbr, ndir, base, size, own in tasks:
            chunk = size // tn
            piece = chunk // ndir
            for d in range(ndir):
                sign = 1 if d == 0 else -1
                at = pl.ds(pl.multiple_of(base + ((me - sign * s) % tn) * chunk + d * piece, 8), piece)
                c = pltpu.make_async_remote_copy(
                    src_ref=o_ref.at[at],
                    dst_ref=o_ref.at[at],
                    send_sem=send_sem.at[sem],
                    recv_sem=recv_sem.at[sem],
                    device_id=nbr(me + sign),
                    device_id_type=MESH_ID,
                )
                c.start()
                copies.append(c)
                sem += 1
        for c in copies:
            c.wait()
    return sem


def _pass_copy(buf, at, nbr, target, sems, idx):
    c = pltpu.make_async_remote_copy(
        src_ref=buf.at[at],
        dst_ref=buf.at[at],
        send_sem=sems[0].at[idx],
        recv_sem=sems[1].at[idx],
        device_id=nbr(target),
        device_id_type=MESH_ID,
    )
    c.start()
    return c


def _kernel(sizes, *refs):
    parts = len(sizes)
    ins, t_ref = refs[:parts], refs[parts]
    outs, to_ref = refs[parts + 1 : 2 * parts + 1], refs[2 * parts + 1]
    work, rbuf, zbuf, send_sem, recv_sem, tbuf, tsend, trecv, half_ref, hsend, hrecv, o_ref = refs[2 * parts + 2 :]
    rows = sum(sizes)
    start = 0
    for size, in_ref in zip(sizes, ins):
        work[start : start + size] = in_ref[...]
        start += size
    table = _levels()
    lc, ly, lx, lz = (table[k] for k in ("c", "y", "x", "z"))
    _barrier([lc, ly, lx, lz])
    tsems = (tsend, trecv)
    state = {"toff": 0, "tsem": 0}

    def tiny_level(level, first):
        n, me, nbr, ndir = level
        toff = state["toff"]
        tbuf[toff + me] = t_ref[...] if first else to_ref[...]

        def rider(s):
            c = _pass_copy(tbuf, toff + (me - s) % n, nbr, me + 1, tsems, state["tsem"])
            state["tsem"] += 1
            return c

        return rider

    def tiny_done(n):
        to_ref[...] = _small_sum(n, tbuf, state["toff"])
        state["toff"] += n

    slot, sem = 0, 0
    half = rows // 2
    quarter = rows // 4
    nc, core, nbc, _ = lc
    ny, yi, nby, _ = ly
    nx, xi, nbx, _ = lx
    nz, zi, nbz, _ = lz

    rider = tiny_level(lc, True)
    slot, sem = _rs_stage([(nc, core, nbc, 1, 0, rows, work)], work, rbuf, send_sem, recv_sem, slot, sem, rider)
    tiny_done(nc)
    r0 = core * half
    a1, b1 = r0, r0 + quarter
    rider = tiny_level(ly, False)
    slot, sem = _rs_stage(
        [(ny, yi, nby, 2, a1, quarter, work), (nx, xi, nbx, 2, b1, quarter, work)],
        work, rbuf, send_sem, recv_sem, slot, sem, rider,
    )
    tiny_done(ny)
    c1 = quarter // 4
    a2, b2 = a1 + yi * c1, b1 + xi * c1
    rider = tiny_level(lx, False)
    slot, sem = _rs_stage(
        [(nx, xi, nbx, 1, a2, c1, work), (ny, yi, nby, 1, b2, c1, work)],
        work, rbuf, send_sem, recv_sem, slot, sem, rider,
    )
    tiny_done(nx)
    c2 = c1 // 4
    a3, b3 = a2 + xi * c2, b2 + yi * c2
    zbuf[zi, 0] = work[pl.ds(pl.multiple_of(a3, 8), c2)]
    zbuf[zi, 1] = work[pl.ds(pl.multiple_of(b3, 8), c2)]
    toff = state["toff"]
    tbuf[toff + zi] = to_ref[...]
    right = nz // 2
    left = nz - 1 - right
    for s in range(right):
        cs = [
            _pass_copy(zbuf, (zi - s) % nz, nbz, zi + 1, (send_sem, recv_sem), sem),
            _pass_copy(tbuf, toff + (zi - s) % nz, nbz, zi + 1, tsems, state["tsem"]),
        ]
        sem += 1
        state["tsem"] += 1
        if s < left:
            cs.append(_pass_copy(zbuf, (zi + s) % nz, nbz, zi - 1, (send_sem, recv_sem), sem))
            cs.append(_pass_copy(tbuf, toff + (zi + s) % nz, nbz, zi - 1, tsems, state["tsem"]))
            sem += 1
            state["tsem"] += 1
        for c in cs:
            c.wait()
    for colour, at in ((0, a3), (1, b3)):
        acc = zbuf[0, colour]
        for k in range(1, nz):
            acc = acc + zbuf[k, colour]
        o_ref[pl.ds(pl.multiple_of(at, 8), c2)] = acc
    tiny_done(nz)
    sem = _ag_stage([(nx, xi, nbx, 1, a2, c1, None), (ny, yi, nby, 1, b2, c1, None)], o_ref, send_sem, recv_sem, sem)
    for at in (a2, b2):
        region = pl.ds(pl.multiple_of(at, 16), c1)
        half_ref[region] = o_ref[region].astype(half_ref.dtype)
    sem = _ag_stage([(ny, yi, nby, 2, a1, quarter, None), (nx, xi, nbx, 2, b1, quarter, None)], half_ref, hsend, hrecv, 0)
    _ag_stage([(nc, core, nbc, 1, 0, rows, None)], half_ref, hsend, hrecv, sem)
    start = 0
    for size, out_ref in zip(sizes, outs):
        out_ref[...] = half_ref[start : start + size].astype(out_ref.dtype)
        start += size


def _counts(rows):
    half, quarter = rows // 2, rows // 4
    c1 = quarter // 4
    slots = half + 3 * 2 * quarter // 4 + 3 * 2 * c1 // 4
    sems = 1 + 3 * 4 + 3 * 2 + 7 + 3 * 2
    return slots, sems, 2 + 4 + 4 + 8, 1 + 3 + 3 + 7


def all_sum(parts, small):
    sizes = tuple(p.shape[0] for p in parts)
    lanes = parts[0].shape[1]
    rows = sum(sizes)
    slots, sems, tslots, tsems = _counts(rows)
    c2 = rows // 64
    vmem = pl.BlockSpec(memory_space=pltpu.VMEM)
    return pl.pallas_call(
        functools.partial(_kernel, sizes),
        out_shape=tuple(jax.ShapeDtypeStruct(p.shape, p.dtype) for p in parts)
        + (jax.ShapeDtypeStruct(small.shape, small.dtype),),
        in_specs=[vmem] * (len(parts) + 1),
        out_specs=(vmem,) * (len(parts) + 1),
        scratch_shapes=[
            pltpu.VMEM((rows, lanes), jnp.float32),
            pltpu.VMEM((slots, lanes), jnp.float32),
            pltpu.VMEM((8, 2, c2, lanes), jnp.float32),
            pltpu.SemaphoreType.DMA((sems,)),
            pltpu.SemaphoreType.DMA((sems,)),
            pltpu.VMEM((tslots,) + small.shape, small.dtype),
            pltpu.SemaphoreType.DMA((tsems,)),
            pltpu.SemaphoreType.DMA((tsems,)),
            pltpu.VMEM((rows, lanes), jnp.bfloat16),
            pltpu.SemaphoreType.DMA((13,)),
            pltpu.SemaphoreType.DMA((13,)),
            pltpu.VMEM((rows, lanes), jnp.float32),
        ],
        compiler_params=pltpu.CompilerParams(
            collective_id=0, has_side_effects=True, vmem_limit_bytes=48 * 1024 * 1024
        ),
    )(*parts, small)


def _corr_fwd_kernel(ev_ref, win_ref, inv_ref, dots_ref, strip_ref):
    wide = win_ref.shape[0]
    lanes = dots_ref.shape[1]
    rows = lax.broadcasted_iota(jnp.int32, (wide, wide), 0)
    cols = lax.broadcasted_iota(jnp.int32, (wide, wide), 1)
    flip = (rows + cols == wide - 1).astype(jnp.bfloat16)
    win_rev = jnp.dot(flip, win_ref[...], preferred_element_type=jnp.float32).astype(jnp.bfloat16)
    m = lax.dot_general(
        ev_ref[...], win_rev, (((1,), (1,)), ((), ())), preferred_element_type=jnp.float32
    )
    dots_ref[...] = pltpu.roll(m, 0, 1, stride=1, stride_axis=0)[:, wide - lanes :]
    inv = jnp.broadcast_to(inv_ref[...], m.shape)
    strip_ref[...] = pltpu.roll(inv, 0, 1, stride=1, stride_axis=0)[:, wide - lanes :]


def corr_fwd(emb_v, win_pad, inv_pad):
    clips, frames, width = emb_v.shape
    wide = win_pad.shape[1]
    lanes = 128
    return pl.pallas_call(
        _corr_fwd_kernel,
        grid=(clips,),
        in_specs=[
            pl.BlockSpec((None, frames, width), lambda c: (c, 0, 0)),
            pl.BlockSpec((None, wide, width), lambda c: (c, 0, 0)),
            pl.BlockSpec((None, 1, wide), lambda c: (c, 0, 0)),
        ],
        out_specs=[
            pl.BlockSpec((None, frames, lanes), lambda c: (c, 0, 0)),
            pl.BlockSpec((None, frames, lanes), lambda c: (c, 0, 0)),
        ],
        out_shape=[
            jax.ShapeDtypeStruct((clips, frames, lanes), jnp.float32),
            jax.ShapeDtypeStruct((clips, frames, lanes), jnp.float32),
        ],
    )(emb_v, win_pad, inv_pad)


def _corr_bwd_kernel(gd_ref, at_ref, ev_ref, win_ref, lip_ref, wsum_ref, ginv_ref):
    frames, lanes = gd_ref.shape
    wide = win_ref.shape[0]
    pad = jnp.zeros((frames, wide - lanes), jnp.float32)
    g = jnp.concatenate([gd_ref[...].astype(jnp.float32), pad], axis=1)
    band = pltpu.roll(g, 0, 1, stride=1, stride_axis=0)
    lip_ref[...] = jnp.dot(band.astype(jnp.bfloat16), win_ref[...], preferred_element_type=jnp.float32)
    band_t = band.T.astype(jnp.bfloat16)
    wsum_ref[...] = jnp.dot(band_t, ev_ref[...], preferred_element_type=jnp.float32)
    a = jnp.concatenate([at_ref[...], pad], axis=1)
    spread = pltpu.roll(a, 0, 1, stride=1, stride_axis=0)
    ginv_ref[...] = jnp.sum(spread, axis=0, keepdims=True)


def corr_bwd(gd_pad, at_pad, emb_v, win_pad):
    clips, frames, width = emb_v.shape
    wide = win_pad.shape[1]
    lanes = gd_pad.shape[2]
    return pl.pallas_call(
        _corr_bwd_kernel,
        grid=(clips,),
        in_specs=[
            pl.BlockSpec((None, frames, lanes), lambda c: (c, 0, 0)),
            pl.BlockSpec((None, frames, lanes), lambda c: (c, 0, 0)),
            pl.BlockSpec((None, frames, width), lambda c: (c, 0, 0)),
            pl.BlockSpec((None, wide, width), lambda c: (c, 0, 0)),
        ],
        out_specs=[
            pl.BlockSpec((None, frames, width), lambda c: (c, 0, 0)),
            pl.BlockSpec((None, wide, width), lambda c: (c, 0, 0)),
            pl.BlockSpec((None, 1, wide), lambda c: (c, 0, 0)),
        ],
        out_shape=[
            jax.ShapeDtypeStruct((clips, frames, width), jnp.float32),
            jax.ShapeDtypeStruct((clips, wide, width), jnp.float32),
            jax.ShapeDtypeStruct((clips, 1, wide), jnp.float32),
        ],
    )(gd_pad, at_pad, emb_v, win_pad)


logit_sharpening_divisor = 10.0
loss_scale = 1024.0
epsilon = 1e-06


def padded_2(cells, sides, width):
    for axis, dim in sides:
        count = lax.axis_size(axis)
        ends = count - 1
        head = lax.slice_in_dim(cells, 0, width, axis=dim)
        tail = lax.slice_in_dim(cells, cells.shape[dim] - width, cells.shape[dim], axis=dim)
        cells = jnp.concatenate(
            [
                lax.ppermute(tail, axis, [(i, (i + 1) % count) for i in range(ends)]),
                cells,
                lax.ppermute(head, axis, [((i + 1) % count, i) for i in range(ends)]),
            ],
            axis=dim,
        )
    return cells


def from_behind(value, axis, steps):
    count = lax.axis_size(axis)
    initial, last = (max(0, -steps), min(count, count - steps))
    return lax.ppermute(value, axis, [(source, source + steps) for source in range(initial, last)])


def silu_slope(values):
    sigma = jax.nn.sigmoid(values)
    return sigma * (1.0 + values * (1.0 - sigma))


def encoder(padded, w_conv, w_proj):
    clip_num, frame_pad, chan_num = padded.shape
    frame_num = frame_pad - 2
    columns = jnp.concatenate(
        [padded[:, 0:frame_num], padded[:, 1 : frame_num + 1], padded[:, 2 : frame_num + 2]], axis=2
    )
    before = jnp.einsum(
        "cfk,ke->cfe",
        columns,
        w_conv.reshape(3 * chan_num, w_conv.shape[2]),
        preferred_element_type=jnp.float32,
    )
    hidden = jax.nn.silu(before).astype(jnp.bfloat16)
    embedded = jnp.einsum("cfe,eg->cfg", hidden, w_proj, preferred_element_type=jnp.float32).astype(
        jnp.bfloat16
    )
    return (columns, before, hidden, embedded)


def inverse_norm(embedded):
    values = embedded.astype(jnp.float32)
    return lax.rsqrt(jnp.sum(values * values, axis=-1) + epsilon)


def spread_band(band, wide_len):
    clip_num, row_num, band_len = band.shape
    full_band = jnp.pad(band, ((0, 0), (0, 0), (0, wide_len + 1 - band_len)))
    flat_band = full_band.reshape(clip_num, row_num * (wide_len + 1))[:, : row_num * wide_len]
    return flat_band.reshape(clip_num, row_num, wide_len)


def narrow_band(matrix, band_len):
    clip_num, row_num, wide_len = matrix.shape
    flat_mat = jnp.pad(matrix.reshape(clip_num, row_num * wide_len), ((0, 0), (0, row_num)))
    return flat_mat.reshape(clip_num, row_num, wide_len + 1)[:, :, :band_len]


def flatten_rows(values):
    return values.reshape(values.shape[0] * values.shape[1], values.shape[2])


def proj_grad(hidden, grad_emb):
    return jnp.einsum("re,rf->ef", hidden, grad_emb, preferred_element_type=jnp.float32)


def conv_grad(columns, before, grad_emb, w_proj, w_conv):
    grad_hidden = jnp.einsum("rf,ef->re", grad_emb, w_proj, preferred_element_type=jnp.float32)
    grad_before = (grad_hidden * silu_slope(before)).astype(jnp.bfloat16)
    grad_conv = jnp.einsum("rk,re->ke", columns, grad_before, preferred_element_type=jnp.float32)
    return grad_conv.reshape(w_conv.shape)


def shards(
    audio_feats, lip_feats, lengths, labels, w_audio_conv, w_audio_proj, w_lip_conv, w_lip_proj
):
    clip_num, frame_num, chan_num = audio_feats.shape
    width = w_audio_proj.shape[1]
    offsets = 2 * SPAN + 1
    wide_len = frame_num + 2 * SPAN
    first_frame = lax.axis_index("tm") * frame_num
    stacked = jnp.stack([audio_feats, lip_feats])
    padded = padded_2(stacked, (("tm", 2),), 1)
    cols_a, pre_a, hid_a, emb_a = encoder(padded[0], w_audio_conv, w_audio_proj)
    cols_v, pre_v, hid_v, emb_v = encoder(padded[1], w_lip_conv, w_lip_proj)
    window = padded_2(emb_a, (("tm", 1),), SPAN)
    cols_a, pre_a, hid_a = (flatten_rows(cols_a), flatten_rows(pre_a), flatten_rows(hid_a))
    cols_v, pre_v, hid_v = (flatten_rows(cols_v), flatten_rows(pre_v), flatten_rows(hid_v))
    count_part = jnp.sum(lengths - jnp.abs(labels))
    count_block = jnp.zeros((8, 128), jnp.int32).at[0, 0].set(count_part)
    count = small_sum(count_block, ("k",), 1)[0, 0].astype(jnp.float32)
    inv_win = inverse_norm(window)
    reciprocal_visual_length = inverse_norm(emb_v)
    wide_pad = -(-wide_len // 128) * 128
    win_pad = jnp.pad(window, ((0, 0), (0, wide_pad - wide_len), (0, 0)))
    inv_pad = jnp.pad(inv_win, ((0, 0), (0, wide_pad - wide_len)))[:, None, :]
    dots_rev, strip_rev = corr_fwd(emb_v, win_pad, inv_pad[:, :, ::-1])
    lagged_inner_terms = dots_rev[:, :, ::-1][:, :, :offsets]
    reciprocal_lag_strip = strip_rev[:, :, ::-1][:, :, :offsets]
    frame_ids = first_frame + jnp.arange(frame_num, dtype=jnp.int32)
    shifts = jnp.arange(offsets, dtype=jnp.int32) - SPAN
    positions = frame_ids[:, None] + shifts[None, :]
    inside = frame_ids[None, :] < lengths[:, None]
    valid = inside[:, :, None] & (positions[None] >= 0) & (positions[None] < lengths[:, None, None])
    target_pos = frame_ids[None, :] + labels[:, None]
    counted = inside & (target_pos >= 0) & (target_pos < lengths[:, None])
    correct_lag_position = (shifts[None, :] == labels[:, None]).astype(jnp.float32)
    lag_similarity_logits = (
        logit_sharpening_divisor
        * lagged_inner_terms
        * reciprocal_visual_length[:, :, None]
        * reciprocal_lag_strip
    )
    exponentiated_logits = jnp.where(valid, jnp.exp(lag_similarity_logits), 0.0)
    partition_sums = jnp.where(inside, jnp.sum(exponentiated_logits, axis=2), 1.0)
    picked = jnp.sum(lag_similarity_logits * correct_lag_position[:, None, :], axis=2)
    loss_local = jnp.sum(jnp.where(counted, jnp.log(partition_sums) - picked, 0.0))
    normalized_probabilities = jnp.where(counted, loss_scale / count, 0.0)
    logit_derivative = (
        logit_sharpening_divisor
        * normalized_probabilities[:, :, None]
        * (exponentiated_logits / partition_sums[:, :, None] - correct_lag_position[:, None, :])
    )
    grad_dots = (
        logit_derivative * reciprocal_visual_length[:, :, None] * reciprocal_lag_strip
    ).astype(jnp.bfloat16)
    grad_inv_v = jnp.sum(logit_derivative * lagged_inner_terms * reciprocal_lag_strip, axis=2)
    audio_term = logit_derivative * lagged_inner_terms * reciprocal_visual_length[:, :, None]
    band_pad = ((0, 0), (0, 0), (0, 128 - offsets))
    lip_sum, win_sum_pad, ginv_pad = corr_bwd(
        jnp.pad(grad_dots, band_pad), jnp.pad(audio_term, band_pad), emb_v, win_pad
    )
    grad_inv_win = ginv_pad[:, 0, :wide_len]
    lip_vals = emb_v.astype(jnp.float32)
    grad_lip = (
        lip_sum
        - (
            reciprocal_visual_length
            * reciprocal_visual_length
            * reciprocal_visual_length
            * grad_inv_v
        )[:, :, None]
        * lip_vals
    ).astype(jnp.bfloat16)
    win_sum = win_sum_pad[:, :wide_len]
    win_sum = win_sum - (inv_win * inv_win * inv_win * grad_inv_win)[:, :, None] * window.astype(
        jnp.float32
    )
    own_grad = win_sum[:, SPAN : SPAN + frame_num]
    from_after = from_behind(win_sum[:, :SPAN], "tm", -1)
    from_before = from_behind(win_sum[:, frame_num + SPAN :], "tm", 1)
    own_grad = own_grad.at[:, frame_num - SPAN :].add(from_after)
    own_grad = own_grad.at[:, :SPAN].add(from_before)
    grad_audio = own_grad.astype(jnp.bfloat16).reshape(clip_num * frame_num, width)
    grad_lip = grad_lip.reshape(clip_num * frame_num, width)
    grad_ap = proj_grad(hid_a, grad_audio)
    grad_vp = proj_grad(hid_v, grad_lip)
    grad_ac = conv_grad(cols_a, pre_a, grad_audio, w_audio_proj, w_audio_conv)
    grad_vc = conv_grad(cols_v, pre_v, grad_lip, w_lip_proj, w_lip_conv)
    parts = (grad_ac, grad_vc, grad_ap, grad_vp)
    lanes = grad_ap.shape[1]
    loss_block = jnp.zeros((8, 128), jnp.float32).at[0, 0].set(loss_local)
    *sums, loss_total = all_sum([g.reshape(-1, lanes) for g in parts], loss_block)
    grad_ac, grad_vc, grad_ap, grad_vp = (t.reshape(g.shape) for t, g in zip(sums, parts))
    loss_sum = loss_total[0, 0]
    return (loss_sum / count, grad_ac, grad_ap, grad_vc, grad_vp)


def solution(mesh):
    placed = (
        P("clip", "tm", None),
        P("clip", "tm", None),
        P("clip"),
        P("clip"),
        P(),
        P(),
        P(),
        P(),
    )
    return jax.shard_map(
        shards, mesh=mesh, in_specs=placed, out_specs=(P(), P(), P(), P(), P()), check_vma=False
    )
```

```python
import jax
import jax.numpy as jnp
from jax import lax
from jax.sharding import PartitionSpec as P
import functools
from jax.experimental import pallas as pl
from jax.experimental.pallas import tpu as pltpu

SPAN = 15


MESH_ID = pl.DeviceIdType.MESH


def _coords():
    ci = lax.axis_index("clip")
    ti = lax.axis_index("tm")
    return ci, ti, ci % 4, (ci // 4) % 4, ci // 16, ti % 2, ti // 2


def _levels():
    ci, ti, y, x, zh, core, zl = _coords()
    z = zh * 4 + zl

    def at_y(v):
        return (zh * 16 + x * 4 + v % 4, ti)

    def at_x(v):
        return (zh * 16 + (v % 4) * 4 + y, ti)

    def at_z(v):
        w = v % 8
        return ((w // 4) * 16 + x * 4 + y, (w % 4) * 2 + core)

    def at_c(v):
        return (ci, zl * 2 + v % 2)

    def at_h(v):
        return ((v % 2) * 16 + x * 4 + y, ti)

    def at_k(v):
        return (v % 32, ti)

    return {
        "c": (2, core, at_c, 1),
        "y": (4, y, at_y, 2),
        "x": (4, x, at_x, 2),
        "z": (8, z, at_z, 1),
        "h": (2, zh, at_h, 1),
        "k": (32, ci, at_k, 1),
    }


def _barrier(levels):
    barrier = pltpu.get_barrier_semaphore()
    peers = []
    for n, me, nbr, ndir in levels:
        peers.append(nbr(me + 1))
        if n > 2:
            peers.append(nbr(me - 1))
    for p in peers:
        pl.semaphore_signal(barrier, inc=1, device_id=p, device_id_type=MESH_ID)
    pl.semaphore_wait(barrier, len(peers))


def _small_start(n, me, nbr, s, tbuf, toff, tsend, trecv, tsem):
    at = toff + (me - s) % n
    c = pltpu.make_async_remote_copy(
        src_ref=tbuf.at[at],
        dst_ref=tbuf.at[at],
        send_sem=tsend.at[tsem],
        recv_sem=trecv.at[tsem],
        device_id=nbr(me + 1),
        device_id_type=MESH_ID,
    )
    c.start()
    return c


def _small_sum(n, tbuf, toff):
    acc = tbuf[toff]
    for k in range(1, n):
        acc = acc + tbuf[toff + k]
    return acc


def _small_kernel(names, t_ref, to_ref, tbuf, tsend, trecv):
    table = _levels()
    levels = [table[k] for k in names]
    barrier = pltpu.get_barrier_semaphore()
    peers = [nbr(me + j) for n, me, nbr, ndir in levels for j in range(1, n)]
    for p in peers:
        pl.semaphore_signal(barrier, inc=1, device_id=p, device_id_type=MESH_ID)
    pl.semaphore_wait(barrier, len(peers))
    toff = 0
    tsem = 0
    for li, (n, me, nbr, ndir) in enumerate(levels):
        tbuf[toff + me] = t_ref[...] if li == 0 else to_ref[...]
        copies = []
        for j in range(1, n):
            c = pltpu.make_async_remote_copy(
                src_ref=tbuf.at[toff + me],
                dst_ref=tbuf.at[toff + me],
                send_sem=tsend.at[tsem],
                recv_sem=trecv.at[tsem],
                device_id=nbr(me + j),
                device_id_type=MESH_ID,
            )
            c.start()
            copies.append(c)
            tsem += 1
        for c in copies:
            c.wait()
        to_ref[...] = _small_sum(n, tbuf, toff)
        toff += n


def small_sum(t, names, cid):
    table_n = {"c": 2, "y": 4, "x": 4, "z": 8, "h": 2, "k": 32}
    slots = sum(table_n[k] for k in names)
    sems = sum(table_n[k] - 1 for k in names)
    return pl.pallas_call(
        functools.partial(_small_kernel, names),
        out_shape=jax.ShapeDtypeStruct(t.shape, t.dtype),
        in_specs=[pl.BlockSpec(memory_space=pltpu.VMEM)],
        out_specs=pl.BlockSpec(memory_space=pltpu.VMEM),
        scratch_shapes=[
            pltpu.VMEM((slots,) + t.shape, t.dtype),
            pltpu.SemaphoreType.DMA((sems,)),
            pltpu.SemaphoreType.DMA((sems,)),
        ],
        compiler_params=pltpu.CompilerParams(collective_id=cid, has_side_effects=True),
    )(t)


def _rs_stage(tasks, work, rbuf, send_sem, recv_sem, slot, sem, rider=None):
    n = tasks[0][0]
    for s in range(n - 1):
        copies = []
        for tn, me, nbr, ndir, base, size, own in tasks:
            chunk = size // tn
            piece = chunk // ndir
            for d in range(ndir):
                sign = 1 if d == 0 else -1
                send_at = pl.multiple_of(base + ((me - sign * (s + 1)) % tn) * chunk + d * piece, 8)
                recv_at = pl.multiple_of(base + ((me - sign * (s + 2)) % tn) * chunk + d * piece, 8)
                src = own if s == 0 else work
                c = pltpu.make_async_remote_copy(
                    src_ref=src.at[pl.ds(send_at, piece)],
                    dst_ref=rbuf.at[pl.ds(slot, piece)],
                    send_sem=send_sem.at[sem],
                    recv_sem=recv_sem.at[sem],
                    device_id=nbr(me + sign),
                    device_id_type=MESH_ID,
                )
                c.start()
                copies.append((c, slot, recv_at, piece, own))
                slot += piece
                sem += 1
        ride = rider(s) if rider is not None else None
        for c, sl, recv_at, piece, own in copies:
            c.wait_recv()
            at = pl.ds(recv_at, piece)
            work[at] = rbuf[pl.ds(sl, piece)] + own[at]
        for c, sl, recv_at, piece, own in copies:
            c.wait_send()
        if ride is not None:
            ride.wait()
    return slot, sem


def _ag_stage(tasks, o_ref, send_sem, recv_sem, sem):
    n = tasks[0][0]
    for s in range(n - 1):
        copies = []
        for tn, me, nbr, ndir, base, size, own in tasks:
            chunk = size // tn
            piece = chunk // ndir
            for d in range(ndir):
                sign = 1 if d == 0 else -1
                at = pl.ds(pl.multiple_of(base + ((me - sign * s) % tn) * chunk + d * piece, 8), piece)
                c = pltpu.make_async_remote_copy(
                    src_ref=o_ref.at[at],
                    dst_ref=o_ref.at[at],
                    send_sem=send_sem.at[sem],
                    recv_sem=recv_sem.at[sem],
                    device_id=nbr(me + sign),
                    device_id_type=MESH_ID,
                )
                c.start()
                copies.append(c)
                sem += 1
        for c in copies:
            c.wait()
    return sem


def _pass_copy(buf, at, nbr, target, sems, idx):
    c = pltpu.make_async_remote_copy(
        src_ref=buf.at[at],
        dst_ref=buf.at[at],
        send_sem=sems[0].at[idx],
        recv_sem=sems[1].at[idx],
        device_id=nbr(target),
        device_id_type=MESH_ID,
    )
    c.start()
    return c


def _kernel(sizes, *refs):
    parts = len(sizes)
    ins, t_ref = refs[:parts], refs[parts]
    outs, to_ref = refs[parts + 1 : 2 * parts + 1], refs[2 * parts + 1]
    work, rbuf, zbuf, send_sem, recv_sem, tbuf, tsend, trecv, half_ref, hsend, hrecv, o_ref = refs[2 * parts + 2 :]
    rows = sum(sizes)
    start = 0
    for size, in_ref in zip(sizes, ins):
        work[start : start + size] = in_ref[...]
        start += size
    table = _levels()
    lc, ly, lx, lz = (table[k] for k in ("c", "y", "x", "z"))
    _barrier([lc, ly, lx, lz])
    tsems = (tsend, trecv)
    state = {"toff": 0, "tsem": 0}

    def tiny_level(level, first):
        n, me, nbr, ndir = level
        toff = state["toff"]
        tbuf[toff + me] = t_ref[...] if first else to_ref[...]

        def rider(s):
            c = _pass_copy(tbuf, toff + (me - s) % n, nbr, me + 1, tsems, state["tsem"])
            state["tsem"] += 1
            return c

        return rider

    def tiny_done(n):
        to_ref[...] = _small_sum(n, tbuf, state["toff"])
        state["toff"] += n

    slot, sem = 0, 0
    half = rows // 2
    quarter = rows // 4
    nc, core, nbc, _ = lc
    ny, yi, nby, _ = ly
    nx, xi, nbx, _ = lx
    nz, zi, nbz, _ = lz

    rider = tiny_level(lc, True)
    slot, sem = _rs_stage([(nc, core, nbc, 2, 0, rows, work)], work, rbuf, send_sem, recv_sem, slot, sem, rider)
    tiny_done(nc)
    r0 = core * half
    a1, b1 = r0, r0 + quarter
    rider = tiny_level(ly, False)
    slot, sem = _rs_stage(
        [(ny, yi, nby, 2, a1, quarter, work), (nx, xi, nbx, 2, b1, quarter, work)],
        work, rbuf, send_sem, recv_sem, slot, sem, rider,
    )
    tiny_done(ny)
    c1 = quarter // 4
    a2, b2 = a1 + yi * c1, b1 + xi * c1
    rider = tiny_level(lx, False)
    slot, sem = _rs_stage(
        [(nx, xi, nbx, 1, a2, c1, work), (ny, yi, nby, 1, b2, c1, work)],
        work, rbuf, send_sem, recv_sem, slot, sem, rider,
    )
    tiny_done(nx)
    c2 = c1 // 4
    a3, b3 = a2 + xi * c2, b2 + yi * c2
    zbuf[zi, 0] = work[pl.ds(pl.multiple_of(a3, 8), c2)]
    zbuf[zi, 1] = work[pl.ds(pl.multiple_of(b3, 8), c2)]
    toff = state["toff"]
    tbuf[toff + zi] = to_ref[...]
    right = nz // 2
    left = nz - 1 - right
    for s in range(right):
        cs = [
            _pass_copy(zbuf, (zi - s) % nz, nbz, zi + 1, (send_sem, recv_sem), sem),
            _pass_copy(tbuf, toff + (zi - s) % nz, nbz, zi + 1, tsems, state["tsem"]),
        ]
        sem += 1
        state["tsem"] += 1
        if s < left:
            cs.append(_pass_copy(zbuf, (zi + s) % nz, nbz, zi - 1, (send_sem, recv_sem), sem))
            cs.append(_pass_copy(tbuf, toff + (zi + s) % nz, nbz, zi - 1, tsems, state["tsem"]))
            sem += 1
            state["tsem"] += 1
        for c in cs:
            c.wait()
    for colour, at in ((0, a3), (1, b3)):
        acc = zbuf[0, colour]
        for k in range(1, nz):
            acc = acc + zbuf[k, colour]
        o_ref[pl.ds(pl.multiple_of(at, 8), c2)] = acc
    tiny_done(nz)
    sem = _ag_stage([(nx, xi, nbx, 1, a2, c1, None), (ny, yi, nby, 1, b2, c1, None)], o_ref, send_sem, recv_sem, sem)
    for at in (a2, b2):
        region = pl.ds(pl.multiple_of(at, 16), c1)
        half_ref[region] = o_ref[region].astype(half_ref.dtype)
    sem = _ag_stage([(ny, yi, nby, 2, a1, quarter, None), (nx, xi, nbx, 2, b1, quarter, None)], half_ref, hsend, hrecv, 0)
    _ag_stage([(nc, core, nbc, 2, 0, rows, None)], half_ref, hsend, hrecv, sem)
    start = 0
    for size, out_ref in zip(sizes, outs):
        out_ref[...] = half_ref[start : start + size].astype(out_ref.dtype)
        start += size


def _counts(rows):
    half, quarter = rows // 2, rows // 4
    c1 = quarter // 4
    slots = half + 3 * 2 * quarter // 4 + 3 * 2 * c1 // 4
    sems = 2 + 3 * 4 + 3 * 2 + 7 + 3 * 2
    return slots, sems, 2 + 4 + 4 + 8, 1 + 3 + 3 + 7


def all_sum(parts, small):
    sizes = tuple(p.shape[0] for p in parts)
    lanes = parts[0].shape[1]
    rows = sum(sizes)
    slots, sems, tslots, tsems = _counts(rows)
    c2 = rows // 64
    vmem = pl.BlockSpec(memory_space=pltpu.VMEM)
    return pl.pallas_call(
        functools.partial(_kernel, sizes),
        out_shape=tuple(jax.ShapeDtypeStruct(p.shape, p.dtype) for p in parts)
        + (jax.ShapeDtypeStruct(small.shape, small.dtype),),
        in_specs=[vmem] * (len(parts) + 1),
        out_specs=(vmem,) * (len(parts) + 1),
        scratch_shapes=[
            pltpu.VMEM((rows, lanes), jnp.float32),
            pltpu.VMEM((slots, lanes), jnp.float32),
            pltpu.VMEM((8, 2, c2, lanes), jnp.float32),
            pltpu.SemaphoreType.DMA((sems,)),
            pltpu.SemaphoreType.DMA((sems,)),
            pltpu.VMEM((tslots,) + small.shape, small.dtype),
            pltpu.SemaphoreType.DMA((tsems,)),
            pltpu.SemaphoreType.DMA((tsems,)),
            pltpu.VMEM((rows, lanes), jnp.bfloat16),
            pltpu.SemaphoreType.DMA((14,)),
            pltpu.SemaphoreType.DMA((14,)),
            pltpu.VMEM((rows, lanes), jnp.float32),
        ],
        compiler_params=pltpu.CompilerParams(
            collective_id=0, has_side_effects=True, vmem_limit_bytes=48 * 1024 * 1024
        ),
    )(*parts, small)


def _corr_fwd_kernel(ev_ref, win_ref, inv_ref, dots_ref, strip_ref):
    wide = win_ref.shape[0]
    lanes = dots_ref.shape[1]
    rows = lax.broadcasted_iota(jnp.int32, (wide, wide), 0)
    cols = lax.broadcasted_iota(jnp.int32, (wide, wide), 1)
    flip = (rows + cols == wide - 1).astype(jnp.bfloat16)
    win_rev = jnp.dot(flip, win_ref[...], preferred_element_type=jnp.float32).astype(jnp.bfloat16)
    m = lax.dot_general(
        ev_ref[...], win_rev, (((1,), (1,)), ((), ())), preferred_element_type=jnp.float32
    )
    dots_ref[...] = pltpu.roll(m, 0, 1, stride=1, stride_axis=0)[:, wide - lanes :]
    inv = jnp.broadcast_to(inv_ref[...], m.shape)
    strip_ref[...] = pltpu.roll(inv, 0, 1, stride=1, stride_axis=0)[:, wide - lanes :]


def corr_fwd(emb_v, win_pad, inv_pad):
    clips, frames, width = emb_v.shape
    wide = win_pad.shape[1]
    lanes = 128
    return pl.pallas_call(
        _corr_fwd_kernel,
        grid=(clips,),
        in_specs=[
            pl.BlockSpec((None, frames, width), lambda c: (c, 0, 0)),
            pl.BlockSpec((None, wide, width), lambda c: (c, 0, 0)),
            pl.BlockSpec((None, 1, wide), lambda c: (c, 0, 0)),
        ],
        out_specs=[
            pl.BlockSpec((None, frames, lanes), lambda c: (c, 0, 0)),
            pl.BlockSpec((None, frames, lanes), lambda c: (c, 0, 0)),
        ],
        out_shape=[
            jax.ShapeDtypeStruct((clips, frames, lanes), jnp.float32),
            jax.ShapeDtypeStruct((clips, frames, lanes), jnp.float32),
        ],
    )(emb_v, win_pad, inv_pad)


def _corr_bwd_kernel(gd_ref, at_ref, ev_ref, win_ref, lip_ref, wsum_ref, ginv_ref):
    frames, lanes = gd_ref.shape
    wide = win_ref.shape[0]
    pad = jnp.zeros((frames, wide - lanes), jnp.float32)
    g = jnp.concatenate([gd_ref[...].astype(jnp.float32), pad], axis=1)
    band = pltpu.roll(g, 0, 1, stride=1, stride_axis=0)
    lip_ref[...] = jnp.dot(band.astype(jnp.bfloat16), win_ref[...], preferred_element_type=jnp.float32)
    band_t = band.T.astype(jnp.bfloat16)
    wsum_ref[...] = jnp.dot(band_t, ev_ref[...], preferred_element_type=jnp.float32)
    a = jnp.concatenate([at_ref[...], pad], axis=1)
    spread = pltpu.roll(a, 0, 1, stride=1, stride_axis=0)
    ginv_ref[...] = jnp.sum(spread, axis=0, keepdims=True)


def corr_bwd(gd_pad, at_pad, emb_v, win_pad):
    clips, frames, width = emb_v.shape
    wide = win_pad.shape[1]
    lanes = gd_pad.shape[2]
    return pl.pallas_call(
        _corr_bwd_kernel,
        grid=(clips,),
        in_specs=[
            pl.BlockSpec((None, frames, lanes), lambda c: (c, 0, 0)),
            pl.BlockSpec((None, frames, lanes), lambda c: (c, 0, 0)),
            pl.BlockSpec((None, frames, width), lambda c: (c, 0, 0)),
            pl.BlockSpec((None, wide, width), lambda c: (c, 0, 0)),
        ],
        out_specs=[
            pl.BlockSpec((None, frames, width), lambda c: (c, 0, 0)),
            pl.BlockSpec((None, wide, width), lambda c: (c, 0, 0)),
            pl.BlockSpec((None, 1, wide), lambda c: (c, 0, 0)),
        ],
        out_shape=[
            jax.ShapeDtypeStruct((clips, frames, width), jnp.float32),
            jax.ShapeDtypeStruct((clips, wide, width), jnp.float32),
            jax.ShapeDtypeStruct((clips, 1, wide), jnp.float32),
        ],
    )(gd_pad, at_pad, emb_v, win_pad)


logit_sharpening_divisor = 10.0
loss_scale = 1024.0
epsilon = 1e-06


def padded_2(cells, sides, width):
    for axis, dim in sides:
        count = lax.axis_size(axis)
        ends = count - 1
        head = lax.slice_in_dim(cells, 0, width, axis=dim)
        tail = lax.slice_in_dim(cells, cells.shape[dim] - width, cells.shape[dim], axis=dim)
        cells = jnp.concatenate(
            [
                lax.ppermute(tail, axis, [(i, (i + 1) % count) for i in range(ends)]),
                cells,
                lax.ppermute(head, axis, [((i + 1) % count, i) for i in range(ends)]),
            ],
            axis=dim,
        )
    return cells


def from_behind(value, axis, steps):
    count = lax.axis_size(axis)
    initial, last = (max(0, -steps), min(count, count - steps))
    return lax.ppermute(value, axis, [(source, source + steps) for source in range(initial, last)])


def silu_slope(values):
    sigma = jax.nn.sigmoid(values)
    return sigma * (1.0 + values * (1.0 - sigma))


def encoder(padded, w_conv, w_proj):
    clip_num, frame_pad, chan_num = padded.shape
    frame_num = frame_pad - 2
    columns = jnp.concatenate(
        [padded[:, 0:frame_num], padded[:, 1 : frame_num + 1], padded[:, 2 : frame_num + 2]], axis=2
    )
    before = jnp.einsum(
        "cfk,ke->cfe",
        columns,
        w_conv.reshape(3 * chan_num, w_conv.shape[2]),
        preferred_element_type=jnp.float32,
    )
    hidden = jax.nn.silu(before).astype(jnp.bfloat16)
    embedded = jnp.einsum("cfe,eg->cfg", hidden, w_proj, preferred_element_type=jnp.float32).astype(
        jnp.bfloat16
    )
    return (columns, before, hidden, embedded)


def inverse_norm(embedded):
    values = embedded.astype(jnp.float32)
    return lax.rsqrt(jnp.sum(values * values, axis=-1) + epsilon)


def spread_band(band, wide_len):
    clip_num, row_num, band_len = band.shape
    full_band = jnp.pad(band, ((0, 0), (0, 0), (0, wide_len + 1 - band_len)))
    flat_band = full_band.reshape(clip_num, row_num * (wide_len + 1))[:, : row_num * wide_len]
    return flat_band.reshape(clip_num, row_num, wide_len)


def narrow_band(matrix, band_len):
    clip_num, row_num, wide_len = matrix.shape
    flat_mat = jnp.pad(matrix.reshape(clip_num, row_num * wide_len), ((0, 0), (0, row_num)))
    return flat_mat.reshape(clip_num, row_num, wide_len + 1)[:, :, :band_len]


def flatten_rows(values):
    return values.reshape(values.shape[0] * values.shape[1], values.shape[2])


def proj_grad(hidden, grad_emb):
    return jnp.einsum("re,rf->ef", hidden, grad_emb, preferred_element_type=jnp.float32)


def conv_grad(columns, before, grad_emb, w_proj, w_conv):
    grad_hidden = jnp.einsum("rf,ef->re", grad_emb, w_proj, preferred_element_type=jnp.float32)
    grad_before = (grad_hidden * silu_slope(before)).astype(jnp.bfloat16)
    grad_conv = jnp.einsum("rk,re->ke", columns, grad_before, preferred_element_type=jnp.float32)
    return grad_conv.reshape(w_conv.shape)


def shards(
    audio_feats, lip_feats, lengths, labels, w_audio_conv, w_audio_proj, w_lip_conv, w_lip_proj
):
    clip_num, frame_num, chan_num = audio_feats.shape
    width = w_audio_proj.shape[1]
    offsets = 2 * SPAN + 1
    wide_len = frame_num + 2 * SPAN
    first_frame = lax.axis_index("tm") * frame_num
    stacked = jnp.stack([audio_feats, lip_feats])
    padded = padded_2(stacked, (("tm", 2),), 1)
    cols_a, pre_a, hid_a, emb_a = encoder(padded[0], w_audio_conv, w_audio_proj)
    cols_v, pre_v, hid_v, emb_v = encoder(padded[1], w_lip_conv, w_lip_proj)
    window = padded_2(emb_a, (("tm", 1),), SPAN)
    cols_a, pre_a, hid_a = (flatten_rows(cols_a), flatten_rows(pre_a), flatten_rows(hid_a))
    cols_v, pre_v, hid_v = (flatten_rows(cols_v), flatten_rows(pre_v), flatten_rows(hid_v))
    count_part = jnp.sum(lengths - jnp.abs(labels))
    count_block = jnp.zeros((8, 128), jnp.int32).at[0, 0].set(count_part)
    count = small_sum(count_block, ("k",), 1)[0, 0].astype(jnp.float32)
    inv_win = inverse_norm(window)
    reciprocal_visual_length = inverse_norm(emb_v)
    wide_pad = -(-wide_len // 128) * 128
    win_pad = jnp.pad(window, ((0, 0), (0, wide_pad - wide_len), (0, 0)))
    inv_pad = jnp.pad(inv_win, ((0, 0), (0, wide_pad - wide_len)))[:, None, :]
    dots_rev, strip_rev = corr_fwd(emb_v, win_pad, inv_pad[:, :, ::-1])
    lagged_inner_terms = dots_rev[:, :, ::-1][:, :, :offsets]
    reciprocal_lag_strip = strip_rev[:, :, ::-1][:, :, :offsets]
    frame_ids = first_frame + jnp.arange(frame_num, dtype=jnp.int32)
    shifts = jnp.arange(offsets, dtype=jnp.int32) - SPAN
    positions = frame_ids[:, None] + shifts[None, :]
    inside = frame_ids[None, :] < lengths[:, None]
    valid = inside[:, :, None] & (positions[None] >= 0) & (positions[None] < lengths[:, None, None])
    target_pos = frame_ids[None, :] + labels[:, None]
    counted = inside & (target_pos >= 0) & (target_pos < lengths[:, None])
    correct_lag_position = (shifts[None, :] == labels[:, None]).astype(jnp.float32)
    lag_similarity_logits = (
        logit_sharpening_divisor
        * lagged_inner_terms
        * reciprocal_visual_length[:, :, None]
        * reciprocal_lag_strip
    )
    exponentiated_logits = jnp.where(valid, jnp.exp(lag_similarity_logits), 0.0)
    partition_sums = jnp.where(inside, jnp.sum(exponentiated_logits, axis=2), 1.0)
    picked = jnp.sum(lag_similarity_logits * correct_lag_position[:, None, :], axis=2)
    loss_local = jnp.sum(jnp.where(counted, jnp.log(partition_sums) - picked, 0.0))
    normalized_probabilities = jnp.where(counted, loss_scale / count, 0.0)
    logit_derivative = (
        logit_sharpening_divisor
        * normalized_probabilities[:, :, None]
        * (exponentiated_logits / partition_sums[:, :, None] - correct_lag_position[:, None, :])
    )
    grad_dots = (
        logit_derivative * reciprocal_visual_length[:, :, None] * reciprocal_lag_strip
    ).astype(jnp.bfloat16)
    grad_inv_v = jnp.sum(logit_derivative * lagged_inner_terms * reciprocal_lag_strip, axis=2)
    audio_term = logit_derivative * lagged_inner_terms * reciprocal_visual_length[:, :, None]
    band_pad = ((0, 0), (0, 0), (0, 128 - offsets))
    lip_sum, win_sum_pad, ginv_pad = corr_bwd(
        jnp.pad(grad_dots, band_pad), jnp.pad(audio_term, band_pad), emb_v, win_pad
    )
    grad_inv_win = ginv_pad[:, 0, :wide_len]
    lip_vals = emb_v.astype(jnp.float32)
    grad_lip = (
        lip_sum
        - (
            reciprocal_visual_length
            * reciprocal_visual_length
            * reciprocal_visual_length
            * grad_inv_v
        )[:, :, None]
        * lip_vals
    ).astype(jnp.bfloat16)
    win_sum = win_sum_pad[:, :wide_len]
    win_sum = win_sum - (inv_win * inv_win * inv_win * grad_inv_win)[:, :, None] * window.astype(
        jnp.float32
    )
    own_grad = win_sum[:, SPAN : SPAN + frame_num]
    from_after = from_behind(win_sum[:, :SPAN], "tm", -1)
    from_before = from_behind(win_sum[:, frame_num + SPAN :], "tm", 1)
    own_grad = own_grad.at[:, frame_num - SPAN :].add(from_after)
    own_grad = own_grad.at[:, :SPAN].add(from_before)
    grad_audio = own_grad.astype(jnp.bfloat16).reshape(clip_num * frame_num, width)
    grad_lip = grad_lip.reshape(clip_num * frame_num, width)
    grad_ap = proj_grad(hid_a, grad_audio)
    grad_vp = proj_grad(hid_v, grad_lip)
    grad_ac = conv_grad(cols_a, pre_a, grad_audio, w_audio_proj, w_audio_conv)
    grad_vc = conv_grad(cols_v, pre_v, grad_lip, w_lip_proj, w_lip_conv)
    parts = (grad_ac, grad_vc, grad_ap, grad_vp)
    lanes = grad_ap.shape[1]
    loss_block = jnp.zeros((8, 128), jnp.float32).at[0, 0].set(loss_local)
    *sums, loss_total = all_sum([g.reshape(-1, lanes) for g in parts], loss_block)
    grad_ac, grad_vc, grad_ap, grad_vp = (t.reshape(g.shape) for t, g in zip(sums, parts))
    loss_sum = loss_total[0, 0]
    return (loss_sum / count, grad_ac, grad_ap, grad_vc, grad_vp)


def solution(mesh):
    placed = (
        P("clip", "tm", None),
        P("clip", "tm", None),
        P("clip"),
        P("clip"),
        P(),
        P(),
        P(),
        P(),
    )
    return jax.shard_map(
        shards, mesh=mesh, in_specs=placed, out_specs=(P(), P(), P(), P(), P()), check_vma=False
    )
```

```python
import jax
import jax.numpy as jnp
from jax import lax
from jax.sharding import PartitionSpec as P
import functools
from jax.experimental import pallas as pl
from jax.experimental.pallas import tpu as pltpu

SPAN = 15


MESH_ID = pl.DeviceIdType.MESH


def _coords():
    ci = lax.axis_index("clip")
    ti = lax.axis_index("tm")
    return ci, ti, ci % 4, (ci // 4) % 4, ci // 16, ti % 2, ti // 2


def _levels():
    ci, ti, y, x, zh, core, zl = _coords()
    z = zh * 4 + zl

    def at_y(v):
        return (zh * 16 + x * 4 + v % 4, ti)

    def at_x(v):
        return (zh * 16 + (v % 4) * 4 + y, ti)

    def at_z(v):
        w = v % 8
        return ((w // 4) * 16 + x * 4 + y, (w % 4) * 2 + core)

    def at_c(v):
        return (ci, zl * 2 + v % 2)

    def at_h(v):
        return ((v % 2) * 16 + x * 4 + y, ti)

    def at_k(v):
        return (v % 32, ti)

    return {
        "c": (2, core, at_c, 1),
        "y": (4, y, at_y, 2),
        "x": (4, x, at_x, 2),
        "z": (8, z, at_z, 1),
        "h": (2, zh, at_h, 1),
        "k": (32, ci, at_k, 1),
    }


def _barrier(levels):
    barrier = pltpu.get_barrier_semaphore()
    peers = []
    for n, me, nbr, ndir in levels:
        peers.append(nbr(me + 1))
        if n > 2:
            peers.append(nbr(me - 1))
    for p in peers:
        pl.semaphore_signal(barrier, inc=1, device_id=p, device_id_type=MESH_ID)
    pl.semaphore_wait(barrier, len(peers))


def _small_start(n, me, nbr, s, tbuf, toff, tsend, trecv, tsem):
    at = toff + (me - s) % n
    c = pltpu.make_async_remote_copy(
        src_ref=tbuf.at[at],
        dst_ref=tbuf.at[at],
        send_sem=tsend.at[tsem],
        recv_sem=trecv.at[tsem],
        device_id=nbr(me + 1),
        device_id_type=MESH_ID,
    )
    c.start()
    return c


def _small_sum(n, tbuf, toff):
    acc = tbuf[toff]
    for k in range(1, n):
        acc = acc + tbuf[toff + k]
    return acc


def _small_kernel(names, t_ref, to_ref, tbuf, tsend, trecv):
    table = _levels()
    levels = [table[k] for k in names]
    barrier = pltpu.get_barrier_semaphore()
    peers = [nbr(me + j) for n, me, nbr, ndir in levels for j in range(1, n)]
    for p in peers:
        pl.semaphore_signal(barrier, inc=1, device_id=p, device_id_type=MESH_ID)
    pl.semaphore_wait(barrier, len(peers))
    toff = 0
    tsem = 0
    for li, (n, me, nbr, ndir) in enumerate(levels):
        tbuf[toff + me] = t_ref[...] if li == 0 else to_ref[...]
        copies = []
        for j in range(1, n):
            c = pltpu.make_async_remote_copy(
                src_ref=tbuf.at[toff + me],
                dst_ref=tbuf.at[toff + me],
                send_sem=tsend.at[tsem],
                recv_sem=trecv.at[tsem],
                device_id=nbr(me + j),
                device_id_type=MESH_ID,
            )
            c.start()
            copies.append(c)
            tsem += 1
        for c in copies:
            c.wait()
        to_ref[...] = _small_sum(n, tbuf, toff)
        toff += n


def small_sum(t, names, cid):
    table_n = {"c": 2, "y": 4, "x": 4, "z": 8, "h": 2, "k": 32}
    slots = sum(table_n[k] for k in names)
    sems = sum(table_n[k] - 1 for k in names)
    return pl.pallas_call(
        functools.partial(_small_kernel, names),
        out_shape=jax.ShapeDtypeStruct(t.shape, t.dtype),
        in_specs=[pl.BlockSpec(memory_space=pltpu.VMEM)],
        out_specs=pl.BlockSpec(memory_space=pltpu.VMEM),
        scratch_shapes=[
            pltpu.VMEM((slots,) + t.shape, t.dtype),
            pltpu.SemaphoreType.DMA((sems,)),
            pltpu.SemaphoreType.DMA((sems,)),
        ],
        compiler_params=pltpu.CompilerParams(collective_id=cid, has_side_effects=True),
    )(t)


def _rs_stage(tasks, work, rbuf, send_sem, recv_sem, slot, sem, rider=None):
    n = tasks[0][0]
    for s in range(n - 1):
        copies = []
        for tn, me, nbr, ndir, base, size, own in tasks:
            chunk = size // tn
            piece = chunk // ndir
            for d in range(ndir):
                sign = 1 if d == 0 else -1
                send_at = pl.multiple_of(base + ((me - sign * (s + 1)) % tn) * chunk + d * piece, 8)
                recv_at = pl.multiple_of(base + ((me - sign * (s + 2)) % tn) * chunk + d * piece, 8)
                src = own if s == 0 else work
                c = pltpu.make_async_remote_copy(
                    src_ref=src.at[pl.ds(send_at, piece)],
                    dst_ref=rbuf.at[pl.ds(slot, piece)],
                    send_sem=send_sem.at[sem],
                    recv_sem=recv_sem.at[sem],
                    device_id=nbr(me + sign),
                    device_id_type=MESH_ID,
                )
                c.start()
                copies.append((c, slot, recv_at, piece, own))
                slot += piece
                sem += 1
        ride = rider(s) if rider is not None else None
        for c, sl, recv_at, piece, own in copies:
            c.wait_recv()
            at = pl.ds(recv_at, piece)
            work[at] = rbuf[pl.ds(sl, piece)] + own[at]
        for c, sl, recv_at, piece, own in copies:
            c.wait_send()
        if ride is not None:
            ride.wait()
    return slot, sem


def _ag_stage(tasks, o_ref, send_sem, recv_sem, sem):
    n = tasks[0][0]
    for s in range(n - 1):
        copies = []
        for tn, me, nbr, ndir, base, size, own in tasks:
            chunk = size // tn
            piece = chunk // ndir
            for d in range(ndir):
                sign = 1 if d == 0 else -1
                at = pl.ds(pl.multiple_of(base + ((me - sign * s) % tn) * chunk + d * piece, 8), piece)
                c = pltpu.make_async_remote_copy(
                    src_ref=o_ref.at[at],
                    dst_ref=o_ref.at[at],
                    send_sem=send_sem.at[sem],
                    recv_sem=recv_sem.at[sem],
                    device_id=nbr(me + sign),
                    device_id_type=MESH_ID,
                )
                c.start()
                copies.append(c)
                sem += 1
        for c in copies:
            c.wait()
    return sem


def _pass_copy(buf, at, nbr, target, sems, idx):
    c = pltpu.make_async_remote_copy(
        src_ref=buf.at[at],
        dst_ref=buf.at[at],
        send_sem=sems[0].at[idx],
        recv_sem=sems[1].at[idx],
        device_id=nbr(target),
        device_id_type=MESH_ID,
    )
    c.start()
    return c


def _kernel(sizes, *refs):
    parts = len(sizes)
    ins, t_ref = refs[:parts], refs[parts]
    outs, to_ref = refs[parts + 1 : 2 * parts + 1], refs[2 * parts + 1]
    work, rbuf, zbuf, send_sem, recv_sem, tbuf, tsend, trecv, half_ref, hsend, hrecv, o_ref = refs[2 * parts + 2 :]
    rows = sum(sizes)
    start = 0
    for size, in_ref in zip(sizes, ins):
        work[start : start + size] = in_ref[...]
        start += size
    table = _levels()
    lc, ly, lx, lz = (table[k] for k in ("c", "y", "x", "z"))
    _barrier([lc, ly, lx, lz])
    tsems = (tsend, trecv)
    state = {"toff": 0, "tsem": 0}

    def tiny_level(level, first):
        n, me, nbr, ndir = level
        toff = state["toff"]
        tbuf[toff + me] = t_ref[...] if first else to_ref[...]

        def rider(s):
            c = _pass_copy(tbuf, toff + (me - s) % n, nbr, me + 1, tsems, state["tsem"])
            state["tsem"] += 1
            return c

        return rider

    def tiny_done(n):
        to_ref[...] = _small_sum(n, tbuf, state["toff"])
        state["toff"] += n

    slot, sem = 0, 0
    half = rows // 2
    quarter = rows // 4
    nc, core, nbc, _ = lc
    ny, yi, nby, _ = ly
    nx, xi, nbx, _ = lx
    nz, zi, nbz, _ = lz

    rider = tiny_level(lc, True)
    slot, sem = _rs_stage([(nc, core, nbc, 1, 0, rows, work)], work, rbuf, send_sem, recv_sem, slot, sem, rider)
    tiny_done(nc)
    r0 = core * half
    a1, b1 = r0, r0 + quarter
    rider = tiny_level(ly, False)
    slot, sem = _rs_stage(
        [(ny, yi, nby, 2, a1, quarter, work), (nx, xi, nbx, 2, b1, quarter, work)],
        work, rbuf, send_sem, recv_sem, slot, sem, rider,
    )
    tiny_done(ny)
    c1 = quarter // 4
    a2, b2 = a1 + yi * c1, b1 + xi * c1
    rider = tiny_level(lx, False)
    slot, sem = _rs_stage(
        [(nx, xi, nbx, 1, a2, c1, work), (ny, yi, nby, 1, b2, c1, work)],
        work, rbuf, send_sem, recv_sem, slot, sem, rider,
    )
    tiny_done(nx)
    c2 = c1 // 4
    a3, b3 = a2 + xi * c2, b2 + yi * c2
    zbuf[zi, 0] = work[pl.ds(pl.multiple_of(a3, 8), c2)]
    zbuf[zi, 1] = work[pl.ds(pl.multiple_of(b3, 8), c2)]
    toff = state["toff"]
    tbuf[toff + zi] = to_ref[...]
    right = nz // 2
    left = nz - 1 - right
    for s in range(right):
        cs = [
            _pass_copy(zbuf, (zi - s) % nz, nbz, zi + 1, (send_sem, recv_sem), sem),
            _pass_copy(tbuf, toff + (zi - s) % nz, nbz, zi + 1, tsems, state["tsem"]),
        ]
        sem += 1
        state["tsem"] += 1
        if s < left:
            cs.append(_pass_copy(zbuf, (zi + s) % nz, nbz, zi - 1, (send_sem, recv_sem), sem))
            cs.append(_pass_copy(tbuf, toff + (zi + s) % nz, nbz, zi - 1, tsems, state["tsem"]))
            sem += 1
            state["tsem"] += 1
        for c in cs:
            c.wait()
    for colour, at in ((0, a3), (1, b3)):
        acc = zbuf[0, colour]
        for k in range(1, nz):
            acc = acc + zbuf[k, colour]
        o_ref[pl.ds(pl.multiple_of(at, 8), c2)] = acc
    tiny_done(nz)
    sem = _ag_stage([(nx, xi, nbx, 1, a2, c1, None), (ny, yi, nby, 1, b2, c1, None)], o_ref, send_sem, recv_sem, sem)
    for at in (a2, b2):
        region = pl.ds(pl.multiple_of(at, 16), c1)
        half_ref[region] = o_ref[region].astype(half_ref.dtype)
    sem = _ag_stage([(ny, yi, nby, 2, a1, quarter, None), (nx, xi, nbx, 2, b1, quarter, None)], half_ref, hsend, hrecv, 0)
    _ag_stage([(nc, core, nbc, 1, 0, rows, None)], half_ref, hsend, hrecv, sem)
    start = 0
    for size, out_ref in zip(sizes, outs):
        out_ref[...] = half_ref[start : start + size].astype(out_ref.dtype)
        start += size


def _counts(rows):
    half, quarter = rows // 2, rows // 4
    c1 = quarter // 4
    slots = half + 3 * 2 * quarter // 4 + 3 * 2 * c1 // 4
    sems = 1 + 3 * 4 + 3 * 2 + 7 + 3 * 2
    return slots, sems, 2 + 4 + 4 + 8, 1 + 3 + 3 + 7


def all_sum(parts, small):
    sizes = tuple(p.shape[0] for p in parts)
    lanes = parts[0].shape[1]
    rows = sum(sizes)
    slots, sems, tslots, tsems = _counts(rows)
    c2 = rows // 64
    vmem = pl.BlockSpec(memory_space=pltpu.VMEM)
    return pl.pallas_call(
        functools.partial(_kernel, sizes),
        out_shape=tuple(jax.ShapeDtypeStruct(p.shape, p.dtype) for p in parts)
        + (jax.ShapeDtypeStruct(small.shape, small.dtype),),
        in_specs=[vmem] * (len(parts) + 1),
        out_specs=(vmem,) * (len(parts) + 1),
        scratch_shapes=[
            pltpu.VMEM((rows, lanes), jnp.float32),
            pltpu.VMEM((slots, lanes), jnp.float32),
            pltpu.VMEM((8, 2, c2, lanes), jnp.float32),
            pltpu.SemaphoreType.DMA((sems,)),
            pltpu.SemaphoreType.DMA((sems,)),
            pltpu.VMEM((tslots,) + small.shape, small.dtype),
            pltpu.SemaphoreType.DMA((tsems,)),
            pltpu.SemaphoreType.DMA((tsems,)),
            pltpu.VMEM((rows, lanes), jnp.bfloat16),
            pltpu.SemaphoreType.DMA((13,)),
            pltpu.SemaphoreType.DMA((13,)),
            pltpu.VMEM((rows, lanes), jnp.float32),
        ],
        compiler_params=pltpu.CompilerParams(
            collective_id=0, has_side_effects=True, vmem_limit_bytes=48 * 1024 * 1024
        ),
    )(*parts, small)


def _corr_fwd_kernel(ev_ref, win_ref, inv_ref, dots_ref, strip_ref):
    wide = win_ref.shape[0]
    lanes = dots_ref.shape[1]
    rows = lax.broadcasted_iota(jnp.int32, (wide, wide), 0)
    cols = lax.broadcasted_iota(jnp.int32, (wide, wide), 1)
    flip = (rows + cols == wide - 1).astype(jnp.bfloat16)
    win_rev = jnp.dot(flip, win_ref[...], preferred_element_type=jnp.float32).astype(jnp.bfloat16)
    m = lax.dot_general(
        ev_ref[...], win_rev, (((1,), (1,)), ((), ())), preferred_element_type=jnp.float32
    )
    rows = lax.broadcasted_iota(jnp.int32, (lanes, lanes), 0)
    cols = lax.broadcasted_iota(jnp.int32, (lanes, lanes), 1)
    back = (rows + cols == lanes - 1).astype(jnp.float32)

    def unflip(x):
        return jnp.dot(x, back, precision=lax.Precision.HIGHEST, preferred_element_type=jnp.float32)

    dots_ref[...] = unflip(pltpu.roll(m, 0, 1, stride=1, stride_axis=0)[:, wide - lanes :])
    inv = jnp.broadcast_to(inv_ref[...], m.shape)
    strip_ref[...] = unflip(pltpu.roll(inv, 0, 1, stride=1, stride_axis=0)[:, wide - lanes :])


def corr_fwd(emb_v, win_pad, inv_pad):
    clips, frames, width = emb_v.shape
    wide = win_pad.shape[1]
    lanes = 128
    return pl.pallas_call(
        _corr_fwd_kernel,
        grid=(clips,),
        in_specs=[
            pl.BlockSpec((None, frames, width), lambda c: (c, 0, 0)),
            pl.BlockSpec((None, wide, width), lambda c: (c, 0, 0)),
            pl.BlockSpec((None, 1, wide), lambda c: (c, 0, 0)),
        ],
        out_specs=[
            pl.BlockSpec((None, frames, lanes), lambda c: (c, 0, 0)),
            pl.BlockSpec((None, frames, lanes), lambda c: (c, 0, 0)),
        ],
        out_shape=[
            jax.ShapeDtypeStruct((clips, frames, lanes), jnp.float32),
            jax.ShapeDtypeStruct((clips, frames, lanes), jnp.float32),
        ],
    )(emb_v, win_pad, inv_pad)


def _corr_bwd_kernel(gd_ref, at_ref, ev_ref, win_ref, lip_ref, wsum_ref, ginv_ref):
    frames, lanes = gd_ref.shape
    wide = win_ref.shape[0]
    pad = jnp.zeros((frames, wide - lanes), jnp.float32)
    g = jnp.concatenate([gd_ref[...].astype(jnp.float32), pad], axis=1)
    band = pltpu.roll(g, 0, 1, stride=1, stride_axis=0)
    lip_ref[...] = jnp.dot(band.astype(jnp.bfloat16), win_ref[...], preferred_element_type=jnp.float32)
    band_t = band.T.astype(jnp.bfloat16)
    wsum_ref[...] = jnp.dot(band_t, ev_ref[...], preferred_element_type=jnp.float32)
    a = jnp.concatenate([at_ref[...], pad], axis=1)
    spread = pltpu.roll(a, 0, 1, stride=1, stride_axis=0)
    ginv_ref[...] = jnp.sum(spread, axis=0, keepdims=True)


def corr_bwd(gd_pad, at_pad, emb_v, win_pad):
    clips, frames, width = emb_v.shape
    wide = win_pad.shape[1]
    lanes = gd_pad.shape[2]
    return pl.pallas_call(
        _corr_bwd_kernel,
        grid=(clips,),
        in_specs=[
            pl.BlockSpec((None, frames, lanes), lambda c: (c, 0, 0)),
            pl.BlockSpec((None, frames, lanes), lambda c: (c, 0, 0)),
            pl.BlockSpec((None, frames, width), lambda c: (c, 0, 0)),
            pl.BlockSpec((None, wide, width), lambda c: (c, 0, 0)),
        ],
        out_specs=[
            pl.BlockSpec((None, frames, width), lambda c: (c, 0, 0)),
            pl.BlockSpec((None, wide, width), lambda c: (c, 0, 0)),
            pl.BlockSpec((None, 1, wide), lambda c: (c, 0, 0)),
        ],
        out_shape=[
            jax.ShapeDtypeStruct((clips, frames, width), jnp.float32),
            jax.ShapeDtypeStruct((clips, wide, width), jnp.float32),
            jax.ShapeDtypeStruct((clips, 1, wide), jnp.float32),
        ],
    )(gd_pad, at_pad, emb_v, win_pad)


logit_sharpening_divisor = 10.0
loss_scale = 1024.0
epsilon = 1e-06


def padded_2(cells, sides, width):
    for axis, dim in sides:
        count = lax.axis_size(axis)
        ends = count - 1
        head = lax.slice_in_dim(cells, 0, width, axis=dim)
        tail = lax.slice_in_dim(cells, cells.shape[dim] - width, cells.shape[dim], axis=dim)
        cells = jnp.concatenate(
            [
                lax.ppermute(tail, axis, [(i, (i + 1) % count) for i in range(ends)]),
                cells,
                lax.ppermute(head, axis, [((i + 1) % count, i) for i in range(ends)]),
            ],
            axis=dim,
        )
    return cells


def from_behind(value, axis, steps):
    count = lax.axis_size(axis)
    initial, last = (max(0, -steps), min(count, count - steps))
    return lax.ppermute(value, axis, [(source, source + steps) for source in range(initial, last)])


def silu_slope(values):
    sigma = jax.nn.sigmoid(values)
    return sigma * (1.0 + values * (1.0 - sigma))


def encoder(padded, w_conv, w_proj):
    clip_num, frame_pad, chan_num = padded.shape
    frame_num = frame_pad - 2
    columns = jnp.concatenate(
        [padded[:, 0:frame_num], padded[:, 1 : frame_num + 1], padded[:, 2 : frame_num + 2]], axis=2
    )
    before = jnp.einsum(
        "cfk,ke->cfe",
        columns,
        w_conv.reshape(3 * chan_num, w_conv.shape[2]),
        preferred_element_type=jnp.float32,
    )
    hidden = jax.nn.silu(before).astype(jnp.bfloat16)
    embedded = jnp.einsum("cfe,eg->cfg", hidden, w_proj, preferred_element_type=jnp.float32).astype(
        jnp.bfloat16
    )
    return (columns, before, hidden, embedded)


def inverse_norm(embedded):
    values = embedded.astype(jnp.float32)
    return lax.rsqrt(jnp.sum(values * values, axis=-1) + epsilon)


def spread_band(band, wide_len):
    clip_num, row_num, band_len = band.shape
    full_band = jnp.pad(band, ((0, 0), (0, 0), (0, wide_len + 1 - band_len)))
    flat_band = full_band.reshape(clip_num, row_num * (wide_len + 1))[:, : row_num * wide_len]
    return flat_band.reshape(clip_num, row_num, wide_len)


def narrow_band(matrix, band_len):
    clip_num, row_num, wide_len = matrix.shape
    flat_mat = jnp.pad(matrix.reshape(clip_num, row_num * wide_len), ((0, 0), (0, row_num)))
    return flat_mat.reshape(clip_num, row_num, wide_len + 1)[:, :, :band_len]


def flatten_rows(values):
    return values.reshape(values.shape[0] * values.shape[1], values.shape[2])


def proj_grad(hidden, grad_emb):
    return jnp.einsum("re,rf->ef", hidden, grad_emb, preferred_element_type=jnp.float32)


def conv_grad(columns, before, grad_emb, w_proj, w_conv):
    grad_hidden = jnp.einsum("rf,ef->re", grad_emb, w_proj, preferred_element_type=jnp.float32)
    grad_before = (grad_hidden * silu_slope(before)).astype(jnp.bfloat16)
    grad_conv = jnp.einsum("rk,re->ke", columns, grad_before, preferred_element_type=jnp.float32)
    return grad_conv.reshape(w_conv.shape)


def shards(
    audio_feats, lip_feats, lengths, labels, w_audio_conv, w_audio_proj, w_lip_conv, w_lip_proj
):
    clip_num, frame_num, chan_num = audio_feats.shape
    width = w_audio_proj.shape[1]
    offsets = 2 * SPAN + 1
    wide_len = frame_num + 2 * SPAN
    first_frame = lax.axis_index("tm") * frame_num
    stacked = jnp.stack([audio_feats, lip_feats])
    padded = padded_2(stacked, (("tm", 2),), 1)
    cols_a, pre_a, hid_a, emb_a = encoder(padded[0], w_audio_conv, w_audio_proj)
    cols_v, pre_v, hid_v, emb_v = encoder(padded[1], w_lip_conv, w_lip_proj)
    window = padded_2(emb_a, (("tm", 1),), SPAN)
    cols_a, pre_a, hid_a = (flatten_rows(cols_a), flatten_rows(pre_a), flatten_rows(hid_a))
    cols_v, pre_v, hid_v = (flatten_rows(cols_v), flatten_rows(pre_v), flatten_rows(hid_v))
    count_part = jnp.sum(lengths - jnp.abs(labels))
    count_block = jnp.zeros((8, 128), jnp.int32).at[0, 0].set(count_part)
    count = small_sum(count_block, ("k",), 1)[0, 0].astype(jnp.float32)
    inv_win = inverse_norm(window)
    reciprocal_visual_length = inverse_norm(emb_v)
    wide_pad = -(-wide_len // 128) * 128
    win_pad = jnp.pad(window, ((0, 0), (0, wide_pad - wide_len), (0, 0)))
    inv_pad = jnp.pad(inv_win, ((0, 0), (0, wide_pad - wide_len)))[:, None, :]
    lagged_inner_terms, reciprocal_lag_strip = corr_fwd(emb_v, win_pad, inv_pad[:, :, ::-1])
    lanes_used = lagged_inner_terms.shape[2]
    frame_ids = first_frame + jnp.arange(frame_num, dtype=jnp.int32)
    shifts = jnp.arange(lanes_used, dtype=jnp.int32) - SPAN
    positions = frame_ids[:, None] + shifts[None, :]
    inside = frame_ids[None, :] < lengths[:, None]
    valid = inside[:, :, None] & (positions[None] >= 0) & (positions[None] < lengths[:, None, None])
    valid = valid & (shifts < offsets - SPAN)[None, None, :]
    target_pos = frame_ids[None, :] + labels[:, None]
    counted = inside & (target_pos >= 0) & (target_pos < lengths[:, None])
    correct_lag_position = (shifts[None, :] == labels[:, None]).astype(jnp.float32)
    lag_similarity_logits = (
        logit_sharpening_divisor
        * lagged_inner_terms
        * reciprocal_visual_length[:, :, None]
        * reciprocal_lag_strip
    )
    exponentiated_logits = jnp.where(valid, jnp.exp(lag_similarity_logits), 0.0)
    partition_sums = jnp.where(inside, jnp.sum(exponentiated_logits, axis=2), 1.0)
    picked = jnp.sum(lag_similarity_logits * correct_lag_position[:, None, :], axis=2)
    loss_local = jnp.sum(jnp.where(counted, jnp.log(partition_sums) - picked, 0.0))
    normalized_probabilities = jnp.where(counted, loss_scale / count, 0.0)
    logit_derivative = (
        logit_sharpening_divisor
        * normalized_probabilities[:, :, None]
        * (exponentiated_logits / partition_sums[:, :, None] - correct_lag_position[:, None, :])
    )
    grad_dots = (
        logit_derivative * reciprocal_visual_length[:, :, None] * reciprocal_lag_strip
    ).astype(jnp.bfloat16)
    grad_inv_v = jnp.sum(logit_derivative * lagged_inner_terms * reciprocal_lag_strip, axis=2)
    audio_term = logit_derivative * lagged_inner_terms * reciprocal_visual_length[:, :, None]
    lip_sum, win_sum_pad, ginv_pad = corr_bwd(
        grad_dots, audio_term, emb_v, win_pad
    )
    grad_inv_win = ginv_pad[:, 0, :wide_len]
    lip_vals = emb_v.astype(jnp.float32)
    grad_lip = (
        lip_sum
        - (
            reciprocal_visual_length
            * reciprocal_visual_length
            * reciprocal_visual_length
            * grad_inv_v
        )[:, :, None]
        * lip_vals
    ).astype(jnp.bfloat16)
    win_sum = win_sum_pad[:, :wide_len]
    win_sum = win_sum - (inv_win * inv_win * inv_win * grad_inv_win)[:, :, None] * window.astype(
        jnp.float32
    )
    own_grad = win_sum[:, SPAN : SPAN + frame_num]
    from_after = from_behind(win_sum[:, :SPAN], "tm", -1)
    from_before = from_behind(win_sum[:, frame_num + SPAN :], "tm", 1)
    own_grad = own_grad.at[:, frame_num - SPAN :].add(from_after)
    own_grad = own_grad.at[:, :SPAN].add(from_before)
    grad_audio = own_grad.astype(jnp.bfloat16).reshape(clip_num * frame_num, width)
    grad_lip = grad_lip.reshape(clip_num * frame_num, width)
    grad_ap = proj_grad(hid_a, grad_audio)
    grad_vp = proj_grad(hid_v, grad_lip)
    grad_ac = conv_grad(cols_a, pre_a, grad_audio, w_audio_proj, w_audio_conv)
    grad_vc = conv_grad(cols_v, pre_v, grad_lip, w_lip_proj, w_lip_conv)
    parts = (grad_ac, grad_vc, grad_ap, grad_vp)
    lanes = grad_ap.shape[1]
    loss_block = jnp.zeros((8, 128), jnp.float32).at[0, 0].set(loss_local)
    *sums, loss_total = all_sum([g.reshape(-1, lanes) for g in parts], loss_block)
    grad_ac, grad_vc, grad_ap, grad_vp = (t.reshape(g.shape) for t, g in zip(sums, parts))
    loss_sum = loss_total[0, 0]
    return (loss_sum / count, grad_ac, grad_ap, grad_vc, grad_vp)


def solution(mesh):
    placed = (
        P("clip", "tm", None),
        P("clip", "tm", None),
        P("clip"),
        P("clip"),
        P(),
        P(),
        P(),
        P(),
    )
    return jax.shard_map(
        shards, mesh=mesh, in_specs=placed, out_specs=(P(), P(), P(), P(), P()), check_vma=False
    )
```

```python
import jax
import jax.numpy as jnp
from jax import lax
from jax.sharding import PartitionSpec as P
import functools
from jax.experimental import pallas as pl
from jax.experimental.pallas import tpu as pltpu

SPAN = 15


MESH_ID = pl.DeviceIdType.MESH


def _coords():
    ci = lax.axis_index("clip")
    ti = lax.axis_index("tm")
    return ci, ti, ci % 4, (ci // 4) % 4, ci // 16, ti % 2, ti // 2


def _levels():
    ci, ti, y, x, zh, core, zl = _coords()
    z = zh * 4 + zl

    def at_y(v):
        return (zh * 16 + x * 4 + v % 4, ti)

    def at_x(v):
        return (zh * 16 + (v % 4) * 4 + y, ti)

    def at_z(v):
        w = v % 8
        return ((w // 4) * 16 + x * 4 + y, (w % 4) * 2 + core)

    def at_c(v):
        return (ci, zl * 2 + v % 2)

    def at_h(v):
        return ((v % 2) * 16 + x * 4 + y, ti)

    def at_k(v):
        return (v % 32, ti)

    return {
        "c": (2, core, at_c, 1),
        "y": (4, y, at_y, 2),
        "x": (4, x, at_x, 2),
        "z": (8, z, at_z, 1),
        "h": (2, zh, at_h, 1),
        "k": (32, ci, at_k, 1),
    }


def _barrier(levels):
    barrier = pltpu.get_barrier_semaphore()
    peers = []
    for n, me, nbr, ndir in levels:
        peers.append(nbr(me + 1))
        if n > 2:
            peers.append(nbr(me - 1))
    for p in peers:
        pl.semaphore_signal(barrier, inc=1, device_id=p, device_id_type=MESH_ID)
    pl.semaphore_wait(barrier, len(peers))


def _small_start(n, me, nbr, s, tbuf, toff, tsend, trecv, tsem):
    at = toff + (me - s) % n
    c = pltpu.make_async_remote_copy(
        src_ref=tbuf.at[at],
        dst_ref=tbuf.at[at],
        send_sem=tsend.at[tsem],
        recv_sem=trecv.at[tsem],
        device_id=nbr(me + 1),
        device_id_type=MESH_ID,
    )
    c.start()
    return c


def _small_sum(n, tbuf, toff):
    acc = tbuf[toff]
    for k in range(1, n):
        acc = acc + tbuf[toff + k]
    return acc


def _small_kernel(names, t_ref, to_ref, tbuf, tsend, trecv):
    table = _levels()
    levels = [table[k] for k in names]
    barrier = pltpu.get_barrier_semaphore()
    peers = [nbr(me + j) for n, me, nbr, ndir in levels for j in range(1, n)]
    for p in peers:
        pl.semaphore_signal(barrier, inc=1, device_id=p, device_id_type=MESH_ID)
    pl.semaphore_wait(barrier, len(peers))
    toff = 0
    tsem = 0
    for li, (n, me, nbr, ndir) in enumerate(levels):
        tbuf[toff + me] = t_ref[...] if li == 0 else to_ref[...]
        copies = []
        for j in range(1, n):
            c = pltpu.make_async_remote_copy(
                src_ref=tbuf.at[toff + me],
                dst_ref=tbuf.at[toff + me],
                send_sem=tsend.at[tsem],
                recv_sem=trecv.at[tsem],
                device_id=nbr(me + j),
                device_id_type=MESH_ID,
            )
            c.start()
            copies.append(c)
            tsem += 1
        for c in copies:
            c.wait()
        to_ref[...] = _small_sum(n, tbuf, toff)
        toff += n


def small_sum(t, names, cid):
    table_n = {"c": 2, "y": 4, "x": 4, "z": 8, "h": 2, "k": 32}
    slots = sum(table_n[k] for k in names)
    sems = sum(table_n[k] - 1 for k in names)
    return pl.pallas_call(
        functools.partial(_small_kernel, names),
        out_shape=jax.ShapeDtypeStruct(t.shape, t.dtype),
        in_specs=[pl.BlockSpec(memory_space=pltpu.VMEM)],
        out_specs=pl.BlockSpec(memory_space=pltpu.VMEM),
        scratch_shapes=[
            pltpu.VMEM((slots,) + t.shape, t.dtype),
            pltpu.SemaphoreType.DMA((sems,)),
            pltpu.SemaphoreType.DMA((sems,)),
        ],
        compiler_params=pltpu.CompilerParams(collective_id=cid, has_side_effects=True),
    )(t)


def _rs_stage(tasks, work, rbuf, send_sem, recv_sem, slot, sem, rider=None):
    n = tasks[0][0]
    for s in range(n - 1):
        copies = []
        for tn, me, nbr, ndir, base, size, own in tasks:
            chunk = size // tn
            piece = chunk // ndir
            for d in range(ndir):
                sign = 1 if d == 0 else -1
                send_at = pl.multiple_of(base + ((me - sign * (s + 1)) % tn) * chunk + d * piece, 8)
                recv_at = pl.multiple_of(base + ((me - sign * (s + 2)) % tn) * chunk + d * piece, 8)
                src = own if s == 0 else work
                c = pltpu.make_async_remote_copy(
                    src_ref=src.at[pl.ds(send_at, piece)],
                    dst_ref=rbuf.at[pl.ds(slot, piece)],
                    send_sem=send_sem.at[sem],
                    recv_sem=recv_sem.at[sem],
                    device_id=nbr(me + sign),
                    device_id_type=MESH_ID,
                )
                c.start()
                copies.append((c, slot, recv_at, piece, own))
                slot += piece
                sem += 1
        ride = rider(s) if rider is not None else None
        for c, sl, recv_at, piece, own in copies:
            c.wait_recv()
            at = pl.ds(recv_at, piece)
            work[at] = rbuf[pl.ds(sl, piece)] + own[at]
        for c, sl, recv_at, piece, own in copies:
            c.wait_send()
        if ride is not None:
            ride.wait()
    return slot, sem


def _ag_stage(tasks, o_ref, send_sem, recv_sem, sem):
    n = tasks[0][0]
    for s in range(n - 1):
        copies = []
        for tn, me, nbr, ndir, base, size, own in tasks:
            chunk = size // tn
            piece = chunk // ndir
            for d in range(ndir):
                sign = 1 if d == 0 else -1
                at = pl.ds(pl.multiple_of(base + ((me - sign * s) % tn) * chunk + d * piece, 8), piece)
                c = pltpu.make_async_remote_copy(
                    src_ref=o_ref.at[at],
                    dst_ref=o_ref.at[at],
                    send_sem=send_sem.at[sem],
                    recv_sem=recv_sem.at[sem],
                    device_id=nbr(me + sign),
                    device_id_type=MESH_ID,
                )
                c.start()
                copies.append(c)
                sem += 1
        for c in copies:
            c.wait()
    return sem


def _pass_copy(buf, at, nbr, target, sems, idx):
    c = pltpu.make_async_remote_copy(
        src_ref=buf.at[at],
        dst_ref=buf.at[at],
        send_sem=sems[0].at[idx],
        recv_sem=sems[1].at[idx],
        device_id=nbr(target),
        device_id_type=MESH_ID,
    )
    c.start()
    return c


def _kernel(sizes, *refs):
    parts = len(sizes)
    ins, t_ref = refs[:parts], refs[parts]
    outs, to_ref = refs[parts + 1 : 2 * parts + 1], refs[2 * parts + 1]
    work, rbuf, zbuf, send_sem, recv_sem, tbuf, tsend, trecv, half_ref, hsend, hrecv, o_ref = refs[2 * parts + 2 :]
    rows = sum(sizes)
    start = 0
    for size, in_ref in zip(sizes, ins):
        work[start : start + size] = in_ref[...]
        start += size
    table = _levels()
    lc, ly, lx, lz = (table[k] for k in ("c", "y", "x", "z"))
    _barrier([lc, ly, lx, lz])
    tsems = (tsend, trecv)
    state = {"toff": 0, "tsem": 0}

    def tiny_level(level, first):
        n, me, nbr, ndir = level
        toff = state["toff"]
        tbuf[toff + me] = t_ref[...] if first else to_ref[...]

        def rider(s):
            c = _pass_copy(tbuf, toff + (me - s) % n, nbr, me + 1, tsems, state["tsem"])
            state["tsem"] += 1
            return c

        return rider

    def tiny_done(n):
        to_ref[...] = _small_sum(n, tbuf, state["toff"])
        state["toff"] += n

    slot, sem = 0, 0
    half = rows // 2
    quarter = rows // 4
    nc, core, nbc, _ = lc
    ny, yi, nby, _ = ly
    nx, xi, nbx, _ = lx
    nz, zi, nbz, _ = lz

    rider = tiny_level(lc, True)
    slot, sem = _rs_stage([(nc, core, nbc, 1, 0, rows, work)], work, rbuf, send_sem, recv_sem, slot, sem, rider)
    tiny_done(nc)
    r0 = core * half
    a1, b1 = r0, r0 + quarter
    rider = tiny_level(ly, False)
    slot, sem = _rs_stage(
        [(ny, yi, nby, 2, a1, quarter, work), (nx, xi, nbx, 2, b1, quarter, work)],
        work, rbuf, send_sem, recv_sem, slot, sem, rider,
    )
    tiny_done(ny)
    c1 = quarter // 4
    a2, b2 = a1 + yi * c1, b1 + xi * c1
    rider = tiny_level(lx, False)
    slot, sem = _rs_stage(
        [(nx, xi, nbx, 1, a2, c1, work), (ny, yi, nby, 1, b2, c1, work)],
        work, rbuf, send_sem, recv_sem, slot, sem, rider,
    )
    tiny_done(nx)
    c2 = c1 // 4
    a3, b3 = a2 + xi * c2, b2 + yi * c2
    zbuf[zi, 0] = work[pl.ds(pl.multiple_of(a3, 8), c2)]
    zbuf[zi, 1] = work[pl.ds(pl.multiple_of(b3, 8), c2)]
    toff = state["toff"]
    tbuf[toff + zi] = to_ref[...]
    right = nz // 2
    left = nz - 1 - right
    for s in range(right):
        cs = [
            _pass_copy(zbuf, (zi - s) % nz, nbz, zi + 1, (send_sem, recv_sem), sem),
            _pass_copy(tbuf, toff + (zi - s) % nz, nbz, zi + 1, tsems, state["tsem"]),
        ]
        sem += 1
        state["tsem"] += 1
        if s < left:
            cs.append(_pass_copy(zbuf, (zi + s) % nz, nbz, zi - 1, (send_sem, recv_sem), sem))
            cs.append(_pass_copy(tbuf, toff + (zi + s) % nz, nbz, zi - 1, tsems, state["tsem"]))
            sem += 1
            state["tsem"] += 1
        for c in cs:
            c.wait()
    for colour, at in ((0, a3), (1, b3)):
        acc = zbuf[0, colour]
        for k in range(1, nz):
            acc = acc + zbuf[k, colour]
        o_ref[pl.ds(pl.multiple_of(at, 8), c2)] = acc
    tiny_done(nz)
    sem = _ag_stage([(nx, xi, nbx, 1, a2, c1, None), (ny, yi, nby, 1, b2, c1, None)], o_ref, send_sem, recv_sem, sem)
    for at in (a2, b2):
        region = pl.ds(pl.multiple_of(at, 16), c1)
        half_ref[region] = o_ref[region].astype(half_ref.dtype)
    sem = _ag_stage([(ny, yi, nby, 2, a1, quarter, None), (nx, xi, nbx, 2, b1, quarter, None)], half_ref, hsend, hrecv, 0)
    _ag_stage([(nc, core, nbc, 1, 0, rows, None)], half_ref, hsend, hrecv, sem)
    start = 0
    for size, out_ref in zip(sizes, outs):
        out_ref[...] = half_ref[start : start + size].astype(out_ref.dtype)
        start += size


def _counts(rows):
    half, quarter = rows // 2, rows // 4
    c1 = quarter // 4
    slots = half + 3 * 2 * quarter // 4 + 3 * 2 * c1 // 4
    sems = 1 + 3 * 4 + 3 * 2 + 7 + 3 * 2
    return slots, sems, 2 + 4 + 4 + 8, 1 + 3 + 3 + 7


def all_sum(parts, small):
    sizes = tuple(p.shape[0] for p in parts)
    lanes = parts[0].shape[1]
    rows = sum(sizes)
    slots, sems, tslots, tsems = _counts(rows)
    c2 = rows // 64
    vmem = pl.BlockSpec(memory_space=pltpu.VMEM)
    return pl.pallas_call(
        functools.partial(_kernel, sizes),
        out_shape=tuple(jax.ShapeDtypeStruct(p.shape, p.dtype) for p in parts)
        + (jax.ShapeDtypeStruct(small.shape, small.dtype),),
        in_specs=[vmem] * (len(parts) + 1),
        out_specs=(vmem,) * (len(parts) + 1),
        scratch_shapes=[
            pltpu.VMEM((rows, lanes), jnp.float32),
            pltpu.VMEM((slots, lanes), jnp.float32),
            pltpu.VMEM((8, 2, c2, lanes), jnp.float32),
            pltpu.SemaphoreType.DMA((sems,)),
            pltpu.SemaphoreType.DMA((sems,)),
            pltpu.VMEM((tslots,) + small.shape, small.dtype),
            pltpu.SemaphoreType.DMA((tsems,)),
            pltpu.SemaphoreType.DMA((tsems,)),
            pltpu.VMEM((rows, lanes), jnp.bfloat16),
            pltpu.SemaphoreType.DMA((13,)),
            pltpu.SemaphoreType.DMA((13,)),
            pltpu.VMEM((rows, lanes), jnp.float32),
        ],
        compiler_params=pltpu.CompilerParams(
            collective_id=0, has_side_effects=True, vmem_limit_bytes=48 * 1024 * 1024
        ),
    )(*parts, small)


def _corr_fwd_kernel(ev_ref, win_ref, inv_ref, dots_ref, strip_ref):
    wide = win_ref.shape[0]
    lanes = dots_ref.shape[1]
    rows = lax.broadcasted_iota(jnp.int32, (wide, wide), 0)
    cols = lax.broadcasted_iota(jnp.int32, (wide, wide), 1)
    flip = (rows + cols == wide - 1).astype(jnp.bfloat16)
    win_rev = jnp.dot(flip, win_ref[...], preferred_element_type=jnp.float32).astype(jnp.bfloat16)
    m = lax.dot_general(
        ev_ref[...], win_rev, (((1,), (1,)), ((), ())), preferred_element_type=jnp.float32
    )
    rows = lax.broadcasted_iota(jnp.int32, (lanes, lanes), 0)
    cols = lax.broadcasted_iota(jnp.int32, (lanes, lanes), 1)
    back = (rows + cols == lanes - 1).astype(jnp.float32)

    def unflip(x):
        return jnp.dot(x, back, precision=lax.Precision.HIGHEST, preferred_element_type=jnp.float32)

    dots_ref[...] = unflip(pltpu.roll(m, 0, 1, stride=1, stride_axis=0)[:, wide - lanes :])
    inv = jnp.broadcast_to(inv_ref[...], m.shape)
    strip_ref[...] = unflip(pltpu.roll(inv, 0, 1, stride=1, stride_axis=0)[:, wide - lanes :])


def corr_fwd(emb_v, win_pad, inv_pad):
    clips, frames, width = emb_v.shape
    wide = win_pad.shape[1]
    lanes = 128
    return pl.pallas_call(
        _corr_fwd_kernel,
        grid=(clips,),
        in_specs=[
            pl.BlockSpec((None, frames, width), lambda c: (c, 0, 0)),
            pl.BlockSpec((None, wide, width), lambda c: (c, 0, 0)),
            pl.BlockSpec((None, 1, wide), lambda c: (c, 0, 0)),
        ],
        out_specs=[
            pl.BlockSpec((None, frames, lanes), lambda c: (c, 0, 0)),
            pl.BlockSpec((None, frames, lanes), lambda c: (c, 0, 0)),
        ],
        out_shape=[
            jax.ShapeDtypeStruct((clips, frames, lanes), jnp.float32),
            jax.ShapeDtypeStruct((clips, frames, lanes), jnp.float32),
        ],
    )(emb_v, win_pad, inv_pad)


def _corr_bwd_kernel(gd_ref, at_ref, ev_ref, win_ref, lip_ref, wsum_ref, ginv_ref):
    frames, lanes = gd_ref.shape
    wide = win_ref.shape[0]
    pad = jnp.zeros((frames, wide - lanes), jnp.float32)
    g = jnp.concatenate([gd_ref[...].astype(jnp.float32), pad], axis=1)
    band = pltpu.roll(g, 0, 1, stride=1, stride_axis=0)
    lip_ref[...] = jnp.dot(band.astype(jnp.bfloat16), win_ref[...], preferred_element_type=jnp.float32)
    band_t = band.T.astype(jnp.bfloat16)
    wsum_ref[...] = jnp.dot(band_t, ev_ref[...], preferred_element_type=jnp.float32)
    a = jnp.concatenate([at_ref[...], pad], axis=1)
    spread = pltpu.roll(a, 0, 1, stride=1, stride_axis=0)
    ginv_ref[...] = jnp.sum(spread, axis=0, keepdims=True)


def corr_bwd(gd_pad, at_pad, emb_v, win_pad):
    clips, frames, width = emb_v.shape
    wide = win_pad.shape[1]
    lanes = gd_pad.shape[2]
    return pl.pallas_call(
        _corr_bwd_kernel,
        grid=(clips,),
        in_specs=[
            pl.BlockSpec((None, frames, lanes), lambda c: (c, 0, 0)),
            pl.BlockSpec((None, frames, lanes), lambda c: (c, 0, 0)),
            pl.BlockSpec((None, frames, width), lambda c: (c, 0, 0)),
            pl.BlockSpec((None, wide, width), lambda c: (c, 0, 0)),
        ],
        out_specs=[
            pl.BlockSpec((None, frames, width), lambda c: (c, 0, 0)),
            pl.BlockSpec((None, wide, width), lambda c: (c, 0, 0)),
            pl.BlockSpec((None, 1, wide), lambda c: (c, 0, 0)),
        ],
        out_shape=[
            jax.ShapeDtypeStruct((clips, frames, width), jnp.float32),
            jax.ShapeDtypeStruct((clips, wide, width), jnp.float32),
            jax.ShapeDtypeStruct((clips, 1, wide), jnp.float32),
        ],
    )(gd_pad, at_pad, emb_v, win_pad)


logit_sharpening_divisor = 10.0
loss_scale = 1024.0
epsilon = 1e-06


def padded_2(cells, sides, width):
    for axis, dim in sides:
        count = lax.axis_size(axis)
        ends = count - 1
        head = lax.slice_in_dim(cells, 0, width, axis=dim)
        tail = lax.slice_in_dim(cells, cells.shape[dim] - width, cells.shape[dim], axis=dim)
        cells = jnp.concatenate(
            [
                lax.ppermute(tail, axis, [(i, (i + 1) % count) for i in range(ends)]),
                cells,
                lax.ppermute(head, axis, [((i + 1) % count, i) for i in range(ends)]),
            ],
            axis=dim,
        )
    return cells


def from_behind(value, axis, steps):
    count = lax.axis_size(axis)
    initial, last = (max(0, -steps), min(count, count - steps))
    return lax.ppermute(value, axis, [(source, source + steps) for source in range(initial, last)])


def silu_slope(values):
    sigma = jax.nn.sigmoid(values)
    return sigma * (1.0 + values * (1.0 - sigma))


def encoder(padded, w_conv, w_proj):
    clip_num, frame_pad, chan_num = padded.shape
    frame_num = frame_pad - 2
    columns = jnp.concatenate(
        [padded[:, 0:frame_num], padded[:, 1 : frame_num + 1], padded[:, 2 : frame_num + 2]], axis=2
    )
    before = jnp.einsum(
        "cfk,ke->cfe",
        columns,
        w_conv.reshape(3 * chan_num, w_conv.shape[2]),
        preferred_element_type=jnp.float32,
    )
    hidden = jax.nn.silu(before).astype(jnp.bfloat16)
    embedded = jnp.einsum("cfe,eg->cfg", hidden, w_proj, preferred_element_type=jnp.float32).astype(
        jnp.bfloat16
    )
    return (columns, before, hidden, embedded)


def inverse_norm(embedded):
    values = embedded.astype(jnp.float32)
    return lax.rsqrt(jnp.sum(values * values, axis=-1) + epsilon)


def spread_band(band, wide_len):
    clip_num, row_num, band_len = band.shape
    full_band = jnp.pad(band, ((0, 0), (0, 0), (0, wide_len + 1 - band_len)))
    flat_band = full_band.reshape(clip_num, row_num * (wide_len + 1))[:, : row_num * wide_len]
    return flat_band.reshape(clip_num, row_num, wide_len)


def narrow_band(matrix, band_len):
    clip_num, row_num, wide_len = matrix.shape
    flat_mat = jnp.pad(matrix.reshape(clip_num, row_num * wide_len), ((0, 0), (0, row_num)))
    return flat_mat.reshape(clip_num, row_num, wide_len + 1)[:, :, :band_len]


def flatten_rows(values):
    return values.reshape(values.shape[0] * values.shape[1], values.shape[2])


def proj_grad(hidden, grad_emb):
    return jnp.einsum("re,rf->ef", hidden, grad_emb, preferred_element_type=jnp.float32)


def conv_grad(columns, before, grad_emb, w_proj, w_conv):
    grad_hidden = jnp.einsum("rf,ef->re", grad_emb, w_proj, preferred_element_type=jnp.float32)
    grad_before = (grad_hidden * silu_slope(before)).astype(jnp.bfloat16)
    grad_conv = jnp.einsum("rk,re->ke", columns, grad_before, preferred_element_type=jnp.float32)
    return grad_conv.reshape(w_conv.shape)


def shards(
    audio_feats, lip_feats, lengths, labels, w_audio_conv, w_audio_proj, w_lip_conv, w_lip_proj
):
    clip_num, frame_num, chan_num = audio_feats.shape
    width = w_audio_proj.shape[1]
    offsets = 2 * SPAN + 1
    wide_len = frame_num + 2 * SPAN
    first_frame = lax.axis_index("tm") * frame_num
    stacked = jnp.stack([audio_feats, lip_feats])
    padded = padded_2(stacked, (("tm", 2),), 1)
    cols_a, pre_a, hid_a, emb_a = encoder(padded[0], w_audio_conv, w_audio_proj)
    cols_v, pre_v, hid_v, emb_v = encoder(padded[1], w_lip_conv, w_lip_proj)
    window = padded_2(emb_a, (("tm", 1),), SPAN)
    cols_a, pre_a, hid_a = (flatten_rows(cols_a), flatten_rows(pre_a), flatten_rows(hid_a))
    cols_v, pre_v, hid_v = (flatten_rows(cols_v), flatten_rows(pre_v), flatten_rows(hid_v))
    count_part = jnp.sum(lengths - jnp.abs(labels))
    count_block = jnp.zeros((8, 128), jnp.int32).at[0, 0].set(count_part)
    count = small_sum(count_block, ("k",), 1)[0, 0].astype(jnp.float32)
    inv_win = inverse_norm(window)
    reciprocal_visual_length = inverse_norm(emb_v)
    wide_pad = -(-wide_len // 128) * 128
    win_pad = jnp.pad(window, ((0, 0), (0, wide_pad - wide_len), (0, 0)))
    inv_pad = jnp.pad(inv_win, ((0, 0), (0, wide_pad - wide_len)))[:, None, :]
    lagged_inner_terms, reciprocal_lag_strip = corr_fwd(emb_v, win_pad, inv_pad[:, :, ::-1])
    lanes_used = lagged_inner_terms.shape[2]
    frame_ids = first_frame + jnp.arange(frame_num, dtype=jnp.int32)
    shifts = jnp.arange(lanes_used, dtype=jnp.int32) - SPAN
    positions = frame_ids[:, None] + shifts[None, :]
    inside = frame_ids[None, :] < lengths[:, None]
    valid = inside[:, :, None] & (positions[None] >= 0) & (positions[None] < lengths[:, None, None])
    valid = valid & (shifts < offsets - SPAN)[None, None, :]
    target_pos = frame_ids[None, :] + labels[:, None]
    counted = inside & (target_pos >= 0) & (target_pos < lengths[:, None])
    correct_lag_position = (shifts[None, :] == labels[:, None]).astype(jnp.float32)
    lag_similarity_logits = (
        logit_sharpening_divisor
        * lagged_inner_terms
        * reciprocal_visual_length[:, :, None]
        * reciprocal_lag_strip
    )
    exponentiated_logits = jnp.where(valid, jnp.exp(lag_similarity_logits), 0.0)
    partition_sums = jnp.where(inside, jnp.sum(exponentiated_logits, axis=2), 1.0)
    picked = jnp.sum(lag_similarity_logits * correct_lag_position[:, None, :], axis=2)
    loss_local = jnp.sum(jnp.where(counted, jnp.log(partition_sums) - picked, 0.0))
    normalized_probabilities = jnp.where(counted, loss_scale / count, 0.0)
    logit_derivative = (
        logit_sharpening_divisor
        * normalized_probabilities[:, :, None]
        * (exponentiated_logits / partition_sums[:, :, None] - correct_lag_position[:, None, :])
    )
    grad_dots = (
        logit_derivative * reciprocal_visual_length[:, :, None] * reciprocal_lag_strip
    ).astype(jnp.bfloat16)
    grad_inv_v = jnp.sum(logit_derivative * lagged_inner_terms * reciprocal_lag_strip, axis=2)
    audio_term = logit_derivative * lagged_inner_terms * reciprocal_visual_length[:, :, None]
    lip_sum, win_sum_pad, ginv_pad = corr_bwd(
        grad_dots, audio_term, emb_v, win_pad
    )
    grad_inv_win = ginv_pad[:, 0, :wide_len]
    lip_vals = emb_v.astype(jnp.float32)
    grad_lip = (
        lip_sum
        - (
            reciprocal_visual_length
            * reciprocal_visual_length
            * reciprocal_visual_length
            * grad_inv_v
        )[:, :, None]
        * lip_vals
    ).astype(jnp.bfloat16)
    win_sum = win_sum_pad[:, :wide_len]
    win_sum = win_sum - (inv_win * inv_win * inv_win * grad_inv_win)[:, :, None] * window.astype(
        jnp.float32
    )
    own_grad = win_sum[:, SPAN : SPAN + frame_num]
    from_after = from_behind(win_sum[:, :SPAN], "tm", -1)
    from_before = from_behind(win_sum[:, frame_num + SPAN :], "tm", 1)
    body = frame_num - SPAN
    own_grad = (
        own_grad
        + jnp.pad(from_after, ((0, 0), (body, 0), (0, 0)))
        + jnp.pad(from_before, ((0, 0), (0, body), (0, 0)))
    )
    grad_audio = own_grad.astype(jnp.bfloat16).reshape(clip_num * frame_num, width)
    grad_lip = grad_lip.reshape(clip_num * frame_num, width)
    grad_ap = proj_grad(hid_a, grad_audio)
    grad_vp = proj_grad(hid_v, grad_lip)
    grad_ac = conv_grad(cols_a, pre_a, grad_audio, w_audio_proj, w_audio_conv)
    grad_vc = conv_grad(cols_v, pre_v, grad_lip, w_lip_proj, w_lip_conv)
    parts = (grad_ac, grad_vc, grad_ap, grad_vp)
    lanes = grad_ap.shape[1]
    loss_block = jnp.zeros((8, 128), jnp.float32).at[0, 0].set(loss_local)
    *sums, loss_total = all_sum([g.reshape(-1, lanes) for g in parts], loss_block)
    grad_ac, grad_vc, grad_ap, grad_vp = (t.reshape(g.shape) for t, g in zip(sums, parts))
    loss_sum = loss_total[0, 0]
    return (loss_sum / count, grad_ac, grad_ap, grad_vc, grad_vp)


def solution(mesh):
    placed = (
        P("clip", "tm", None),
        P("clip", "tm", None),
        P("clip"),
        P("clip"),
        P(),
        P(),
        P(),
        P(),
    )
    return jax.shard_map(
        shards, mesh=mesh, in_specs=placed, out_specs=(P(), P(), P(), P(), P()), check_vma=False
    )
```

```python
import jax
import jax.numpy as jnp
from jax import lax
from jax.sharding import PartitionSpec as P
import functools
from jax.experimental import pallas as pl
from jax.experimental.pallas import tpu as pltpu

SPAN = 15


MESH_ID = pl.DeviceIdType.MESH


def _coords():
    ci = lax.axis_index("clip")
    ti = lax.axis_index("tm")
    return ci, ti, ci % 4, (ci // 4) % 4, ci // 16, ti % 2, ti // 2


def _levels():
    ci, ti, y, x, zh, core, zl = _coords()
    z = zh * 4 + zl

    def at_y(v):
        return (zh * 16 + x * 4 + v % 4, ti)

    def at_x(v):
        return (zh * 16 + (v % 4) * 4 + y, ti)

    def at_z(v):
        w = v % 8
        return ((w // 4) * 16 + x * 4 + y, (w % 4) * 2 + core)

    def at_c(v):
        return (ci, zl * 2 + v % 2)

    def at_h(v):
        return ((v % 2) * 16 + x * 4 + y, ti)

    def at_k(v):
        return (v % 32, ti)

    return {
        "c": (2, core, at_c, 1),
        "y": (4, y, at_y, 2),
        "x": (4, x, at_x, 2),
        "z": (8, z, at_z, 1),
        "h": (2, zh, at_h, 1),
        "k": (32, ci, at_k, 1),
    }


def _barrier(levels):
    barrier = pltpu.get_barrier_semaphore()
    peers = []
    for n, me, nbr, ndir in levels:
        peers.append(nbr(me + 1))
        if n > 2:
            peers.append(nbr(me - 1))
    for p in peers:
        pl.semaphore_signal(barrier, inc=1, device_id=p, device_id_type=MESH_ID)
    pl.semaphore_wait(barrier, len(peers))


def _small_start(n, me, nbr, s, tbuf, toff, tsend, trecv, tsem):
    at = toff + (me - s) % n
    c = pltpu.make_async_remote_copy(
        src_ref=tbuf.at[at],
        dst_ref=tbuf.at[at],
        send_sem=tsend.at[tsem],
        recv_sem=trecv.at[tsem],
        device_id=nbr(me + 1),
        device_id_type=MESH_ID,
    )
    c.start()
    return c


def _small_sum(n, tbuf, toff):
    acc = tbuf[toff]
    for k in range(1, n):
        acc = acc + tbuf[toff + k]
    return acc


def _small_kernel(names, t_ref, to_ref, tbuf, tsend, trecv):
    table = _levels()
    levels = [table[k] for k in names]
    barrier = pltpu.get_barrier_semaphore()
    peers = [nbr(me + j) for n, me, nbr, ndir in levels for j in range(1, n)]
    for p in peers:
        pl.semaphore_signal(barrier, inc=1, device_id=p, device_id_type=MESH_ID)
    pl.semaphore_wait(barrier, len(peers))
    toff = 0
    tsem = 0
    for li, (n, me, nbr, ndir) in enumerate(levels):
        tbuf[toff + me] = t_ref[...] if li == 0 else to_ref[...]
        copies = []
        for j in range(1, n):
            c = pltpu.make_async_remote_copy(
                src_ref=tbuf.at[toff + me],
                dst_ref=tbuf.at[toff + me],
                send_sem=tsend.at[tsem],
                recv_sem=trecv.at[tsem],
                device_id=nbr(me + j),
                device_id_type=MESH_ID,
            )
            c.start()
            copies.append(c)
            tsem += 1
        for c in copies:
            c.wait()
        to_ref[...] = _small_sum(n, tbuf, toff)
        toff += n


def small_sum(t, names, cid):
    table_n = {"c": 2, "y": 4, "x": 4, "z": 8, "h": 2, "k": 32}
    slots = sum(table_n[k] for k in names)
    sems = sum(table_n[k] - 1 for k in names)
    return pl.pallas_call(
        functools.partial(_small_kernel, names),
        out_shape=jax.ShapeDtypeStruct(t.shape, t.dtype),
        in_specs=[pl.BlockSpec(memory_space=pltpu.VMEM)],
        out_specs=pl.BlockSpec(memory_space=pltpu.VMEM),
        scratch_shapes=[
            pltpu.VMEM((slots,) + t.shape, t.dtype),
            pltpu.SemaphoreType.DMA((sems,)),
            pltpu.SemaphoreType.DMA((sems,)),
        ],
        compiler_params=pltpu.CompilerParams(collective_id=cid, has_side_effects=True),
    )(t)


def _rs_stage(tasks, work, rbuf, send_sem, recv_sem, slot, sem, rider=None):
    n = tasks[0][0]
    for s in range(n - 1):
        copies = []
        for tn, me, nbr, ndir, base, size, own in tasks:
            chunk = size // tn
            piece = chunk // ndir
            for d in range(ndir):
                sign = 1 if d == 0 else -1
                send_at = pl.multiple_of(base + ((me - sign * (s + 1)) % tn) * chunk + d * piece, 8)
                recv_at = pl.multiple_of(base + ((me - sign * (s + 2)) % tn) * chunk + d * piece, 8)
                src = own if s == 0 else work
                c = pltpu.make_async_remote_copy(
                    src_ref=src.at[pl.ds(send_at, piece)],
                    dst_ref=rbuf.at[pl.ds(slot, piece)],
                    send_sem=send_sem.at[sem],
                    recv_sem=recv_sem.at[sem],
                    device_id=nbr(me + sign),
                    device_id_type=MESH_ID,
                )
                c.start()
                copies.append((c, slot, recv_at, piece, own))
                slot += piece
                sem += 1
        ride = rider(s) if rider is not None else None
        for c, sl, recv_at, piece, own in copies:
            c.wait_recv()
            at = pl.ds(recv_at, piece)
            work[at] = rbuf[pl.ds(sl, piece)] + own[at]
        for c, sl, recv_at, piece, own in copies:
            c.wait_send()
        if ride is not None:
            ride.wait()
    return slot, sem


def _ag_stage(tasks, o_ref, send_sem, recv_sem, sem):
    n = tasks[0][0]
    for s in range(n - 1):
        copies = []
        for tn, me, nbr, ndir, base, size, own in tasks:
            chunk = size // tn
            piece = chunk // ndir
            for d in range(ndir):
                sign = 1 if d == 0 else -1
                at = pl.ds(pl.multiple_of(base + ((me - sign * s) % tn) * chunk + d * piece, 8), piece)
                c = pltpu.make_async_remote_copy(
                    src_ref=o_ref.at[at],
                    dst_ref=o_ref.at[at],
                    send_sem=send_sem.at[sem],
                    recv_sem=recv_sem.at[sem],
                    device_id=nbr(me + sign),
                    device_id_type=MESH_ID,
                )
                c.start()
                copies.append(c)
                sem += 1
        for c in copies:
            c.wait()
    return sem


def _pass_copy(buf, at, nbr, target, sems, idx):
    c = pltpu.make_async_remote_copy(
        src_ref=buf.at[at],
        dst_ref=buf.at[at],
        send_sem=sems[0].at[idx],
        recv_sem=sems[1].at[idx],
        device_id=nbr(target),
        device_id_type=MESH_ID,
    )
    c.start()
    return c


def _kernel(sizes, *refs):
    parts = len(sizes)
    ins, t_ref = refs[:parts], refs[parts]
    outs, to_ref = refs[parts + 1 : 2 * parts + 1], refs[2 * parts + 1]
    work, rbuf, zbuf, send_sem, recv_sem, tbuf, tsend, trecv, half_ref, hsend, hrecv, o_ref = refs[2 * parts + 2 :]
    rows = sum(sizes)
    start = 0
    for size, in_ref in zip(sizes, ins):
        work[start : start + size] = in_ref[...]
        start += size
    table = _levels()
    lc, ly, lx, lz = (table[k] for k in ("c", "y", "x", "z"))
    _barrier([lc, ly, lx, lz])
    tsems = (tsend, trecv)
    state = {"toff": 0, "tsem": 0}

    def tiny_level(level, first):
        n, me, nbr, ndir = level
        toff = state["toff"]
        tbuf[toff + me] = t_ref[...] if first else to_ref[...]

        def rider(s):
            c = _pass_copy(tbuf, toff + (me - s) % n, nbr, me + 1, tsems, state["tsem"])
            state["tsem"] += 1
            return c

        return rider

    def tiny_done(n):
        to_ref[...] = _small_sum(n, tbuf, state["toff"])
        state["toff"] += n

    slot, sem = 0, 0
    half = rows // 2
    quarter = rows // 4
    nc, core, nbc, _ = lc
    ny, yi, nby, _ = ly
    nx, xi, nbx, _ = lx
    nz, zi, nbz, _ = lz

    rider = tiny_level(lc, True)
    slot, sem = _rs_stage([(nc, core, nbc, 1, 0, rows, work)], work, rbuf, send_sem, recv_sem, slot, sem, rider)
    tiny_done(nc)
    r0 = core * half
    a1, b1 = r0, r0 + quarter
    rider = tiny_level(ly, False)
    slot, sem = _rs_stage(
        [(ny, yi, nby, 2, a1, quarter, work), (nx, xi, nbx, 2, b1, quarter, work)],
        work, rbuf, send_sem, recv_sem, slot, sem, rider,
    )
    tiny_done(ny)
    c1 = quarter // 4
    a2, b2 = a1 + yi * c1, b1 + xi * c1
    rider = tiny_level(lx, False)
    slot, sem = _rs_stage(
        [(nx, xi, nbx, 1, a2, c1, work), (ny, yi, nby, 1, b2, c1, work)],
        work, rbuf, send_sem, recv_sem, slot, sem, rider,
    )
    tiny_done(nx)
    c2 = c1 // 4
    a3, b3 = a2 + xi * c2, b2 + yi * c2
    zbuf[zi, 0] = work[pl.ds(pl.multiple_of(a3, 8), c2)]
    zbuf[zi, 1] = work[pl.ds(pl.multiple_of(b3, 8), c2)]
    toff = state["toff"]
    tbuf[toff + zi] = to_ref[...]
    right = nz // 2
    left = nz - 1 - right
    for s in range(right):
        cs = [
            _pass_copy(zbuf, (zi - s) % nz, nbz, zi + 1, (send_sem, recv_sem), sem),
            _pass_copy(tbuf, toff + (zi - s) % nz, nbz, zi + 1, tsems, state["tsem"]),
        ]
        sem += 1
        state["tsem"] += 1
        if s < left:
            cs.append(_pass_copy(zbuf, (zi + s) % nz, nbz, zi - 1, (send_sem, recv_sem), sem))
            cs.append(_pass_copy(tbuf, toff + (zi + s) % nz, nbz, zi - 1, tsems, state["tsem"]))
            sem += 1
            state["tsem"] += 1
        for c in cs:
            c.wait()
    for colour, at in ((0, a3), (1, b3)):
        acc = zbuf[0, colour]
        for k in range(1, nz):
            acc = acc + zbuf[k, colour]
        o_ref[pl.ds(pl.multiple_of(at, 8), c2)] = acc
    tiny_done(nz)
    sem = _ag_stage([(nx, xi, nbx, 1, a2, c1, None), (ny, yi, nby, 1, b2, c1, None)], o_ref, send_sem, recv_sem, sem)
    for at in (a2, b2):
        region = pl.ds(pl.multiple_of(at, 16), c1)
        half_ref[region] = o_ref[region].astype(half_ref.dtype)
    sem = _ag_stage([(ny, yi, nby, 2, a1, quarter, None), (nx, xi, nbx, 2, b1, quarter, None)], half_ref, hsend, hrecv, 0)
    _ag_stage([(nc, core, nbc, 1, 0, rows, None)], half_ref, hsend, hrecv, sem)
    start = 0
    for size, out_ref in zip(sizes, outs):
        out_ref[...] = half_ref[start : start + size].astype(out_ref.dtype)
        start += size


def _counts(rows):
    half, quarter = rows // 2, rows // 4
    c1 = quarter // 4
    slots = half + 3 * 2 * quarter // 4 + 3 * 2 * c1 // 4
    sems = 1 + 3 * 4 + 3 * 2 + 7 + 3 * 2
    return slots, sems, 2 + 4 + 4 + 8, 1 + 3 + 3 + 7


def all_sum(parts, small):
    sizes = tuple(p.shape[0] for p in parts)
    lanes = parts[0].shape[1]
    rows = sum(sizes)
    slots, sems, tslots, tsems = _counts(rows)
    c2 = rows // 64
    vmem = pl.BlockSpec(memory_space=pltpu.VMEM)
    return pl.pallas_call(
        functools.partial(_kernel, sizes),
        out_shape=tuple(jax.ShapeDtypeStruct(p.shape, p.dtype) for p in parts)
        + (jax.ShapeDtypeStruct(small.shape, small.dtype),),
        in_specs=[vmem] * (len(parts) + 1),
        out_specs=(vmem,) * (len(parts) + 1),
        scratch_shapes=[
            pltpu.VMEM((rows, lanes), jnp.float32),
            pltpu.VMEM((slots, lanes), jnp.float32),
            pltpu.VMEM((8, 2, c2, lanes), jnp.float32),
            pltpu.SemaphoreType.DMA((sems,)),
            pltpu.SemaphoreType.DMA((sems,)),
            pltpu.VMEM((tslots,) + small.shape, small.dtype),
            pltpu.SemaphoreType.DMA((tsems,)),
            pltpu.SemaphoreType.DMA((tsems,)),
            pltpu.VMEM((rows, lanes), jnp.bfloat16),
            pltpu.SemaphoreType.DMA((13,)),
            pltpu.SemaphoreType.DMA((13,)),
            pltpu.VMEM((rows, lanes), jnp.float32),
        ],
        compiler_params=pltpu.CompilerParams(
            collective_id=0, has_side_effects=True, vmem_limit_bytes=48 * 1024 * 1024
        ),
    )(*parts, small)


def _corr_fwd_kernel(ev_ref, win_ref, inv_ref, dots_ref, strip_ref):
    wide = win_ref.shape[0]
    lanes = dots_ref.shape[1]
    rows = lax.broadcasted_iota(jnp.int32, (wide, wide), 0)
    cols = lax.broadcasted_iota(jnp.int32, (wide, wide), 1)
    flip = (rows + cols == wide - 1).astype(jnp.bfloat16)
    win_rev = jnp.dot(flip, win_ref[...], preferred_element_type=jnp.float32).astype(jnp.bfloat16)
    m = lax.dot_general(
        ev_ref[...], win_rev, (((1,), (1,)), ((), ())), preferred_element_type=jnp.float32
    )
    rows = lax.broadcasted_iota(jnp.int32, (lanes, lanes), 0)
    cols = lax.broadcasted_iota(jnp.int32, (lanes, lanes), 1)
    back = (rows + cols == lanes - 1).astype(jnp.float32)

    def unflip(x):
        return jnp.dot(x, back, precision=lax.Precision.HIGHEST, preferred_element_type=jnp.float32)

    dots_ref[...] = unflip(pltpu.roll(m, 0, 1, stride=1, stride_axis=0)[:, wide - lanes :])
    inv = jnp.broadcast_to(inv_ref[...], m.shape)
    strip_ref[...] = unflip(pltpu.roll(inv, 0, 1, stride=1, stride_axis=0)[:, wide - lanes :])


def corr_fwd(emb_v, win_pad, inv_pad):
    clips, frames, width = emb_v.shape
    wide = win_pad.shape[1]
    lanes = 128
    return pl.pallas_call(
        _corr_fwd_kernel,
        grid=(clips,),
        in_specs=[
            pl.BlockSpec((None, frames, width), lambda c: (c, 0, 0)),
            pl.BlockSpec((None, wide, width), lambda c: (c, 0, 0)),
            pl.BlockSpec((None, 1, wide), lambda c: (c, 0, 0)),
        ],
        out_specs=[
            pl.BlockSpec((None, frames, lanes), lambda c: (c, 0, 0)),
            pl.BlockSpec((None, frames, lanes), lambda c: (c, 0, 0)),
        ],
        out_shape=[
            jax.ShapeDtypeStruct((clips, frames, lanes), jnp.float32),
            jax.ShapeDtypeStruct((clips, frames, lanes), jnp.float32),
        ],
    )(emb_v, win_pad, inv_pad)


def _corr_bwd_kernel(gd_ref, at_ref, ev_ref, win_ref, lip_ref, wsum_ref, ginv_ref):
    frames, lanes = gd_ref.shape
    wide = win_ref.shape[0]
    pad = jnp.zeros((frames, wide - lanes), jnp.float32)
    g = jnp.concatenate([gd_ref[...].astype(jnp.float32), pad], axis=1)
    band = pltpu.roll(g, 0, 1, stride=1, stride_axis=0)
    lip_ref[...] = jnp.dot(band.astype(jnp.bfloat16), win_ref[...], preferred_element_type=jnp.float32)
    band_t = band.T.astype(jnp.bfloat16)
    wsum_ref[...] = jnp.dot(band_t, ev_ref[...], preferred_element_type=jnp.float32)
    a = jnp.concatenate([at_ref[...], pad], axis=1)
    spread = pltpu.roll(a, 0, 1, stride=1, stride_axis=0)
    ginv_ref[...] = jnp.sum(spread, axis=0, keepdims=True)


def corr_bwd(gd_pad, at_pad, emb_v, win_pad):
    clips, frames, width = emb_v.shape
    wide = win_pad.shape[1]
    lanes = gd_pad.shape[2]
    return pl.pallas_call(
        _corr_bwd_kernel,
        grid=(clips,),
        in_specs=[
            pl.BlockSpec((None, frames, lanes), lambda c: (c, 0, 0)),
            pl.BlockSpec((None, frames, lanes), lambda c: (c, 0, 0)),
            pl.BlockSpec((None, frames, width), lambda c: (c, 0, 0)),
            pl.BlockSpec((None, wide, width), lambda c: (c, 0, 0)),
        ],
        out_specs=[
            pl.BlockSpec((None, frames, width), lambda c: (c, 0, 0)),
            pl.BlockSpec((None, wide, width), lambda c: (c, 0, 0)),
            pl.BlockSpec((None, 1, wide), lambda c: (c, 0, 0)),
        ],
        out_shape=[
            jax.ShapeDtypeStruct((clips, frames, width), jnp.float32),
            jax.ShapeDtypeStruct((clips, wide, width), jnp.float32),
            jax.ShapeDtypeStruct((clips, 1, wide), jnp.float32),
        ],
    )(gd_pad, at_pad, emb_v, win_pad)


logit_sharpening_divisor = 10.0
loss_scale = 1024.0
epsilon = 1e-06


def padded_2(cells, sides, width):
    for axis, dim in sides:
        count = lax.axis_size(axis)
        ends = count - 1
        head = lax.slice_in_dim(cells, 0, width, axis=dim)
        tail = lax.slice_in_dim(cells, cells.shape[dim] - width, cells.shape[dim], axis=dim)
        cells = jnp.concatenate(
            [
                lax.ppermute(tail, axis, [(i, (i + 1) % count) for i in range(ends)]),
                cells,
                lax.ppermute(head, axis, [((i + 1) % count, i) for i in range(ends)]),
            ],
            axis=dim,
        )
    return cells


def from_behind(value, axis, steps):
    count = lax.axis_size(axis)
    initial, last = (max(0, -steps), min(count, count - steps))
    return lax.ppermute(value, axis, [(source, source + steps) for source in range(initial, last)])


def silu_slope(values):
    sigma = jax.nn.sigmoid(values)
    return sigma * (1.0 + values * (1.0 - sigma))


def encoder(padded, w_conv, w_proj):
    clip_num, frame_pad, chan_num = padded.shape
    frame_num = frame_pad - 2
    columns = jnp.concatenate(
        [padded[:, 0:frame_num], padded[:, 1 : frame_num + 1], padded[:, 2 : frame_num + 2]], axis=2
    )
    before = jnp.einsum(
        "cfk,ke->cfe",
        columns,
        w_conv.reshape(3 * chan_num, w_conv.shape[2]),
        preferred_element_type=jnp.float32,
    )
    hidden = jax.nn.silu(before).astype(jnp.bfloat16)
    embedded = jnp.einsum("cfe,eg->cfg", hidden, w_proj, preferred_element_type=jnp.float32).astype(
        jnp.bfloat16
    )
    return (columns, before, hidden, embedded)


def inverse_norm(embedded):
    values = embedded.astype(jnp.float32)
    return lax.rsqrt(jnp.sum(values * values, axis=-1) + epsilon)


def spread_band(band, wide_len):
    clip_num, row_num, band_len = band.shape
    full_band = jnp.pad(band, ((0, 0), (0, 0), (0, wide_len + 1 - band_len)))
    flat_band = full_band.reshape(clip_num, row_num * (wide_len + 1))[:, : row_num * wide_len]
    return flat_band.reshape(clip_num, row_num, wide_len)


def narrow_band(matrix, band_len):
    clip_num, row_num, wide_len = matrix.shape
    flat_mat = jnp.pad(matrix.reshape(clip_num, row_num * wide_len), ((0, 0), (0, row_num)))
    return flat_mat.reshape(clip_num, row_num, wide_len + 1)[:, :, :band_len]


def flatten_rows(values):
    return values.reshape(values.shape[0] * values.shape[1], values.shape[2])


def proj_grad(hidden, grad_emb):
    return jnp.einsum("re,rf->ef", hidden, grad_emb, preferred_element_type=jnp.float32)


def conv_grad(columns, before, grad_emb, w_proj, w_conv):
    grad_hidden = jnp.einsum("rf,ef->re", grad_emb, w_proj, preferred_element_type=jnp.float32)
    grad_before = (grad_hidden * silu_slope(before)).astype(jnp.bfloat16)
    grad_conv = jnp.einsum("rk,re->ke", columns, grad_before, preferred_element_type=jnp.float32)
    return grad_conv.reshape(w_conv.shape)


def shards(
    audio_feats, lip_feats, lengths, labels, w_audio_conv, w_audio_proj, w_lip_conv, w_lip_proj
):
    clip_num, frame_num, chan_num = audio_feats.shape
    width = w_audio_proj.shape[1]
    offsets = 2 * SPAN + 1
    wide_len = frame_num + 2 * SPAN
    first_frame = lax.axis_index("tm") * frame_num
    stacked = jnp.stack([audio_feats, lip_feats])
    padded = padded_2(stacked, (("tm", 2),), 1)
    cols_a, pre_a, hid_a, emb_a = encoder(padded[0], w_audio_conv, w_audio_proj)
    cols_v, pre_v, hid_v, emb_v = encoder(padded[1], w_lip_conv, w_lip_proj)
    window = padded_2(emb_a, (("tm", 1),), SPAN)
    cols_a, pre_a, hid_a = (flatten_rows(cols_a), flatten_rows(pre_a), flatten_rows(hid_a))
    cols_v, pre_v, hid_v = (flatten_rows(cols_v), flatten_rows(pre_v), flatten_rows(hid_v))
    count_part = jnp.sum(lengths - jnp.abs(labels))
    corner = (lax.broadcasted_iota(jnp.int32, (8, 128), 0) + lax.broadcasted_iota(jnp.int32, (8, 128), 1)) == 0
    count_block = jnp.where(corner, count_part, 0)
    count = small_sum(count_block, ("k",), 1)[0, 0].astype(jnp.float32)
    inv_win = inverse_norm(window)
    reciprocal_visual_length = inverse_norm(emb_v)
    wide_pad = -(-wide_len // 128) * 128
    win_pad = jnp.pad(window, ((0, 0), (0, wide_pad - wide_len), (0, 0)))
    inv_pad = jnp.pad(inv_win, ((0, 0), (0, wide_pad - wide_len)))[:, None, :]
    lagged_inner_terms, reciprocal_lag_strip = corr_fwd(emb_v, win_pad, inv_pad[:, :, ::-1])
    lanes_used = lagged_inner_terms.shape[2]
    frame_ids = first_frame + jnp.arange(frame_num, dtype=jnp.int32)
    shifts = jnp.arange(lanes_used, dtype=jnp.int32) - SPAN
    positions = frame_ids[:, None] + shifts[None, :]
    inside = frame_ids[None, :] < lengths[:, None]
    valid = inside[:, :, None] & (positions[None] >= 0) & (positions[None] < lengths[:, None, None])
    valid = valid & (shifts < offsets - SPAN)[None, None, :]
    target_pos = frame_ids[None, :] + labels[:, None]
    counted = inside & (target_pos >= 0) & (target_pos < lengths[:, None])
    correct_lag_position = (shifts[None, :] == labels[:, None]).astype(jnp.float32)
    lag_similarity_logits = (
        logit_sharpening_divisor
        * lagged_inner_terms
        * reciprocal_visual_length[:, :, None]
        * reciprocal_lag_strip
    )
    exponentiated_logits = jnp.where(valid, jnp.exp(lag_similarity_logits), 0.0)
    partition_sums = jnp.where(inside, jnp.sum(exponentiated_logits, axis=2), 1.0)
    picked = jnp.sum(lag_similarity_logits * correct_lag_position[:, None, :], axis=2)
    loss_local = jnp.sum(jnp.where(counted, jnp.log(partition_sums) - picked, 0.0))
    normalized_probabilities = jnp.where(counted, loss_scale / count, 0.0)
    logit_derivative = (
        logit_sharpening_divisor
        * normalized_probabilities[:, :, None]
        * (exponentiated_logits / partition_sums[:, :, None] - correct_lag_position[:, None, :])
    )
    grad_dots = (
        logit_derivative * reciprocal_visual_length[:, :, None] * reciprocal_lag_strip
    ).astype(jnp.bfloat16)
    grad_inv_v = jnp.sum(logit_derivative * lagged_inner_terms * reciprocal_lag_strip, axis=2)
    audio_term = logit_derivative * lagged_inner_terms * reciprocal_visual_length[:, :, None]
    lip_sum, win_sum_pad, ginv_pad = corr_bwd(
        grad_dots, audio_term, emb_v, win_pad
    )
    grad_inv_win = ginv_pad[:, 0, :wide_len]
    lip_vals = emb_v.astype(jnp.float32)
    grad_lip = (
        lip_sum
        - (
            reciprocal_visual_length
            * reciprocal_visual_length
            * reciprocal_visual_length
            * grad_inv_v
        )[:, :, None]
        * lip_vals
    ).astype(jnp.bfloat16)
    win_sum = win_sum_pad[:, :wide_len]
    win_sum = win_sum - (inv_win * inv_win * inv_win * grad_inv_win)[:, :, None] * window.astype(
        jnp.float32
    )
    own_grad = win_sum[:, SPAN : SPAN + frame_num]
    from_after = from_behind(win_sum[:, :SPAN], "tm", -1)
    from_before = from_behind(win_sum[:, frame_num + SPAN :], "tm", 1)
    body = frame_num - SPAN
    own_grad = (
        own_grad
        + jnp.pad(from_after, ((0, 0), (body, 0), (0, 0)))
        + jnp.pad(from_before, ((0, 0), (0, body), (0, 0)))
    )
    grad_audio = own_grad.astype(jnp.bfloat16).reshape(clip_num * frame_num, width)
    grad_lip = grad_lip.reshape(clip_num * frame_num, width)
    grad_ap = proj_grad(hid_a, grad_audio)
    grad_vp = proj_grad(hid_v, grad_lip)
    grad_ac = conv_grad(cols_a, pre_a, grad_audio, w_audio_proj, w_audio_conv)
    grad_vc = conv_grad(cols_v, pre_v, grad_lip, w_lip_proj, w_lip_conv)
    parts = (grad_ac, grad_vc, grad_ap, grad_vp)
    lanes = grad_ap.shape[1]
    loss_block = jnp.where(corner, loss_local, 0.0)
    *sums, loss_total = all_sum([g.reshape(-1, lanes) for g in parts], loss_block)
    grad_ac, grad_vc, grad_ap, grad_vp = (t.reshape(g.shape) for t, g in zip(sums, parts))
    loss_sum = loss_total[0, 0]
    return (loss_sum / count, grad_ac, grad_ap, grad_vc, grad_vp)


def solution(mesh):
    placed = (
        P("clip", "tm", None),
        P("clip", "tm", None),
        P("clip"),
        P("clip"),
        P(),
        P(),
        P(),
        P(),
    )
    return jax.shard_map(
        shards, mesh=mesh, in_specs=placed, out_specs=(P(), P(), P(), P(), P()), check_vma=False
    )
```

```python
import jax
import jax.numpy as jnp
from jax import lax
from jax.sharding import PartitionSpec as P
import functools
from jax.experimental import pallas as pl
from jax.experimental.pallas import tpu as pltpu

SPAN = 15


MESH_ID = pl.DeviceIdType.MESH


def _coords():
    ci = lax.axis_index("clip")
    ti = lax.axis_index("tm")
    return ci, ti, ci % 4, (ci // 4) % 4, ci // 16, ti % 2, ti // 2


def _levels():
    ci, ti, y, x, zh, core, zl = _coords()
    z = zh * 4 + zl

    def at_y(v):
        return (zh * 16 + x * 4 + v % 4, ti)

    def at_x(v):
        return (zh * 16 + (v % 4) * 4 + y, ti)

    def at_z(v):
        w = v % 8
        return ((w // 4) * 16 + x * 4 + y, (w % 4) * 2 + core)

    def at_c(v):
        return (ci, zl * 2 + v % 2)

    def at_h(v):
        return ((v % 2) * 16 + x * 4 + y, ti)

    def at_k(v):
        return (v % 32, ti)

    return {
        "c": (2, core, at_c, 1),
        "y": (4, y, at_y, 2),
        "x": (4, x, at_x, 2),
        "z": (8, z, at_z, 1),
        "h": (2, zh, at_h, 1),
        "k": (32, ci, at_k, 1),
    }


def _barrier(levels):
    barrier = pltpu.get_barrier_semaphore()
    peers = []
    for n, me, nbr, ndir in levels:
        peers.append(nbr(me + 1))
        if n > 2:
            peers.append(nbr(me - 1))
    for p in peers:
        pl.semaphore_signal(barrier, inc=1, device_id=p, device_id_type=MESH_ID)
    pl.semaphore_wait(barrier, len(peers))


def _small_start(n, me, nbr, s, tbuf, toff, tsend, trecv, tsem):
    at = toff + (me - s) % n
    c = pltpu.make_async_remote_copy(
        src_ref=tbuf.at[at],
        dst_ref=tbuf.at[at],
        send_sem=tsend.at[tsem],
        recv_sem=trecv.at[tsem],
        device_id=nbr(me + 1),
        device_id_type=MESH_ID,
    )
    c.start()
    return c


def _small_sum(n, tbuf, toff):
    acc = tbuf[toff]
    for k in range(1, n):
        acc = acc + tbuf[toff + k]
    return acc


def _small_kernel(names, t_ref, to_ref, tbuf, tsend, trecv):
    table = _levels()
    levels = [table[k] for k in names]
    barrier = pltpu.get_barrier_semaphore()
    peers = [nbr(me + j) for n, me, nbr, ndir in levels for j in range(1, n)]
    for p in peers:
        pl.semaphore_signal(barrier, inc=1, device_id=p, device_id_type=MESH_ID)
    pl.semaphore_wait(barrier, len(peers))
    toff = 0
    tsem = 0
    for li, (n, me, nbr, ndir) in enumerate(levels):
        tbuf[toff + me] = t_ref[...] if li == 0 else to_ref[...]
        copies = []
        for j in range(1, n):
            c = pltpu.make_async_remote_copy(
                src_ref=tbuf.at[toff + me],
                dst_ref=tbuf.at[toff + me],
                send_sem=tsend.at[tsem],
                recv_sem=trecv.at[tsem],
                device_id=nbr(me + j),
                device_id_type=MESH_ID,
            )
            c.start()
            copies.append(c)
            tsem += 1
        for c in copies:
            c.wait()
        to_ref[...] = _small_sum(n, tbuf, toff)
        toff += n


def small_sum(t, names, cid):
    table_n = {"c": 2, "y": 4, "x": 4, "z": 8, "h": 2, "k": 32}
    slots = sum(table_n[k] for k in names)
    sems = sum(table_n[k] - 1 for k in names)
    return pl.pallas_call(
        functools.partial(_small_kernel, names),
        out_shape=jax.ShapeDtypeStruct(t.shape, t.dtype),
        in_specs=[pl.BlockSpec(memory_space=pltpu.VMEM)],
        out_specs=pl.BlockSpec(memory_space=pltpu.VMEM),
        scratch_shapes=[
            pltpu.VMEM((slots,) + t.shape, t.dtype),
            pltpu.SemaphoreType.DMA((sems,)),
            pltpu.SemaphoreType.DMA((sems,)),
        ],
        compiler_params=pltpu.CompilerParams(collective_id=cid, has_side_effects=True),
    )(t)


def _rs_stage(tasks, work, rbuf, send_sem, recv_sem, slot, sem, rider=None):
    n = tasks[0][0]
    for s in range(n - 1):
        copies = []
        for tn, me, nbr, ndir, base, size, own in tasks:
            chunk = size // tn
            piece = chunk // ndir
            for d in range(ndir):
                sign = 1 if d == 0 else -1
                send_at = pl.multiple_of(base + ((me - sign * (s + 1)) % tn) * chunk + d * piece, 8)
                recv_at = pl.multiple_of(base + ((me - sign * (s + 2)) % tn) * chunk + d * piece, 8)
                src = own if s == 0 else work
                c = pltpu.make_async_remote_copy(
                    src_ref=src.at[pl.ds(send_at, piece)],
                    dst_ref=rbuf.at[pl.ds(slot, piece)],
                    send_sem=send_sem.at[sem],
                    recv_sem=recv_sem.at[sem],
                    device_id=nbr(me + sign),
                    device_id_type=MESH_ID,
                )
                c.start()
                copies.append((c, slot, recv_at, piece, own))
                slot += piece
                sem += 1
        ride = rider(s) if rider is not None else None
        for c, sl, recv_at, piece, own in copies:
            c.wait_recv()
            at = pl.ds(recv_at, piece)
            work[at] = rbuf[pl.ds(sl, piece)] + own[at]
        for c, sl, recv_at, piece, own in copies:
            c.wait_send()
        if ride is not None:
            ride.wait()
    return slot, sem


def _ag_stage(tasks, o_ref, send_sem, recv_sem, sem):
    n = tasks[0][0]
    for s in range(n - 1):
        copies = []
        for tn, me, nbr, ndir, base, size, own in tasks:
            chunk = size // tn
            piece = chunk // ndir
            for d in range(ndir):
                sign = 1 if d == 0 else -1
                at = pl.ds(pl.multiple_of(base + ((me - sign * s) % tn) * chunk + d * piece, 8), piece)
                c = pltpu.make_async_remote_copy(
                    src_ref=o_ref.at[at],
                    dst_ref=o_ref.at[at],
                    send_sem=send_sem.at[sem],
                    recv_sem=recv_sem.at[sem],
                    device_id=nbr(me + sign),
                    device_id_type=MESH_ID,
                )
                c.start()
                copies.append(c)
                sem += 1
        for c in copies:
            c.wait()
    return sem


def _pass_copy(buf, at, nbr, target, sems, idx):
    c = pltpu.make_async_remote_copy(
        src_ref=buf.at[at],
        dst_ref=buf.at[at],
        send_sem=sems[0].at[idx],
        recv_sem=sems[1].at[idx],
        device_id=nbr(target),
        device_id_type=MESH_ID,
    )
    c.start()
    return c


def _kernel(sizes, *refs):
    parts = len(sizes)
    ins, t_ref = refs[:parts], refs[parts]
    outs, to_ref = refs[parts + 1 : 2 * parts + 1], refs[2 * parts + 1]
    work, rbuf, zbuf, send_sem, recv_sem, tbuf, tsend, trecv, half_ref, hsend, hrecv, o_ref = refs[2 * parts + 2 :]
    rows = sum(sizes)
    start = 0
    for size, in_ref in zip(sizes, ins):
        work[start : start + size] = in_ref[...]
        start += size
    table = _levels()
    lc, ly, lx, lz = (table[k] for k in ("c", "y", "x", "z"))
    _barrier([lc, ly, lx, lz])
    tsems = (tsend, trecv)
    state = {"toff": 0, "tsem": 0}

    def tiny_level(level, first):
        n, me, nbr, ndir = level
        toff = state["toff"]
        tbuf[toff + me] = t_ref[...] if first else to_ref[...]

        def rider(s):
            c = _pass_copy(tbuf, toff + (me - s) % n, nbr, me + 1, tsems, state["tsem"])
            state["tsem"] += 1
            return c

        return rider

    def tiny_done(n):
        to_ref[...] = _small_sum(n, tbuf, state["toff"])
        state["toff"] += n

    slot, sem = 0, 0
    half = rows // 2
    quarter = rows // 4
    nc, core, nbc, _ = lc
    ny, yi, nby, _ = ly
    nx, xi, nbx, _ = lx
    nz, zi, nbz, _ = lz

    rider = tiny_level(lc, True)
    slot, sem = _rs_stage([(nc, core, nbc, 1, 0, rows, work)], work, rbuf, send_sem, recv_sem, slot, sem, rider)
    tiny_done(nc)
    r0 = core * half
    a1, b1 = r0, r0 + quarter
    rider = tiny_level(ly, False)
    slot, sem = _rs_stage(
        [(ny, yi, nby, 2, a1, quarter, work), (nx, xi, nbx, 2, b1, quarter, work)],
        work, rbuf, send_sem, recv_sem, slot, sem, rider,
    )
    tiny_done(ny)
    c1 = quarter // 4
    a2, b2 = a1 + yi * c1, b1 + xi * c1
    rider = tiny_level(lx, False)
    slot, sem = _rs_stage(
        [(nx, xi, nbx, 1, a2, c1, work), (ny, yi, nby, 1, b2, c1, work)],
        work, rbuf, send_sem, recv_sem, slot, sem, rider,
    )
    tiny_done(nx)
    c2 = c1 // 4
    a3, b3 = a2 + xi * c2, b2 + yi * c2
    zbuf[zi, 0] = work[pl.ds(pl.multiple_of(a3, 8), c2)]
    zbuf[zi, 1] = work[pl.ds(pl.multiple_of(b3, 8), c2)]
    toff = state["toff"]
    tbuf[toff + zi] = to_ref[...]
    right = nz // 2
    left = nz - 1 - right
    for s in range(right):
        cs = [
            _pass_copy(zbuf, (zi - s) % nz, nbz, zi + 1, (send_sem, recv_sem), sem),
            _pass_copy(tbuf, toff + (zi - s) % nz, nbz, zi + 1, tsems, state["tsem"]),
        ]
        sem += 1
        state["tsem"] += 1
        if s < left:
            cs.append(_pass_copy(zbuf, (zi + s) % nz, nbz, zi - 1, (send_sem, recv_sem), sem))
            cs.append(_pass_copy(tbuf, toff + (zi + s) % nz, nbz, zi - 1, tsems, state["tsem"]))
            sem += 1
            state["tsem"] += 1
        for c in cs:
            c.wait()
    for colour, at in ((0, a3), (1, b3)):
        acc = zbuf[0, colour]
        for k in range(1, nz):
            acc = acc + zbuf[k, colour]
        o_ref[pl.ds(pl.multiple_of(at, 8), c2)] = acc
    tiny_done(nz)
    sem = _ag_stage([(nx, xi, nbx, 1, a2, c1, None), (ny, yi, nby, 1, b2, c1, None)], o_ref, send_sem, recv_sem, sem)
    for at in (a2, b2):
        region = pl.ds(pl.multiple_of(at, 16), c1)
        half_ref[region] = o_ref[region].astype(half_ref.dtype)
    sem = _ag_stage([(ny, yi, nby, 2, a1, quarter, None), (nx, xi, nbx, 2, b1, quarter, None)], half_ref, hsend, hrecv, 0)
    _ag_stage([(nc, core, nbc, 1, 0, rows, None)], half_ref, hsend, hrecv, sem)
    start = 0
    for size, out_ref in zip(sizes, outs):
        out_ref[...] = half_ref[start : start + size]
        start += size


def _counts(rows):
    half, quarter = rows // 2, rows // 4
    c1 = quarter // 4
    slots = half + 3 * 2 * quarter // 4 + 3 * 2 * c1 // 4
    sems = 1 + 3 * 4 + 3 * 2 + 7 + 3 * 2
    return slots, sems, 2 + 4 + 4 + 8, 1 + 3 + 3 + 7


def all_sum(parts, small):
    sizes = tuple(p.shape[0] for p in parts)
    lanes = parts[0].shape[1]
    rows = sum(sizes)
    slots, sems, tslots, tsems = _counts(rows)
    c2 = rows // 64
    vmem = pl.BlockSpec(memory_space=pltpu.VMEM)
    return pl.pallas_call(
        functools.partial(_kernel, sizes),
        out_shape=tuple(jax.ShapeDtypeStruct(p.shape, jnp.bfloat16) for p in parts)
        + (jax.ShapeDtypeStruct(small.shape, small.dtype),),
        in_specs=[vmem] * (len(parts) + 1),
        out_specs=(vmem,) * (len(parts) + 1),
        scratch_shapes=[
            pltpu.VMEM((rows, lanes), jnp.float32),
            pltpu.VMEM((slots, lanes), jnp.float32),
            pltpu.VMEM((8, 2, c2, lanes), jnp.float32),
            pltpu.SemaphoreType.DMA((sems,)),
            pltpu.SemaphoreType.DMA((sems,)),
            pltpu.VMEM((tslots,) + small.shape, small.dtype),
            pltpu.SemaphoreType.DMA((tsems,)),
            pltpu.SemaphoreType.DMA((tsems,)),
            pltpu.VMEM((rows, lanes), jnp.bfloat16),
            pltpu.SemaphoreType.DMA((13,)),
            pltpu.SemaphoreType.DMA((13,)),
            pltpu.VMEM((rows, lanes), jnp.float32),
        ],
        compiler_params=pltpu.CompilerParams(
            collective_id=0, has_side_effects=True, vmem_limit_bytes=48 * 1024 * 1024
        ),
    )(*parts, small)


def _corr_fwd_kernel(ev_ref, win_ref, inv_ref, dots_ref, strip_ref):
    wide = win_ref.shape[0]
    lanes = dots_ref.shape[1]
    rows = lax.broadcasted_iota(jnp.int32, (wide, wide), 0)
    cols = lax.broadcasted_iota(jnp.int32, (wide, wide), 1)
    flip = (rows + cols == wide - 1).astype(jnp.bfloat16)
    win_rev = jnp.dot(flip, win_ref[...], preferred_element_type=jnp.float32).astype(jnp.bfloat16)
    m = lax.dot_general(
        ev_ref[...], win_rev, (((1,), (1,)), ((), ())), preferred_element_type=jnp.float32
    )
    rows = lax.broadcasted_iota(jnp.int32, (lanes, lanes), 0)
    cols = lax.broadcasted_iota(jnp.int32, (lanes, lanes), 1)
    back = (rows + cols == lanes - 1).astype(jnp.float32)

    def unflip(x):
        return jnp.dot(x, back, precision=lax.Precision.HIGHEST, preferred_element_type=jnp.float32)

    dots_ref[...] = unflip(pltpu.roll(m, 0, 1, stride=1, stride_axis=0)[:, wide - lanes :])
    inv = jnp.broadcast_to(inv_ref[...], m.shape)
    strip_ref[...] = unflip(pltpu.roll(inv, 0, 1, stride=1, stride_axis=0)[:, wide - lanes :])


def corr_fwd(emb_v, win_pad, inv_pad):
    clips, frames, width = emb_v.shape
    wide = win_pad.shape[1]
    lanes = 128
    return pl.pallas_call(
        _corr_fwd_kernel,
        grid=(clips,),
        in_specs=[
            pl.BlockSpec((None, frames, width), lambda c: (c, 0, 0)),
            pl.BlockSpec((None, wide, width), lambda c: (c, 0, 0)),
            pl.BlockSpec((None, 1, wide), lambda c: (c, 0, 0)),
        ],
        out_specs=[
            pl.BlockSpec((None, frames, lanes), lambda c: (c, 0, 0)),
            pl.BlockSpec((None, frames, lanes), lambda c: (c, 0, 0)),
        ],
        out_shape=[
            jax.ShapeDtypeStruct((clips, frames, lanes), jnp.float32),
            jax.ShapeDtypeStruct((clips, frames, lanes), jnp.float32),
        ],
    )(emb_v, win_pad, inv_pad)


def _corr_bwd_kernel(gd_ref, at_ref, ev_ref, win_ref, lip_ref, wsum_ref, ginv_ref):
    frames, lanes = gd_ref.shape
    wide = win_ref.shape[0]
    pad = jnp.zeros((frames, wide - lanes), jnp.float32)
    g = jnp.concatenate([gd_ref[...].astype(jnp.float32), pad], axis=1)
    band = pltpu.roll(g, 0, 1, stride=1, stride_axis=0)
    lip_ref[...] = jnp.dot(band.astype(jnp.bfloat16), win_ref[...], preferred_element_type=jnp.float32)
    band_t = band.T.astype(jnp.bfloat16)
    wsum_ref[...] = jnp.dot(band_t, ev_ref[...], preferred_element_type=jnp.float32)
    a = jnp.concatenate([at_ref[...], pad], axis=1)
    spread = pltpu.roll(a, 0, 1, stride=1, stride_axis=0)
    ginv_ref[...] = jnp.sum(spread, axis=0, keepdims=True)


def corr_bwd(gd_pad, at_pad, emb_v, win_pad):
    clips, frames, width = emb_v.shape
    wide = win_pad.shape[1]
    lanes = gd_pad.shape[2]
    return pl.pallas_call(
        _corr_bwd_kernel,
        grid=(clips,),
        in_specs=[
            pl.BlockSpec((None, frames, lanes), lambda c: (c, 0, 0)),
            pl.BlockSpec((None, frames, lanes), lambda c: (c, 0, 0)),
            pl.BlockSpec((None, frames, width), lambda c: (c, 0, 0)),
            pl.BlockSpec((None, wide, width), lambda c: (c, 0, 0)),
        ],
        out_specs=[
            pl.BlockSpec((None, frames, width), lambda c: (c, 0, 0)),
            pl.BlockSpec((None, wide, width), lambda c: (c, 0, 0)),
            pl.BlockSpec((None, 1, wide), lambda c: (c, 0, 0)),
        ],
        out_shape=[
            jax.ShapeDtypeStruct((clips, frames, width), jnp.float32),
            jax.ShapeDtypeStruct((clips, wide, width), jnp.float32),
            jax.ShapeDtypeStruct((clips, 1, wide), jnp.float32),
        ],
    )(gd_pad, at_pad, emb_v, win_pad)


logit_sharpening_divisor = 10.0
loss_scale = 1024.0
epsilon = 1e-06


def padded_2(cells, sides, width):
    for axis, dim in sides:
        count = lax.axis_size(axis)
        ends = count - 1
        head = lax.slice_in_dim(cells, 0, width, axis=dim)
        tail = lax.slice_in_dim(cells, cells.shape[dim] - width, cells.shape[dim], axis=dim)
        cells = jnp.concatenate(
            [
                lax.ppermute(tail, axis, [(i, (i + 1) % count) for i in range(ends)]),
                cells,
                lax.ppermute(head, axis, [((i + 1) % count, i) for i in range(ends)]),
            ],
            axis=dim,
        )
    return cells


def from_behind(value, axis, steps):
    count = lax.axis_size(axis)
    initial, last = (max(0, -steps), min(count, count - steps))
    return lax.ppermute(value, axis, [(source, source + steps) for source in range(initial, last)])


def silu_slope(values):
    sigma = jax.nn.sigmoid(values)
    return sigma * (1.0 + values * (1.0 - sigma))


def encoder(padded, w_conv, w_proj):
    clip_num, frame_pad, chan_num = padded.shape
    frame_num = frame_pad - 2
    columns = jnp.concatenate(
        [padded[:, 0:frame_num], padded[:, 1 : frame_num + 1], padded[:, 2 : frame_num + 2]], axis=2
    )
    before = jnp.einsum(
        "cfk,ke->cfe",
        columns,
        w_conv.reshape(3 * chan_num, w_conv.shape[2]),
        preferred_element_type=jnp.float32,
    )
    hidden = jax.nn.silu(before).astype(jnp.bfloat16)
    embedded = jnp.einsum("cfe,eg->cfg", hidden, w_proj, preferred_element_type=jnp.float32).astype(
        jnp.bfloat16
    )
    return (columns, before, hidden, embedded)


def inverse_norm(embedded):
    values = embedded.astype(jnp.float32)
    return lax.rsqrt(jnp.sum(values * values, axis=-1) + epsilon)


def spread_band(band, wide_len):
    clip_num, row_num, band_len = band.shape
    full_band = jnp.pad(band, ((0, 0), (0, 0), (0, wide_len + 1 - band_len)))
    flat_band = full_band.reshape(clip_num, row_num * (wide_len + 1))[:, : row_num * wide_len]
    return flat_band.reshape(clip_num, row_num, wide_len)


def narrow_band(matrix, band_len):
    clip_num, row_num, wide_len = matrix.shape
    flat_mat = jnp.pad(matrix.reshape(clip_num, row_num * wide_len), ((0, 0), (0, row_num)))
    return flat_mat.reshape(clip_num, row_num, wide_len + 1)[:, :, :band_len]


def flatten_rows(values):
    return values.reshape(values.shape[0] * values.shape[1], values.shape[2])


def proj_grad(hidden, grad_emb):
    return jnp.einsum("re,rf->ef", hidden, grad_emb, preferred_element_type=jnp.float32)


def conv_grad(columns, before, grad_emb, w_proj, w_conv):
    grad_hidden = jnp.einsum("rf,ef->re", grad_emb, w_proj, preferred_element_type=jnp.float32)
    grad_before = (grad_hidden * silu_slope(before)).astype(jnp.bfloat16)
    grad_conv = jnp.einsum("rk,re->ke", columns, grad_before, preferred_element_type=jnp.float32)
    return grad_conv.reshape(w_conv.shape)


def shards(
    audio_feats, lip_feats, lengths, labels, w_audio_conv, w_audio_proj, w_lip_conv, w_lip_proj
):
    clip_num, frame_num, chan_num = audio_feats.shape
    width = w_audio_proj.shape[1]
    offsets = 2 * SPAN + 1
    wide_len = frame_num + 2 * SPAN
    first_frame = lax.axis_index("tm") * frame_num
    stacked = jnp.stack([audio_feats, lip_feats])
    padded = padded_2(stacked, (("tm", 2),), 1)
    cols_a, pre_a, hid_a, emb_a = encoder(padded[0], w_audio_conv, w_audio_proj)
    cols_v, pre_v, hid_v, emb_v = encoder(padded[1], w_lip_conv, w_lip_proj)
    window = padded_2(emb_a, (("tm", 1),), SPAN)
    cols_a, pre_a, hid_a = (flatten_rows(cols_a), flatten_rows(pre_a), flatten_rows(hid_a))
    cols_v, pre_v, hid_v = (flatten_rows(cols_v), flatten_rows(pre_v), flatten_rows(hid_v))
    count_part = jnp.sum(lengths - jnp.abs(labels))
    count_block = jnp.zeros((8, 128), jnp.int32).at[0, 0].set(count_part)
    count = small_sum(count_block, ("k",), 1)[0, 0].astype(jnp.float32)
    inv_win = inverse_norm(window)
    reciprocal_visual_length = inverse_norm(emb_v)
    wide_pad = -(-wide_len // 128) * 128
    win_pad = jnp.pad(window, ((0, 0), (0, wide_pad - wide_len), (0, 0)))
    inv_pad = jnp.pad(inv_win, ((0, 0), (0, wide_pad - wide_len)))[:, None, :]
    lagged_inner_terms, reciprocal_lag_strip = corr_fwd(emb_v, win_pad, inv_pad[:, :, ::-1])
    lanes_used = lagged_inner_terms.shape[2]
    frame_ids = first_frame + jnp.arange(frame_num, dtype=jnp.int32)
    shifts = jnp.arange(lanes_used, dtype=jnp.int32) - SPAN
    positions = frame_ids[:, None] + shifts[None, :]
    inside = frame_ids[None, :] < lengths[:, None]
    valid = inside[:, :, None] & (positions[None] >= 0) & (positions[None] < lengths[:, None, None])
    valid = valid & (shifts < offsets - SPAN)[None, None, :]
    target_pos = frame_ids[None, :] + labels[:, None]
    counted = inside & (target_pos >= 0) & (target_pos < lengths[:, None])
    correct_lag_position = (shifts[None, :] == labels[:, None]).astype(jnp.float32)
    lag_similarity_logits = (
        logit_sharpening_divisor
        * lagged_inner_terms
        * reciprocal_visual_length[:, :, None]
        * reciprocal_lag_strip
    )
    exponentiated_logits = jnp.where(valid, jnp.exp(lag_similarity_logits), 0.0)
    partition_sums = jnp.where(inside, jnp.sum(exponentiated_logits, axis=2), 1.0)
    picked = jnp.sum(lag_similarity_logits * correct_lag_position[:, None, :], axis=2)
    loss_local = jnp.sum(jnp.where(counted, jnp.log(partition_sums) - picked, 0.0))
    normalized_probabilities = jnp.where(counted, loss_scale / count, 0.0)
    logit_derivative = (
        logit_sharpening_divisor
        * normalized_probabilities[:, :, None]
        * (exponentiated_logits / partition_sums[:, :, None] - correct_lag_position[:, None, :])
    )
    grad_dots = (
        logit_derivative * reciprocal_visual_length[:, :, None] * reciprocal_lag_strip
    ).astype(jnp.bfloat16)
    grad_inv_v = jnp.sum(logit_derivative * lagged_inner_terms * reciprocal_lag_strip, axis=2)
    audio_term = logit_derivative * lagged_inner_terms * reciprocal_visual_length[:, :, None]
    lip_sum, win_sum_pad, ginv_pad = corr_bwd(
        grad_dots, audio_term, emb_v, win_pad
    )
    grad_inv_win = ginv_pad[:, 0, :wide_len]
    lip_vals = emb_v.astype(jnp.float32)
    grad_lip = (
        lip_sum
        - (
            reciprocal_visual_length
            * reciprocal_visual_length
            * reciprocal_visual_length
            * grad_inv_v
        )[:, :, None]
        * lip_vals
    ).astype(jnp.bfloat16)
    win_sum = win_sum_pad[:, :wide_len]
    win_sum = win_sum - (inv_win * inv_win * inv_win * grad_inv_win)[:, :, None] * window.astype(
        jnp.float32
    )
    own_grad = win_sum[:, SPAN : SPAN + frame_num]
    from_after = from_behind(win_sum[:, :SPAN], "tm", -1)
    from_before = from_behind(win_sum[:, frame_num + SPAN :], "tm", 1)
    body = frame_num - SPAN
    own_grad = (
        own_grad
        + jnp.pad(from_after, ((0, 0), (body, 0), (0, 0)))
        + jnp.pad(from_before, ((0, 0), (0, body), (0, 0)))
    )
    grad_audio = own_grad.astype(jnp.bfloat16).reshape(clip_num * frame_num, width)
    grad_lip = grad_lip.reshape(clip_num * frame_num, width)
    grad_ap = proj_grad(hid_a, grad_audio)
    grad_vp = proj_grad(hid_v, grad_lip)
    grad_ac = conv_grad(cols_a, pre_a, grad_audio, w_audio_proj, w_audio_conv)
    grad_vc = conv_grad(cols_v, pre_v, grad_lip, w_lip_proj, w_lip_conv)
    parts = (grad_ac, grad_vc, grad_ap, grad_vp)
    lanes = grad_ap.shape[1]
    loss_block = jnp.zeros((8, 128), jnp.float32).at[0, 0].set(loss_local)
    *sums, loss_total = all_sum([g.reshape(-1, lanes) for g in parts], loss_block)
    grad_ac, grad_vc, grad_ap, grad_vp = (
        t.astype(jnp.float32).reshape(g.shape) for t, g in zip(sums, parts)
    )
    loss_sum = loss_total[0, 0]
    return (loss_sum / count, grad_ac, grad_ap, grad_vc, grad_vp)


def solution(mesh):
    placed = (
        P("clip", "tm", None),
        P("clip", "tm", None),
        P("clip"),
        P("clip"),
        P(),
        P(),
        P(),
        P(),
    )
    return jax.shard_map(
        shards, mesh=mesh, in_specs=placed, out_specs=(P(), P(), P(), P(), P()), check_vma=False
    )
```

```python
import jax
import jax.numpy as jnp
from jax import lax
from jax.sharding import PartitionSpec as P
import functools
from jax.experimental import pallas as pl
from jax.experimental.pallas import tpu as pltpu

SPAN = 15


MESH_ID = pl.DeviceIdType.MESH


def _coords():
    ci = lax.axis_index("clip")
    ti = lax.axis_index("tm")
    return ci, ti, ci % 4, (ci // 4) % 4, ci // 16, ti % 2, ti // 2


def _levels():
    ci, ti, y, x, zh, core, zl = _coords()
    z = zh * 4 + zl

    def at_y(v):
        return (zh * 16 + x * 4 + v % 4, ti)

    def at_x(v):
        return (zh * 16 + (v % 4) * 4 + y, ti)

    def at_z(v):
        w = v % 8
        return ((w // 4) * 16 + x * 4 + y, (w % 4) * 2 + core)

    def at_c(v):
        return (ci, zl * 2 + v % 2)

    def at_h(v):
        return ((v % 2) * 16 + x * 4 + y, ti)

    def at_k(v):
        return (v % 32, ti)

    return {
        "c": (2, core, at_c, 1),
        "y": (4, y, at_y, 2),
        "x": (4, x, at_x, 2),
        "z": (8, z, at_z, 1),
        "h": (2, zh, at_h, 1),
        "k": (32, ci, at_k, 1),
    }


def _barrier(levels):
    barrier = pltpu.get_barrier_semaphore()
    peers = []
    for n, me, nbr, ndir in levels:
        peers.append(nbr(me + 1))
        if n > 2:
            peers.append(nbr(me - 1))
    for p in peers:
        pl.semaphore_signal(barrier, inc=1, device_id=p, device_id_type=MESH_ID)
    pl.semaphore_wait(barrier, len(peers))


def _small_start(n, me, nbr, s, tbuf, toff, tsend, trecv, tsem):
    at = toff + (me - s) % n
    c = pltpu.make_async_remote_copy(
        src_ref=tbuf.at[at],
        dst_ref=tbuf.at[at],
        send_sem=tsend.at[tsem],
        recv_sem=trecv.at[tsem],
        device_id=nbr(me + 1),
        device_id_type=MESH_ID,
    )
    c.start()
    return c


def _small_sum(n, tbuf, toff):
    acc = tbuf[toff]
    for k in range(1, n):
        acc = acc + tbuf[toff + k]
    return acc


def _small_kernel(names, t_ref, to_ref, tbuf, tsend, trecv):
    table = _levels()
    levels = [table[k] for k in names]
    barrier = pltpu.get_barrier_semaphore()
    peers = [nbr(me + j) for n, me, nbr, ndir in levels for j in range(1, n)]
    for p in peers:
        pl.semaphore_signal(barrier, inc=1, device_id=p, device_id_type=MESH_ID)
    pl.semaphore_wait(barrier, len(peers))
    toff = 0
    tsem = 0
    for li, (n, me, nbr, ndir) in enumerate(levels):
        tbuf[toff + me] = t_ref[...] if li == 0 else to_ref[...]
        copies = []
        for j in range(1, n):
            c = pltpu.make_async_remote_copy(
                src_ref=tbuf.at[toff + me],
                dst_ref=tbuf.at[toff + me],
                send_sem=tsend.at[tsem],
                recv_sem=trecv.at[tsem],
                device_id=nbr(me + j),
                device_id_type=MESH_ID,
            )
            c.start()
            copies.append(c)
            tsem += 1
        for c in copies:
            c.wait()
        to_ref[...] = _small_sum(n, tbuf, toff)
        toff += n


def small_sum(t, names, cid):
    table_n = {"c": 2, "y": 4, "x": 4, "z": 8, "h": 2, "k": 32}
    slots = sum(table_n[k] for k in names)
    sems = sum(table_n[k] - 1 for k in names)
    return pl.pallas_call(
        functools.partial(_small_kernel, names),
        out_shape=jax.ShapeDtypeStruct(t.shape, t.dtype),
        in_specs=[pl.BlockSpec(memory_space=pltpu.VMEM)],
        out_specs=pl.BlockSpec(memory_space=pltpu.VMEM),
        scratch_shapes=[
            pltpu.VMEM((slots,) + t.shape, t.dtype),
            pltpu.SemaphoreType.DMA((sems,)),
            pltpu.SemaphoreType.DMA((sems,)),
        ],
        compiler_params=pltpu.CompilerParams(collective_id=cid, has_side_effects=True),
    )(t)


def _rs_stage(tasks, work, rbuf, send_sem, recv_sem, slot, sem, rider=None):
    n = tasks[0][0]
    for s in range(n - 1):
        copies = []
        for tn, me, nbr, ndir, base, size, own in tasks:
            chunk = size // tn
            piece = chunk // ndir
            for d in range(ndir):
                sign = 1 if d == 0 else -1
                send_at = pl.multiple_of(base + ((me - sign * (s + 1)) % tn) * chunk + d * piece, 8)
                recv_at = pl.multiple_of(base + ((me - sign * (s + 2)) % tn) * chunk + d * piece, 8)
                src = own if s == 0 else work
                c = pltpu.make_async_remote_copy(
                    src_ref=src.at[pl.ds(send_at, piece)],
                    dst_ref=rbuf.at[pl.ds(slot, piece)],
                    send_sem=send_sem.at[sem],
                    recv_sem=recv_sem.at[sem],
                    device_id=nbr(me + sign),
                    device_id_type=MESH_ID,
                )
                c.start()
                copies.append((c, slot, recv_at, piece, own))
                slot += piece
                sem += 1
        ride = rider(s) if rider is not None else None
        for c, sl, recv_at, piece, own in copies:
            c.wait_recv()
            at = pl.ds(recv_at, piece)
            work[at] = rbuf[pl.ds(sl, piece)] + own[at]
        for c, sl, recv_at, piece, own in copies:
            c.wait_send()
        if ride is not None:
            ride.wait()
    return slot, sem


def _ag_stage(tasks, o_ref, send_sem, recv_sem, sem):
    n = tasks[0][0]
    for s in range(n - 1):
        copies = []
        for tn, me, nbr, ndir, base, size, own in tasks:
            chunk = size // tn
            piece = chunk // ndir
            for d in range(ndir):
                sign = 1 if d == 0 else -1
                at = pl.ds(pl.multiple_of(base + ((me - sign * s) % tn) * chunk + d * piece, 8), piece)
                c = pltpu.make_async_remote_copy(
                    src_ref=o_ref.at[at],
                    dst_ref=o_ref.at[at],
                    send_sem=send_sem.at[sem],
                    recv_sem=recv_sem.at[sem],
                    device_id=nbr(me + sign),
                    device_id_type=MESH_ID,
                )
                c.start()
                copies.append(c)
                sem += 1
        for c in copies:
            c.wait()
    return sem


def _pass_copy(buf, at, nbr, target, sems, idx):
    c = pltpu.make_async_remote_copy(
        src_ref=buf.at[at],
        dst_ref=buf.at[at],
        send_sem=sems[0].at[idx],
        recv_sem=sems[1].at[idx],
        device_id=nbr(target),
        device_id_type=MESH_ID,
    )
    c.start()
    return c


def _kernel(sizes, *refs):
    parts = len(sizes)
    ins, t_ref = refs[:parts], refs[parts]
    outs, to_ref = refs[parts + 1 : 2 * parts + 1], refs[2 * parts + 1]
    work, rbuf, zbuf, send_sem, recv_sem, tbuf, tsend, trecv, half_ref, hsend, hrecv, o_ref = refs[2 * parts + 2 :]
    rows = sum(sizes)
    start = 0
    for size, in_ref in zip(sizes, ins):
        work[start : start + size] = in_ref[...]
        start += size
    table = _levels()
    lc, ly, lx, lz = (table[k] for k in ("c", "y", "x", "z"))
    _barrier([lc, ly, lx, lz])
    tsems = (tsend, trecv)
    state = {"toff": 0, "tsem": 0}

    def tiny_level(level, first):
        n, me, nbr, ndir = level
        toff = state["toff"]
        tbuf[toff + me] = t_ref[...] if first else to_ref[...]

        def rider(s):
            c = _pass_copy(tbuf, toff + (me - s) % n, nbr, me + 1, tsems, state["tsem"])
            state["tsem"] += 1
            return c

        return rider

    def tiny_done(n):
        to_ref[...] = _small_sum(n, tbuf, state["toff"])
        state["toff"] += n

    slot, sem = 0, 0
    half = rows // 2
    quarter = rows // 4
    nc, core, nbc, _ = lc
    ny, yi, nby, _ = ly
    nx, xi, nbx, _ = lx
    nz, zi, nbz, _ = lz

    rider = tiny_level(lc, True)
    slot, sem = _rs_stage([(nc, core, nbc, 1, 0, rows, work)], work, rbuf, send_sem, recv_sem, slot, sem, rider)
    tiny_done(nc)
    r0 = core * half
    a1, b1 = r0, r0 + quarter
    rider = tiny_level(ly, False)
    slot, sem = _rs_stage(
        [(ny, yi, nby, 2, a1, quarter, work), (nx, xi, nbx, 2, b1, quarter, work)],
        work, rbuf, send_sem, recv_sem, slot, sem, rider,
    )
    tiny_done(ny)
    c1 = quarter // 4
    a2, b2 = a1 + yi * c1, b1 + xi * c1
    rider = tiny_level(lx, False)
    slot, sem = _rs_stage(
        [(nx, xi, nbx, 1, a2, c1, work), (ny, yi, nby, 1, b2, c1, work)],
        work, rbuf, send_sem, recv_sem, slot, sem, rider,
    )
    tiny_done(nx)
    c2 = c1 // 4
    a3, b3 = a2 + xi * c2, b2 + yi * c2
    zbuf[zi, 0] = work[pl.ds(pl.multiple_of(a3, 8), c2)]
    zbuf[zi, 1] = work[pl.ds(pl.multiple_of(b3, 8), c2)]
    toff = state["toff"]
    tbuf[toff + zi] = to_ref[...]
    right = nz // 2
    left = nz - 1 - right
    for s in range(right):
        cs = [
            _pass_copy(zbuf, (zi - s) % nz, nbz, zi + 1, (send_sem, recv_sem), sem),
            _pass_copy(tbuf, toff + (zi - s) % nz, nbz, zi + 1, tsems, state["tsem"]),
        ]
        sem += 1
        state["tsem"] += 1
        if s < left:
            cs.append(_pass_copy(zbuf, (zi + s) % nz, nbz, zi - 1, (send_sem, recv_sem), sem))
            cs.append(_pass_copy(tbuf, toff + (zi + s) % nz, nbz, zi - 1, tsems, state["tsem"]))
            sem += 1
            state["tsem"] += 1
        for c in cs:
            c.wait()
    for colour, at in ((0, a3), (1, b3)):
        acc = zbuf[0, colour]
        for k in range(1, nz):
            acc = acc + zbuf[k, colour]
        o_ref[pl.ds(pl.multiple_of(at, 8), c2)] = acc
    tiny_done(nz)
    sem = _ag_stage([(nx, xi, nbx, 1, a2, c1, None), (ny, yi, nby, 1, b2, c1, None)], o_ref, send_sem, recv_sem, sem)
    for at in (a2, b2):
        region = pl.ds(pl.multiple_of(at, 16), c1)
        half_ref[region] = o_ref[region].astype(half_ref.dtype)
    sem = _ag_stage([(ny, yi, nby, 2, a1, quarter, None), (nx, xi, nbx, 2, b1, quarter, None)], half_ref, hsend, hrecv, 0)
    _ag_stage([(nc, core, nbc, 1, 0, rows, None)], half_ref, hsend, hrecv, sem)
    start = 0
    for size, out_ref in zip(sizes, outs):
        out_ref[...] = half_ref[start : start + size]
        start += size


def _counts(rows):
    half, quarter = rows // 2, rows // 4
    c1 = quarter // 4
    slots = half + 3 * 2 * quarter // 4 + 3 * 2 * c1 // 4
    sems = 1 + 3 * 4 + 3 * 2 + 7 + 3 * 2
    return slots, sems, 2 + 4 + 4 + 8, 1 + 3 + 3 + 7


def all_sum(parts, small):
    sizes = tuple(p.shape[0] for p in parts)
    lanes = parts[0].shape[1]
    rows = sum(sizes)
    slots, sems, tslots, tsems = _counts(rows)
    c2 = rows // 64
    vmem = pl.BlockSpec(memory_space=pltpu.VMEM)
    return pl.pallas_call(
        functools.partial(_kernel, sizes),
        out_shape=tuple(jax.ShapeDtypeStruct(p.shape, jnp.bfloat16) for p in parts)
        + (jax.ShapeDtypeStruct(small.shape, small.dtype),),
        in_specs=[vmem] * (len(parts) + 1),
        out_specs=(vmem,) * (len(parts) + 1),
        scratch_shapes=[
            pltpu.VMEM((rows, lanes), jnp.float32),
            pltpu.VMEM((slots, lanes), jnp.float32),
            pltpu.VMEM((8, 2, c2, lanes), jnp.float32),
            pltpu.SemaphoreType.DMA((sems,)),
            pltpu.SemaphoreType.DMA((sems,)),
            pltpu.VMEM((tslots,) + small.shape, small.dtype),
            pltpu.SemaphoreType.DMA((tsems,)),
            pltpu.SemaphoreType.DMA((tsems,)),
            pltpu.VMEM((rows, lanes), jnp.bfloat16),
            pltpu.SemaphoreType.DMA((13,)),
            pltpu.SemaphoreType.DMA((13,)),
            pltpu.VMEM((rows, lanes), jnp.float32),
        ],
        compiler_params=pltpu.CompilerParams(
            collective_id=0, has_side_effects=True, vmem_limit_bytes=48 * 1024 * 1024
        ),
    )(*parts, small)


def _corr_fwd_kernel(ev_ref, win_ref, inv_ref, dots_ref, strip_ref):
    wide = win_ref.shape[0]
    lanes = dots_ref.shape[1]
    rows = lax.broadcasted_iota(jnp.int32, (wide, wide), 0)
    cols = lax.broadcasted_iota(jnp.int32, (wide, wide), 1)
    flip = (rows + cols == wide - 1).astype(jnp.bfloat16)
    win_rev = jnp.dot(flip, win_ref[...], preferred_element_type=jnp.float32).astype(jnp.bfloat16)
    m = lax.dot_general(
        ev_ref[...], win_rev, (((1,), (1,)), ((), ())), preferred_element_type=jnp.float32
    )
    rows = lax.broadcasted_iota(jnp.int32, (lanes, lanes), 0)
    cols = lax.broadcasted_iota(jnp.int32, (lanes, lanes), 1)
    back = (rows + cols == lanes - 1).astype(jnp.float32)

    def unflip(x):
        return jnp.dot(x, back, precision=lax.Precision.HIGHEST, preferred_element_type=jnp.float32)

    dots_ref[...] = unflip(pltpu.roll(m, 0, 1, stride=1, stride_axis=0)[:, wide - lanes :])
    inv = jnp.broadcast_to(inv_ref[...], m.shape)
    strip_ref[...] = unflip(pltpu.roll(inv, 0, 1, stride=1, stride_axis=0)[:, wide - lanes :])


def corr_fwd(emb_v, win_pad, inv_pad):
    clips, frames, width = emb_v.shape
    wide = win_pad.shape[1]
    lanes = 128
    return pl.pallas_call(
        _corr_fwd_kernel,
        grid=(clips,),
        in_specs=[
            pl.BlockSpec((None, frames, width), lambda c: (c, 0, 0)),
            pl.BlockSpec((None, wide, width), lambda c: (c, 0, 0)),
            pl.BlockSpec((None, 1, wide), lambda c: (c, 0, 0)),
        ],
        out_specs=[
            pl.BlockSpec((None, frames, lanes), lambda c: (c, 0, 0)),
            pl.BlockSpec((None, frames, lanes), lambda c: (c, 0, 0)),
        ],
        out_shape=[
            jax.ShapeDtypeStruct((clips, frames, lanes), jnp.float32),
            jax.ShapeDtypeStruct((clips, frames, lanes), jnp.float32),
        ],
    )(emb_v, win_pad, inv_pad)


def _corr_bwd_kernel(gd_ref, at_ref, ev_ref, win_ref, lip_ref, wsum_ref, ginv_ref):
    frames, lanes = gd_ref.shape
    wide = win_ref.shape[0]
    pad = jnp.zeros((frames, wide - lanes), jnp.float32)
    g = jnp.concatenate([gd_ref[...].astype(jnp.float32), pad], axis=1)
    band = pltpu.roll(g, 0, 1, stride=1, stride_axis=0)
    lip_ref[...] = jnp.dot(band.astype(jnp.bfloat16), win_ref[...], preferred_element_type=jnp.float32)
    band_t = band.T.astype(jnp.bfloat16)
    wsum_ref[...] = jnp.dot(band_t, ev_ref[...], preferred_element_type=jnp.float32)
    a = jnp.concatenate([at_ref[...], pad], axis=1)
    spread = pltpu.roll(a, 0, 1, stride=1, stride_axis=0)
    ginv_ref[...] = jnp.sum(spread, axis=0, keepdims=True)


def corr_bwd(gd_pad, at_pad, emb_v, win_pad):
    clips, frames, width = emb_v.shape
    wide = win_pad.shape[1]
    lanes = gd_pad.shape[2]
    return pl.pallas_call(
        _corr_bwd_kernel,
        grid=(clips,),
        in_specs=[
            pl.BlockSpec((None, frames, lanes), lambda c: (c, 0, 0)),
            pl.BlockSpec((None, frames, lanes), lambda c: (c, 0, 0)),
            pl.BlockSpec((None, frames, width), lambda c: (c, 0, 0)),
            pl.BlockSpec((None, wide, width), lambda c: (c, 0, 0)),
        ],
        out_specs=[
            pl.BlockSpec((None, frames, width), lambda c: (c, 0, 0)),
            pl.BlockSpec((None, wide, width), lambda c: (c, 0, 0)),
            pl.BlockSpec((None, 1, wide), lambda c: (c, 0, 0)),
        ],
        out_shape=[
            jax.ShapeDtypeStruct((clips, frames, width), jnp.float32),
            jax.ShapeDtypeStruct((clips, wide, width), jnp.float32),
            jax.ShapeDtypeStruct((clips, 1, wide), jnp.float32),
        ],
    )(gd_pad, at_pad, emb_v, win_pad)


logit_sharpening_divisor = 10.0
loss_scale = 1024.0
epsilon = 1e-06


def padded_2(cells, sides, width, extra=0):
    for axis, dim in sides:
        count = lax.axis_size(axis)
        ends = count - 1
        head = lax.slice_in_dim(cells, 0, width, axis=dim)
        tail = lax.slice_in_dim(cells, cells.shape[dim] - width, cells.shape[dim], axis=dim)
        cells = jnp.concatenate(
            [
                lax.ppermute(tail, axis, [(i, (i + 1) % count) for i in range(ends)]),
                cells,
                lax.ppermute(head, axis, [((i + 1) % count, i) for i in range(ends)]),
            ]
            + ([jnp.zeros(cells.shape[:dim] + (extra,) + cells.shape[dim + 1 :], cells.dtype)] if extra else []),
            axis=dim,
        )
    return cells


def from_behind(value, axis, steps):
    count = lax.axis_size(axis)
    initial, last = (max(0, -steps), min(count, count - steps))
    return lax.ppermute(value, axis, [(source, source + steps) for source in range(initial, last)])


def silu_slope(values):
    sigma = jax.nn.sigmoid(values)
    return sigma * (1.0 + values * (1.0 - sigma))


def encoder(padded, w_conv, w_proj):
    clip_num, frame_pad, chan_num = padded.shape
    frame_num = frame_pad - 2
    columns = jnp.concatenate(
        [padded[:, 0:frame_num], padded[:, 1 : frame_num + 1], padded[:, 2 : frame_num + 2]], axis=2
    )
    before = jnp.einsum(
        "cfk,ke->cfe",
        columns,
        w_conv.reshape(3 * chan_num, w_conv.shape[2]),
        preferred_element_type=jnp.float32,
    )
    hidden = jax.nn.silu(before).astype(jnp.bfloat16)
    embedded = jnp.einsum("cfe,eg->cfg", hidden, w_proj, preferred_element_type=jnp.float32).astype(
        jnp.bfloat16
    )
    return (columns, before, hidden, embedded)


def inverse_norm(embedded):
    values = embedded.astype(jnp.float32)
    return lax.rsqrt(jnp.sum(values * values, axis=-1) + epsilon)


def spread_band(band, wide_len):
    clip_num, row_num, band_len = band.shape
    full_band = jnp.pad(band, ((0, 0), (0, 0), (0, wide_len + 1 - band_len)))
    flat_band = full_band.reshape(clip_num, row_num * (wide_len + 1))[:, : row_num * wide_len]
    return flat_band.reshape(clip_num, row_num, wide_len)


def narrow_band(matrix, band_len):
    clip_num, row_num, wide_len = matrix.shape
    flat_mat = jnp.pad(matrix.reshape(clip_num, row_num * wide_len), ((0, 0), (0, row_num)))
    return flat_mat.reshape(clip_num, row_num, wide_len + 1)[:, :, :band_len]


def flatten_rows(values):
    return values.reshape(values.shape[0] * values.shape[1], values.shape[2])


def proj_grad(hidden, grad_emb):
    return jnp.einsum("re,rf->ef", hidden, grad_emb, preferred_element_type=jnp.float32)


def conv_grad(columns, before, grad_emb, w_proj, w_conv):
    grad_hidden = jnp.einsum("rf,ef->re", grad_emb, w_proj, preferred_element_type=jnp.float32)
    grad_before = (grad_hidden * silu_slope(before)).astype(jnp.bfloat16)
    grad_conv = jnp.einsum("rk,re->ke", columns, grad_before, preferred_element_type=jnp.float32)
    return grad_conv.reshape(w_conv.shape)


def shards(
    audio_feats, lip_feats, lengths, labels, w_audio_conv, w_audio_proj, w_lip_conv, w_lip_proj
):
    clip_num, frame_num, chan_num = audio_feats.shape
    width = w_audio_proj.shape[1]
    offsets = 2 * SPAN + 1
    wide_len = frame_num + 2 * SPAN
    first_frame = lax.axis_index("tm") * frame_num
    stacked = jnp.stack([audio_feats, lip_feats])
    padded = padded_2(stacked, (("tm", 2),), 1)
    cols_a, pre_a, hid_a, emb_a = encoder(padded[0], w_audio_conv, w_audio_proj)
    cols_v, pre_v, hid_v, emb_v = encoder(padded[1], w_lip_conv, w_lip_proj)
    wide_len = frame_num + 2 * SPAN
    wide_pad = -(-wide_len // 128) * 128
    win_pad = padded_2(emb_a, (("tm", 1),), SPAN, wide_pad - wide_len)
    window = win_pad[:, :wide_len]
    cols_a, pre_a, hid_a = (flatten_rows(cols_a), flatten_rows(pre_a), flatten_rows(hid_a))
    cols_v, pre_v, hid_v = (flatten_rows(cols_v), flatten_rows(pre_v), flatten_rows(hid_v))
    count_part = jnp.sum(lengths - jnp.abs(labels))
    count_block = jnp.zeros((8, 128), jnp.int32).at[0, 0].set(count_part)
    count = small_sum(count_block, ("k",), 1)[0, 0].astype(jnp.float32)
    inv_win = inverse_norm(window)
    reciprocal_visual_length = inverse_norm(emb_v)
    inv_pad = jnp.pad(inv_win, ((0, 0), (0, wide_pad - wide_len)))[:, None, :]
    lagged_inner_terms, reciprocal_lag_strip = corr_fwd(emb_v, win_pad, inv_pad[:, :, ::-1])
    lanes_used = lagged_inner_terms.shape[2]
    frame_ids = first_frame + jnp.arange(frame_num, dtype=jnp.int32)
    shifts = jnp.arange(lanes_used, dtype=jnp.int32) - SPAN
    positions = frame_ids[:, None] + shifts[None, :]
    inside = frame_ids[None, :] < lengths[:, None]
    valid = inside[:, :, None] & (positions[None] >= 0) & (positions[None] < lengths[:, None, None])
    valid = valid & (shifts < offsets - SPAN)[None, None, :]
    target_pos = frame_ids[None, :] + labels[:, None]
    counted = inside & (target_pos >= 0) & (target_pos < lengths[:, None])
    correct_lag_position = (shifts[None, :] == labels[:, None]).astype(jnp.float32)
    lag_similarity_logits = (
        logit_sharpening_divisor
        * lagged_inner_terms
        * reciprocal_visual_length[:, :, None]
        * reciprocal_lag_strip
    )
    exponentiated_logits = jnp.where(valid, jnp.exp(lag_similarity_logits), 0.0)
    partition_sums = jnp.where(inside, jnp.sum(exponentiated_logits, axis=2), 1.0)
    picked = jnp.sum(lag_similarity_logits * correct_lag_position[:, None, :], axis=2)
    loss_local = jnp.sum(jnp.where(counted, jnp.log(partition_sums) - picked, 0.0))
    normalized_probabilities = jnp.where(counted, loss_scale / count, 0.0)
    logit_derivative = (
        logit_sharpening_divisor
        * normalized_probabilities[:, :, None]
        * (exponentiated_logits / partition_sums[:, :, None] - correct_lag_position[:, None, :])
    )
    grad_dots = (
        logit_derivative * reciprocal_visual_length[:, :, None] * reciprocal_lag_strip
    ).astype(jnp.bfloat16)
    grad_inv_v = jnp.sum(logit_derivative * lagged_inner_terms * reciprocal_lag_strip, axis=2)
    audio_term = logit_derivative * lagged_inner_terms * reciprocal_visual_length[:, :, None]
    lip_sum, win_sum_pad, ginv_pad = corr_bwd(
        grad_dots, audio_term, emb_v, win_pad
    )
    grad_inv_win = ginv_pad[:, 0, :wide_len]
    lip_vals = emb_v.astype(jnp.float32)
    grad_lip = (
        lip_sum
        - (
            reciprocal_visual_length
            * reciprocal_visual_length
            * reciprocal_visual_length
            * grad_inv_v
        )[:, :, None]
        * lip_vals
    ).astype(jnp.bfloat16)
    win_sum = win_sum_pad[:, :wide_len]
    win_sum = win_sum - (inv_win * inv_win * inv_win * grad_inv_win)[:, :, None] * window.astype(
        jnp.float32
    )
    own_grad = win_sum[:, SPAN : SPAN + frame_num]
    from_after = from_behind(win_sum[:, :SPAN], "tm", -1)
    from_before = from_behind(win_sum[:, frame_num + SPAN :], "tm", 1)
    body = frame_num - SPAN
    own_grad = (
        own_grad
        + jnp.pad(from_after, ((0, 0), (body, 0), (0, 0)))
        + jnp.pad(from_before, ((0, 0), (0, body), (0, 0)))
    )
    grad_audio = own_grad.astype(jnp.bfloat16).reshape(clip_num * frame_num, width)
    grad_lip = grad_lip.reshape(clip_num * frame_num, width)
    grad_ap = proj_grad(hid_a, grad_audio)
    grad_vp = proj_grad(hid_v, grad_lip)
    grad_ac = conv_grad(cols_a, pre_a, grad_audio, w_audio_proj, w_audio_conv)
    grad_vc = conv_grad(cols_v, pre_v, grad_lip, w_lip_proj, w_lip_conv)
    parts = (grad_ac, grad_vc, grad_ap, grad_vp)
    lanes = grad_ap.shape[1]
    loss_block = jnp.zeros((8, 128), jnp.float32).at[0, 0].set(loss_local)
    *sums, loss_total = all_sum([g.reshape(-1, lanes) for g in parts], loss_block)
    grad_ac, grad_vc, grad_ap, grad_vp = (
        t.astype(jnp.float32).reshape(g.shape) for t, g in zip(sums, parts)
    )
    loss_sum = loss_total[0, 0]
    return (loss_sum / count, grad_ac, grad_ap, grad_vc, grad_vp)


def solution(mesh):
    placed = (
        P("clip", "tm", None),
        P("clip", "tm", None),
        P("clip"),
        P("clip"),
        P(),
        P(),
        P(),
        P(),
    )
    return jax.shard_map(
        shards, mesh=mesh, in_specs=placed, out_specs=(P(), P(), P(), P(), P()), check_vma=False
    )
```
